128 devices in a mesh: ty: 8 (over x_lo, z), tx: 4 (over x_hi, core), pat: 4 (over y).
Axes of the slice: x: 4 (x_hi: 2, x_lo: 2; x = x_hi * 2 + x_lo), y: 4, z: 4, core: 2. Of those that a mesh axis runs over, the one named last changes fastest.
Arguments:
- estimate: float32 [32, 128, 1024], P(None, 'ty', 'tx'), may hold values from 0.5 to 1.5, as said below
- data: float32 [8, 32, 128, 1024], P('pat', None, 'ty', 'tx'), may hold values from 0.1 to 6, as said below
- axial: float32 [32, 32], replicated, may hold values from 0 to 0.6, as said below
- lateral_kernel: float32 [9, 9], replicated, may hold values from 0.01 to 0.04
- psf_radius: int32 [9], replicated, may hold values from 0 to 4
- pattern_codes: int32 [2, 8], replicated, may hold values from 0 to 4, as said below
Outputs:
- object_out: float32 [32, 128, 1024], P(None, 'ty', 'tx')
- residual_rms: float32 [4], replicated
The draws below stay inside these ranges and needn't reach their ends.
Inputs may be any that keep to these rules, and one draw needn't show every extreme that they name: `estimate`: positive values. `data`: positive photon counts. `axial`: nonnegative entries. `pattern_codes`: angle indices are 0 to 2, phase indices 0 to 4.
All inputs are finite; a program needn't handle non-finite values.
Results may differ from the reference program's by a relative error of at most 0.0003.
The reference program's roundings to bfloat16 on the way (of `kernel` and `backward`) count: a program that leaves them out, or rounds other values in their place, can miss the bound.
Values may be sent and summed in bfloat16 or wider, within the bound.
A program may use at most 128 MiB of HBM per device.

```python
import math
import jax
import jax.numpy as jnp
from jax import lax

Z = 32
ROWS_DEV = 16
COLS_DEV = 256
RADIUS = 4
ITERS = 4
PATTERNS = 8
NY = 128
NX = 1024


def tile_table(key):
    row_tile = (jnp.arange(NY).astype(jnp.int32) // ROWS_DEV).astype(jnp.int32)
    col_tile = (jnp.arange(NX).astype(jnp.int32) // COLS_DEV).astype(jnp.int32)
    parity = ((row_tile[:, None] + col_tile[None, :]) % 2).astype(jnp.float32)
    jitter = jax.random.uniform(key, (NY // ROWS_DEV, NX // COLS_DEV), jnp.float32, 0.0, 1.0)
    return (parity, jitter[row_tile[:, None], col_tile[None, :]])


def draw_estimate(key, part):
    parity, jitter = tile_table(jax.random.fold_in(key, 41))
    level = jnp.where(parity > 0.5, 0.6 + 0.2 * jitter, 1.15 + 0.15 * jitter)
    noise = jax.random.uniform(jax.random.fold_in(key, 42), (Z, NY, NX), jnp.float32, 0.85, 1.15)
    return level[None] * noise


def draw_data(key, part):
    parity, jitter = tile_table(jax.random.fold_in(key, 31))
    tile_level = jnp.where(parity > 0.5, 1.6 + 0.8 * jitter, 0.4 + 0.2 * jitter)
    pattern_index = jnp.arange(PATTERNS).astype(jnp.float32)
    pattern_level = 0.5 * jnp.exp(math.log(4.0) * pattern_index / (PATTERNS - 1))
    noise = jax.random.uniform(jax.random.fold_in(key, 32), (PATTERNS, Z, NY, NX), jnp.float32, 0.55, 1.2)
    return pattern_level[:, None, None, None] * tile_level[None, None] * noise


def draw_axial(key, part):
    plane_index = jnp.arange(Z).astype(jnp.float32)
    distance = jnp.abs(plane_index[:, None] - plane_index[None, :])
    spread = jax.random.uniform(jax.random.fold_in(key, 11), (Z, Z), jnp.float32, 0.0, 1.0)
    diagonal = jax.random.uniform(jax.random.fold_in(key, 12), (Z, Z), jnp.float32, 0.4, 0.6)
    offside = spread * 0.05 * jnp.exp(-distance / 8.0)
    return jnp.where(distance == 0.0, diagonal, offside)


def draw_pattern_codes(key, part):
    angle_order = jax.random.permutation(jax.random.fold_in(key, 21), PATTERNS).astype(jnp.int32)
    phase_order = jax.random.permutation(jax.random.fold_in(key, 22), PATTERNS).astype(jnp.int32)
    offset = jax.random.randint(jax.random.fold_in(key, 23), (), 0, 5).astype(jnp.int32)
    angles = angle_order % 3
    phases = (phase_order + offset) % 5
    return jnp.stack([angles, phases]).astype(jnp.int32)


def with_ends(values, own_key, low, largest):
    place = [jax.random.randint(jax.random.fold_in(own_key, axis), (), 0, length) for axis, length in enumerate(values.shape)]
    longest = values.shape.index(max(values.shape))
    neighbour = place[:longest] + [(place[longest] + 1) % values.shape[longest]] + place[longest + 1:]
    return values.at[tuple(place)].set(low).at[tuple(neighbour)].set(largest)


def setup_inputs(seed: int = 0) -> dict:
    arg_keys = jax.random.split(jax.random.key(seed), 7)
    estimate = draw_estimate(jax.random.fold_in(arg_keys[6], 71), 0)
    data = draw_data(jax.random.fold_in(arg_keys[6], 71), 0)
    axial = draw_axial(jax.random.fold_in(arg_keys[6], 71), 0)
    lateral_kernel = jnp.clip(jax.random.uniform(arg_keys[3], (2 * RADIUS + 1, 2 * RADIUS + 1), jnp.float32, 0.01, 0.04), 0.01, 0.04)
    psf_radius = with_ends(jax.random.randint(arg_keys[4], (2 * RADIUS + 1,), 0, RADIUS + 1), jax.random.fold_in(arg_keys[4], 1), 0, RADIUS).astype(jnp.int32)
    pattern_codes = draw_pattern_codes(jax.random.fold_in(arg_keys[6], 71), 0)
    return {"estimate": estimate, "data": data, "axial": axial, "lateral_kernel": lateral_kernel, "psf_radius": psf_radius, "pattern_codes": pattern_codes}


TWO_PI = 2.0 * math.pi

def wave_table(angle_code, phase_code, row_coord, col_coord, planes):
    step_col = jnp.where(angle_code == 0, 2, -1).astype(jnp.int32)
    step_row = jnp.where(angle_code == 0, 0, jnp.where(angle_code == 1, 2, -2)).astype(jnp.int32)
    argument = (step_col[:, None, None] * col_coord[None, None, :] + step_row[:, None, None] * row_coord[None, :, None] + phase_code[:, None, None]) % 5
    lateral_wave = jnp.cos(argument.astype(jnp.float32) * (TWO_PI / 5.0))
    plane_index = jnp.arange(planes).astype(jnp.float32)
    axial_wave = jnp.cos(plane_index * (TWO_PI * 3.0 / planes))
    return 1.0 + 0.7 * lateral_wave[:, None, :, :] * axial_wave[None, :, None, None]

def masked_kernel(lateral_kernel, psf_radius):
    offsets = jnp.arange(2 * RADIUS + 1).astype(jnp.int32) - RADIUS
    within = jnp.abs(offsets)[None, :] <= psf_radius.astype(jnp.int32)[:, None]
    return jnp.where(within, lateral_kernel, jnp.zeros_like(lateral_kernel)).astype(jnp.bfloat16)

def widen(values):
    return lax.optimization_barrier(values).astype(jnp.float32)

def lateral_pass(values, kernel):
    dims = values.shape
    flattened = widen(values).reshape((-1, 1, dims[-2], dims[-1]))
    result = lax.conv_general_dilated(flattened, widen(kernel)[None, None], (1, 1), ((RADIUS, RADIUS), (RADIUS, RADIUS)), precision=lax.Precision.HIGHEST)
    return result.reshape(dims)

def reference(estimate, data, axial, lateral_kernel, psf_radius, pattern_codes):
    kernel = masked_kernel(lateral_kernel, psf_radius)
    flipped = kernel[::-1, ::-1]
    axial_f = widen(axial.astype(jnp.bfloat16))
    row_coord = jnp.arange(NY).astype(jnp.int32)
    col_coord = jnp.arange(NX).astype(jnp.int32)
    lighting = wave_table(pattern_codes[0], pattern_codes[1], row_coord, col_coord, Z)
    inside = jnp.ones((1, NY, NX), jnp.bfloat16)
    coverage = widen(lateral_pass(inside, flipped).astype(jnp.bfloat16))
    spread = jnp.einsum('ba,byx->ayx', axial_f, jnp.broadcast_to(coverage, (Z, NY, NX)), precision=lax.Precision.HIGHEST)
    normalizer = lax.optimization_barrier(jnp.sum(lighting * spread[None], axis=0))
    cell_count = float(PATTERNS * Z * NY * NX)
    current = estimate
    squares_list = []
    for iteration in range(ITERS):
        lighted = widen((lighting * current[None]).astype(jnp.bfloat16))
        blurred = jnp.einsum('ab,pbyx->payx', axial_f, lighted, precision=lax.Precision.HIGHEST).astype(jnp.bfloat16)
        predicted = lateral_pass(blurred, kernel)
        misfit = data - predicted
        squares_list.append(jnp.sum(misfit * misfit))
        quotient = (data / predicted).astype(jnp.bfloat16)
        backward = widen(lateral_pass(quotient, flipped).astype(jnp.bfloat16))
        gathered = jnp.einsum('ba,pbyx->payx', axial_f, backward, precision=lax.Precision.HIGHEST)
        summed = lax.optimization_barrier(jnp.sum(lighting * gathered, axis=0))
        current = current * summed / normalizer
    squares = jnp.stack(squares_list)
    return (current, jnp.sqrt(squares / cell_count))
```

```python
import functools
import math

import jax
import jax.numpy as jnp
from jax import lax
from jax.experimental import pallas as pl
from jax.experimental.pallas import tpu as pltpu
from jax.sharding import PartitionSpec as P

ITERS = 4
TAPS = 9
NPAT = 8
LANES = 128
COSINES = [math.cos(2.0 * math.pi * m / 5.0) for m in range(5)]
MESH = pl.DeviceIdType.MESH


def lane_iota(shape):
    return lax.broadcasted_iota(jnp.int32, shape, len(shape) - 1)


def row_iota(shape):
    return lax.broadcasted_iota(jnp.int32, shape, len(shape) - 2)


def block_transpose(tiles):
    group = lane_iota(tiles[0].shape) // 16
    tiles = list(tiles)
    for bit in (4, 2, 1):
        keep = (group & bit) == 0
        for k in range(8):
            if k & bit:
                continue
            low, high = tiles[k], tiles[k + bit]
            axis = low.ndim - 1
            tiles[k] = jnp.where(keep, low, pltpu.roll(high, 16 * bit, axis))
            tiles[k + bit] = jnp.where(keep, pltpu.roll(low, LANES - 16 * bit, axis), high)
    return tiles


def kernel(
    full_rows,
    full_cols,
    est_ref,
    data_ref,
    axial_ref,
    taps_ref,
    radius_ref,
    codes_ref,
    out_ref,
    squares_ref,
    grid_ref,
    final_ref,
    home_ref,
    data_tiles,
    top_ref,
    bottom_ref,
    left_ref,
    right_ref,
    lit_ref,
    blur_ref,
    pred_ref,
    quot_ref,
    forward_ref,
    adjoint_ref,
    axial_fwd,
    axial_adj,
    wave_ext,
    wave_in,
    planes_ref,
    mask_ext,
    valid_ref,
    norm_ref,
    halo_send,
    halo_recv,
    row_send,
    row_recv,
    edge_send,
    left_recv,
    right_recv,
    pat_send,
    pat_recv,
    out_send,
    out_recv,
):
    ty, tx, q = lax.axis_index("ty"), lax.axis_index("tx"), lax.axis_index("pat")
    nty, ntx, npat = lax.axis_size("ty"), lax.axis_size("tx"), lax.axis_size("pat")
    ncol = ntx * npat
    column = tx * npat + q

    def at(dty, dcol):
        c = lax.rem(column + dcol + ncol, ncol)
        return {"ty": lax.rem(ty + dty + nty, nty), "tx": c // npat, "pat": lax.rem(c, npat)}

    def peer(d):
        return {"ty": ty, "tx": tx, "pat": lax.rem(q + d, npat)}

    barrier = pltpu.get_barrier_semaphore()
    greeted = 0
    for dty in (-1, 0, 1):
        for dtx in (-1, 0, 1):
            for dq in range(npat):
                if dty == 0 and dtx == 0 and dq == 0:
                    continue
                pl.semaphore_signal(
                    barrier,
                    inc=1,
                    device_id={
                        "ty": lax.rem(ty + dty + nty, nty),
                        "tx": lax.rem(tx + dtx + ntx, ntx),
                        "pat": lax.rem(q + dq, npat),
                    },
                    device_id_type=MESH,
                )
                greeted += 1

    for strip in range(2):
        for half in range(2):
            rows = [est_ref[8 * strip + y, :, LANES * half : LANES * (half + 1)] for y in range(8)]
            for k, tile in enumerate(block_transpose(rows)):
                final_ref[2 * half + k // 4, k % 4, strip] = tile
    grid_ref[0, 1:5, 1:3] = final_ref[q]

    pl.semaphore_wait(barrier, greeted)

    def halo_copies(t):
        moves = [
            ((slice(1, 5), 1), (slice(1, 5), 3), -1, 0),
            ((slice(1, 5), 2), (slice(1, 5), 0), 1, 0),
            ((1, slice(1, 3)), (5, slice(1, 3)), 0, -1),
            ((4, slice(1, 3)), (0, slice(1, 3)), 0, 1),
            ((1, 1), (5, 3), -1, -1),
            ((4, 1), (0, 3), -1, 1),
            ((1, 2), (5, 0), 1, -1),
            ((4, 2), (0, 0), 1, 1),
        ]
        copies = []
        for k, (source, target, dty, dcol) in enumerate(moves):
            copies.append(
                pltpu.make_async_remote_copy(
                    src_ref=grid_ref.at[(t, *source)],
                    dst_ref=grid_ref.at[(t, *target)],
                    send_sem=halo_send.at[t, k],
                    recv_sem=halo_recv.at[t, k],
                    device_id=at(dty, dcol),
                    device_id_type=MESH,
                )
            )
        return copies

    for copy in halo_copies(0):
        copy.start()

    row_copies = [
        pltpu.make_async_remote_copy(
            src_ref=data_ref.at[12:16],
            dst_ref=top_ref,
            send_sem=row_send.at[0],
            recv_sem=row_recv.at[0],
            device_id=at(1, 0),
            device_id_type=MESH,
        ),
        pltpu.make_async_remote_copy(
            src_ref=data_ref.at[0:4],
            dst_ref=bottom_ref,
            send_sem=row_send.at[1],
            recv_sem=row_recv.at[1],
            device_id=at(-1, 0),
            device_id_type=MESH,
        ),
    ]
    for copy in row_copies:
        copy.start()

    def data_row(row, block, half):
        rows = slice(8 * block, 8 * block + 8)
        lanes = slice(LANES * half, LANES * (half + 1))
        if row < 4:
            return top_ref[row, rows, lanes]
        if row < 20:
            return data_ref[row - 4, rows, lanes]
        return bottom_ref[row - 20, rows, lanes]

    def make_strip(strip):
        first = lane_iota((8, LANES)) < 4
        for block in range(8):
            at_rows = slice(8 * block, 8 * block + 8)
            low = [pltpu.roll(data_row(8 * strip + y, block, 0), 4, 1) for y in range(8)]
            high = [pltpu.roll(data_row(8 * strip + y, block, 1), 4, 1) for y in range(8)]
            for k, tile in enumerate(block_transpose(low)):
                home_ref[k, strip, at_rows] = tile
            mixed = [jnp.where(first, a, b) for a, b in zip(low, high)]
            for k, tile in enumerate(block_transpose(mixed)):
                home_ref[8 + k, strip, at_rows] = tile
            last = high[0]
            group = lane_iota((8, LANES)) // 16
            for y in range(1, 8):
                last = jnp.where(group == y, pltpu.roll(high[y], 16 * y, 1), last)
            home_ref[16, strip, at_rows] = last

    def strip_copies(strip):
        copies = []
        for d in range(1, npat):
            to = lax.rem(q + d, npat)
            copies.append(
                pltpu.make_async_remote_copy(
                    src_ref=home_ref.at[pl.ds(4 * to, 5), strip],
                    dst_ref=data_tiles.at[q, :, strip],
                    send_sem=pat_send.at[strip, d - 1],
                    recv_sem=pat_recv.at[strip, d - 1],
                    device_id=peer(d),
                    device_id_type=MESH,
                )
            )
        return copies

    def edge_copies():
        return [
            pltpu.make_async_remote_copy(
                src_ref=home_ref.at[16],
                dst_ref=left_ref.at[q],
                send_sem=edge_send.at[0],
                recv_sem=left_recv.at[q],
                device_id={"ty": ty, "tx": lax.rem(tx + 1, ntx), "pat": 0},
                device_id_type=MESH,
            ),
            pltpu.make_async_remote_copy(
                src_ref=home_ref.at[0],
                dst_ref=right_ref.at[q],
                send_sem=edge_send.at[1],
                recv_sem=right_recv.at[q],
                device_id={"ty": ty, "tx": lax.rem(tx + ntx - 1, ntx), "pat": npat - 1},
                device_id_type=MESH,
            ),
        ]

    make_strip(1)
    for copy in strip_copies(1):
        copy.start()

    lane = lane_iota((LANES, LANES))
    line = row_iota((LANES, LANES))
    for backward in (False, True):
        target = adjoint_ref if backward else forward_ref
        target[...] = jnp.zeros_like(target)
        for block in range(2):
            row_gap = 8 * block + line // 16 - lane // 16
            for step in range(2):
                col_gap = 16 * step + lax.rem(line, 16) - lax.rem(lane, 16)
                total = jnp.zeros((LANES, LANES), jnp.float32)
                for i in range(TAPS):
                    here = jnp.zeros((LANES, LANES), jnp.float32)
                    for j in range(TAPS):
                        ki, kj = (TAPS - 1 - i, TAPS - 1 - j) if backward else (i, j)
                        tap = jnp.where(abs(kj - 4) <= radius_ref[ki], taps_ref[ki, kj], 0.0)
                        here = jnp.where(col_gap == j, tap, here)
                    total = jnp.where(row_gap == i, here, total)
                values = total.astype(jnp.bfloat16)
                for out_chunk in range(2):
                    start = 256 * (out_chunk + step) + LANES * block
                    target[start : start + LANES, LANES * out_chunk : LANES * (out_chunk + 1)] = values

    spread = (row_iota((256, 32)) % 32 == lane_iota((256, 32))).astype(jnp.bfloat16)
    axial_b = axial_ref[...].astype(jnp.bfloat16)
    same = row_iota((256, 256)) // 32 == lane_iota((256, 256)) // 32
    nt = (((1,), (1,)), ((), ()))
    right_fwd = lax.dot_general(axial_b, spread, nt, preferred_element_type=jnp.float32)
    full = jnp.dot(spread, right_fwd.astype(jnp.bfloat16), preferred_element_type=jnp.float32)
    axial_fwd[...] = jnp.where(same, full, 0.0).astype(jnp.bfloat16)
    left_adj = lax.dot_general(spread, axial_b, nt, preferred_element_type=jnp.float32)
    full = lax.dot_general(left_adj.astype(jnp.bfloat16), spread, nt, preferred_element_type=jnp.float32)
    axial_adj[...] = jnp.where(same, full, 0.0).astype(jnp.bfloat16)

    plane = row_iota((32, LANES)).astype(jnp.float32)
    planes_ref[...] = jnp.cos(plane * (2.0 * math.pi * 3.0 / 32.0))

    def positions(tile, strips, offset):
        spot = lane_iota(tile.shape)
        chunk, strip = tile // strips, tile % strips
        y = ty * 16 + 8 * strip - offset + spot // 16
        x = column * 64 + 16 * chunk - offset + spot % 16
        return y, x

    def waves(count, strips, offset):
        shape = (count * NPAT, LANES)
        index = row_iota(shape)
        y, x = positions(index // NPAT, strips, offset)
        pattern = index % NPAT
        angle = jnp.zeros(shape, jnp.int32)
        phase = jnp.zeros(shape, jnp.int32)
        for p in range(NPAT):
            angle = jnp.where(pattern == p, codes_ref[0, p], angle)
            phase = jnp.where(pattern == p, codes_ref[1, p], phase)
        cx = jnp.where(angle == 0, 2, -1)
        cy = jnp.where(angle == 0, 0, jnp.where(angle == 1, 2, -2))
        value = cx * x + cy * y + phase
        wide = value.astype(jnp.float32)
        m = wide - 5.0 * jnp.floor((wide + 0.5) * 0.2)
        wave = jnp.full(shape, COSINES[0], jnp.float32)
        for k in range(1, 5):
            wave = jnp.where(m == float(k), COSINES[k], wave)
        return 0.7 * wave

    wave_ext[...] = waves(20, 4, 8)
    wave_in[...] = waves(8, 2, 0)

    def inside(shape, strips, offset):
        y, x = positions(row_iota(shape), strips, offset)
        return (y >= 0) & (y < full_rows) & (x >= 0) & (x < full_cols)

    mask_ext[...] = inside((24, LANES), 4, 8).astype(jnp.float32)
    tile15 = (16, LANES)
    valid = inside(tile15, 3, 4) & ((row_iota(tile15) < 12) | (lane_iota(tile15) % 16 < 8))
    valid_ref[...] = valid.astype(jnp.float32)

    for copy in row_copies:
        copy.wait_recv()
    make_strip(0)
    make_strip(2)
    for copy in strip_copies(0) + strip_copies(2) + edge_copies():
        copy.start()
    data_tiles[q] = home_ref[pl.ds(4 * q, 5)]

    column_sum = lax.dot_general(
        axial_b, jnp.ones((32, LANES), jnp.bfloat16), (((0,), (0,)), ((), ())),
        preferred_element_type=jnp.float32,
    )
    cover_in = [
        jnp.broadcast_to(valid_ref[k : k + 1, :], (16, LANES)).astype(jnp.bfloat16)
        for k in range(15)
    ]
    plane_wave = planes_ref[...]
    for strip in range(2):
        for chunk in (0, 2):
            window = jnp.concatenate(
                [cover_in[3 * (chunk + k) + strip + a] for k in range(3) for a in range(2)], axis=1
            )
            cover = jnp.dot(window, adjoint_ref[...], preferred_element_type=jnp.float32)
            cover = cover.astype(jnp.bfloat16).astype(jnp.float32)
            for k in range(2):
                tile = 2 * (chunk + k) + strip
                row = cover[0:1, LANES * k : LANES * (k + 1)]
                light = jnp.zeros((32, LANES), jnp.float32)
                for p in range(NPAT):
                    light = light + (1.0 + wave_in[NPAT * tile + p : NPAT * tile + p + 1, :] * plane_wave)
                norm_ref[tile] = light * (row * column_sum)

    own = lane_iota((8, LANES))
    own_col, own_row = own % 16, own // 16

    def inner_mask(tile):
        chunk, strip = tile // 3, tile % 3
        x, y = 16 * chunk + own_col, 8 * strip + own_row
        return (x >= 4) & (x < 68) & (y >= 4) & (y < 20)

    def predict(strip, chunk):
        tile = 4 * chunk + strip
        if chunk == 4:
            return jnp.dot(
                blur_ref[:, LANES * tile : LANES * (tile + 2)],
                forward_ref[0:256, 0:LANES],
                preferred_element_type=jnp.float32,
            )
        window = jnp.concatenate(
            [blur_ref[:, LANES * (tile + 4 * k) : LANES * (tile + 4 * k + 2)] for k in range(3)], axis=1
        )
        return jnp.dot(window, forward_ref[...], preferred_element_type=jnp.float32)

    def compare(strip, chunk, predicted, squares):
        for k in range(predicted.shape[1] // LANES):
            tile = 3 * (chunk + k) + strip
            ok = valid_ref[tile : tile + 1, :]
            filler = 1.0 - ok
            total = jnp.zeros((8, LANES), jnp.float32)
            for source in range(4):
                data = data_tiles[source, chunk + k, strip]
                guess = predicted[64 * source : 64 * (source + 1), LANES * k : LANES * (k + 1)]
                misfit = data - guess
                total = total + jnp.sum((misfit * misfit).reshape(8, 8, LANES), axis=0)
                quotient = (data * ok) / (guess + filler)
                quot_ref[64 * source : 64 * (source + 1), LANES * tile : LANES * (tile + 1)] = (
                    quotient.astype(jnp.bfloat16)
                )
            squares = squares + jnp.where(inner_mask(tile), total, 0.0)
        return squares

    def iteration(t, first):
        copies = halo_copies(t)
        for copy in copies:
            copy.wait_recv()
        wave_z = planes_ref[...]
        left_half = lane_iota((32, LANES)) % 16 < 8
        for chunk in range(5):
            for strip in range(4):
                tile = 4 * chunk + strip
                a, b = grid_ref[t, chunk, strip], grid_ref[t, chunk + 1, strip]
                value = jnp.where(left_half, pltpu.roll(a, LANES - 8, 1), pltpu.roll(b, 8, 1))
                value = value * mask_ext[tile : tile + 1, :]
                for p in range(NPAT):
                    light = 1.0 + wave_ext[NPAT * tile + p : NPAT * tile + p + 1, :] * wave_z
                    lit_ref[32 * p : 32 * (p + 1), LANES * tile : LANES * (tile + 1)] = (
                        light * value
                    ).astype(jnp.bfloat16)
        for pair in range(10):
            lanes = slice(256 * pair, 256 * (pair + 1))
            blur_ref[:, lanes] = jnp.dot(
                axial_fwd[...], lit_ref[:, lanes], preferred_element_type=jnp.float32
            ).astype(jnp.bfloat16)
        squares = jnp.zeros((8, LANES), jnp.float32)
        order = [(strip, chunk) for strip in range(3) for chunk in (0, 2, 4)]
        if first:
            for strip, chunk in order:
                width = LANES if chunk == 4 else 2 * LANES
                tile = 5 * strip + chunk
                pred_ref[:, LANES * tile : LANES * tile + width] = predict(strip, chunk)
            for strip in range(3):
                for copy in strip_copies(strip):
                    copy.wait_recv()

            @pl.when(q == 0)
            def _():
                for source in range(4):
                    edge_in(left_ref.at[source], left_recv.at[source])
                    keep = lane_iota((64, LANES)) % 16 < 4
                    for strip in range(3):
                        data_tiles[source, 0, strip] = jnp.where(
                            keep, left_ref[source, strip], data_tiles[source, 0, strip]
                        )

            @pl.when(q == npat - 1)
            def _():
                for source in range(4):
                    edge_in(right_ref.at[source], right_recv.at[source])
                    keep = lane_iota((64, LANES)) % 16 < 4
                    for strip in range(3):
                        data_tiles[source, 4, strip] = jnp.where(
                            keep, data_tiles[source, 4, strip], right_ref[source, strip]
                        )

            for strip, chunk in order:
                width = LANES if chunk == 4 else 2 * LANES
                tile = 5 * strip + chunk
                squares = compare(
                    strip, chunk, pred_ref[:, LANES * tile : LANES * tile + width], squares
                )
        else:
            for strip, chunk in order:
                squares = compare(strip, chunk, predict(strip, chunk), squares)
        squares_ref[t] = squares
        updated = []
        for strip in range(2):
            for chunk in (0, 2):
                tile = 3 * chunk + strip
                window = jnp.concatenate(
                    [quot_ref[:, LANES * (tile + 3 * k) : LANES * (tile + 3 * k + 2)] for k in range(3)],
                    axis=1,
                )
                spread_back = jnp.dot(
                    window, adjoint_ref[...], preferred_element_type=jnp.float32
                ).astype(jnp.bfloat16)
                gathered = jnp.dot(
                    axial_adj[...], spread_back, preferred_element_type=jnp.float32
                )
                for k in range(2):
                    here = 2 * (chunk + k) + strip
                    summed = jnp.zeros((32, LANES), jnp.float32)
                    for p in range(NPAT):
                        light = 1.0 + wave_in[NPAT * here + p : NPAT * here + p + 1, :] * wave_z
                        summed = summed + light * gathered[
                            32 * p : 32 * (p + 1), LANES * k : LANES * (k + 1)
                        ]
                    current = grid_ref[t, 1 + chunk + k, 1 + strip]
                    updated.append((chunk + k, strip, current * summed / norm_ref[here]))
        return updated, copies

    def edge_in(ref, sem):
        pltpu.make_async_copy(ref, ref, sem).wait()

    def advance(t, first):
        updated, copies = iteration(t, first)
        for chunk, strip, value in updated:
            grid_ref[t + 1, 1 + chunk, 1 + strip] = value
        for copy in halo_copies(t + 1):
            copy.start()
        for copy in copies:
            copy.wait_send()

    advance(0, True)
    for copy in row_copies + strip_copies(0) + strip_copies(1) + strip_copies(2) + edge_copies():
        copy.wait_send()

    @pl.loop(1, ITERS - 1)
    def _(t):
        advance(t, False)

    updated, copies = iteration(ITERS - 1, False)
    for chunk, strip, value in updated:
        final_ref[q, chunk, strip] = value
    outs = [
        pltpu.make_async_remote_copy(
            src_ref=final_ref.at[q],
            dst_ref=final_ref.at[q],
            send_sem=out_send.at[d - 1],
            recv_sem=out_recv.at[d - 1],
            device_id=peer(d),
            device_id_type=MESH,
        )
        for d in range(1, npat)
    ]
    for copy in outs:
        copy.start()
    for copy in copies:
        copy.wait_send()
    for copy in outs:
        copy.wait()
    for strip in range(2):
        for half in range(2):
            tiles = [final_ref[2 * half + k // 4, k % 4, strip] for k in range(8)]
            for y, row in enumerate(block_transpose(tiles)):
                out_ref[8 * strip + y, :, LANES * half : LANES * (half + 1)] = row


def per_device(estimate, data, axial, lateral_kernel, psf_radius, pattern_codes):
    planes, height, width = estimate.shape
    local = data.shape[0]
    full_rows = height * lax.axis_size("ty")
    full_cols = width * lax.axis_size("tx")
    est_rows = estimate.transpose(1, 0, 2)
    data_rows = data.transpose(2, 0, 1, 3).reshape(height, local * planes, width)
    vmem = pl.BlockSpec(memory_space=pltpu.VMEM)
    smem = pl.BlockSpec(memory_space=pltpu.SMEM)
    f32, bf16 = jnp.float32, jnp.bfloat16
    dma = pltpu.SemaphoreType.DMA
    rows, squares = pl.pallas_call(
        functools.partial(kernel, full_rows, full_cols),
        name="deconvolve",
        out_shape=(
            jax.ShapeDtypeStruct((height, planes, width), f32),
            jax.ShapeDtypeStruct((ITERS, 8, LANES), f32),
        ),
        in_specs=[vmem, vmem, vmem, smem, smem, smem],
        out_specs=(vmem, vmem),
        scratch_shapes=[
            pltpu.VMEM((ITERS, 6, 4, 32, LANES), f32),
            pltpu.VMEM((4, 4, 2, 32, LANES), f32),
            pltpu.VMEM((17, 3, 64, LANES), f32),
            pltpu.VMEM((4, 5, 3, 64, LANES), f32),
            pltpu.VMEM((4, 64, 256), f32),
            pltpu.VMEM((4, 64, 256), f32),
            pltpu.VMEM((4, 3, 64, LANES), f32),
            pltpu.VMEM((4, 3, 64, LANES), f32),
            pltpu.VMEM((256, 20 * LANES), bf16),
            pltpu.VMEM((256, 20 * LANES), bf16),
            pltpu.VMEM((256, 15 * LANES), f32),
            pltpu.VMEM((256, 15 * LANES), bf16),
            pltpu.VMEM((768, 256), bf16),
            pltpu.VMEM((768, 256), bf16),
            pltpu.VMEM((256, 256), bf16),
            pltpu.VMEM((256, 256), bf16),
            pltpu.VMEM((20 * NPAT, LANES), f32),
            pltpu.VMEM((8 * NPAT, LANES), f32),
            pltpu.VMEM((32, LANES), f32),
            pltpu.VMEM((24, LANES), f32),
            pltpu.VMEM((16, LANES), f32),
            pltpu.VMEM((8, 32, LANES), f32),
            dma((ITERS, 8)),
            dma((ITERS, 8)),
            dma((2,)),
            dma((2,)),
            dma((2,)),
            dma((4,)),
            dma((4,)),
            dma((3, 3)),
            dma((3, 3)),
            dma((3,)),
            dma((3,)),
        ],
        compiler_params=pltpu.CompilerParams(
            collective_id=0, has_side_effects=True, vmem_limit_bytes=56 * 1024 * 1024
        ),
    )(est_rows, data_rows, axial, lateral_kernel, psf_radius, pattern_codes)
    total = lax.psum(jnp.sum(squares, axis=(1, 2)), ("ty", "tx", "pat"))
    cells = float(local * lax.axis_size("pat") * planes * full_rows * full_cols)
    return rows.transpose(1, 0, 2), jnp.sqrt(total / cells)


def solution(mesh):
    in_specs = (P(None, "ty", "tx"), P("pat", None, "ty", "tx"), P(), P(), P(), P())
    out_specs = (P(None, "ty", "tx"), P())
    return jax.shard_map(
        per_device, mesh=mesh, in_specs=in_specs, out_specs=out_specs, check_vma=False
    )
```

```python
import functools
import math

import jax
import jax.numpy as jnp
from jax import lax
from jax.experimental import pallas as pl
from jax.experimental.pallas import tpu as pltpu
from jax.sharding import PartitionSpec as P

ITERS = 4
TAPS = 9
NPAT = 8
LANES = 128
COSINES = [math.cos(2.0 * math.pi * m / 5.0) for m in range(5)]
MESH = pl.DeviceIdType.MESH


def lane_iota(shape):
    return lax.broadcasted_iota(jnp.int32, shape, len(shape) - 1)


def row_iota(shape):
    return lax.broadcasted_iota(jnp.int32, shape, len(shape) - 2)


def block_transpose(tiles):
    group = lane_iota(tiles[0].shape) // 16
    tiles = list(tiles)
    for bit in (4, 2, 1):
        keep = (group & bit) == 0
        for k in range(8):
            if k & bit:
                continue
            low, high = tiles[k], tiles[k + bit]
            axis = low.ndim - 1
            tiles[k] = jnp.where(keep, low, pltpu.roll(high, 16 * bit, axis))
            tiles[k + bit] = jnp.where(keep, pltpu.roll(low, LANES - 16 * bit, axis), high)
    return tiles


def kernel(
    full_rows,
    full_cols,
    cells,
    est_ref,
    data_ref,
    axial_ref,
    taps_ref,
    radius_ref,
    codes_ref,
    out_ref,
    rms_ref,
    squares_ref,
    sums_pat,
    sums_tx,
    sums_ty,
    grid_ref,
    final_ref,
    home_ref,
    data_tiles,
    top_ref,
    bottom_ref,
    left_ref,
    right_ref,
    lit_ref,
    blur_ref,
    pred_ref,
    quot_ref,
    forward_ref,
    adjoint_ref,
    axial_fwd,
    axial_adj,
    wave_ext,
    wave_in,
    planes_ref,
    mask_ext,
    valid_ref,
    norm_ref,
    halo_send,
    halo_recv,
    row_send,
    row_recv,
    edge_send,
    left_recv,
    right_recv,
    pat_send,
    pat_recv,
    out_send,
    out_recv,
    sum_send,
    sum_recv,
):
    ty, tx, q = lax.axis_index("ty"), lax.axis_index("tx"), lax.axis_index("pat")
    nty, ntx, npat = lax.axis_size("ty"), lax.axis_size("tx"), lax.axis_size("pat")
    ncol = ntx * npat
    column = tx * npat + q

    def at(dty, dcol):
        c = lax.rem(column + dcol + ncol, ncol)
        return {"ty": lax.rem(ty + dty + nty, nty), "tx": c // npat, "pat": lax.rem(c, npat)}

    def peer(d):
        return {"ty": ty, "tx": tx, "pat": lax.rem(q + d, npat)}

    def shifted(dty, dtx, dq):
        return {
            "ty": lax.rem(ty + dty + nty, nty),
            "tx": lax.rem(tx + dtx + ntx, ntx),
            "pat": lax.rem(q + dq, npat),
        }

    barrier = pltpu.get_barrier_semaphore()
    greet = [(a, b, c) for a in (-1, 0, 1) for b in (-1, 0, 1) for c in range(npat)]
    greet += [(a, 0, 0) for a in range(2, nty - 1)] + [(0, b, 0) for b in range(2, ntx - 1)]
    greet.remove((0, 0, 0))
    for move in greet:
        pl.semaphore_signal(
            barrier, inc=1, device_id=shifted(*move), device_id_type=MESH
        )

    for strip in range(2):
        for half in range(2):
            rows = [est_ref[8 * strip + y, :, LANES * half : LANES * (half + 1)] for y in range(8)]
            for k, tile in enumerate(block_transpose(rows)):
                final_ref[2 * half + k // 4, k % 4, strip] = tile
    grid_ref[0, 1:5, 1:3] = final_ref[q]

    pl.semaphore_wait(barrier, len(greet))

    def halo_copies(t):
        moves = [
            ((slice(1, 5), 1), (slice(1, 5), 3), -1, 0),
            ((slice(1, 5), 2), (slice(1, 5), 0), 1, 0),
            ((1, slice(1, 3)), (5, slice(1, 3)), 0, -1),
            ((4, slice(1, 3)), (0, slice(1, 3)), 0, 1),
            ((1, 1), (5, 3), -1, -1),
            ((4, 1), (0, 3), -1, 1),
            ((1, 2), (5, 0), 1, -1),
            ((4, 2), (0, 0), 1, 1),
        ]
        copies = []
        for k, (source, target, dty, dcol) in enumerate(moves):
            copies.append(
                pltpu.make_async_remote_copy(
                    src_ref=grid_ref.at[(t, *source)],
                    dst_ref=grid_ref.at[(t, *target)],
                    send_sem=halo_send.at[t, k],
                    recv_sem=halo_recv.at[t, k],
                    device_id=at(dty, dcol),
                    device_id_type=MESH,
                )
            )
        return copies

    for copy in halo_copies(0):
        copy.start()

    row_copies = [
        pltpu.make_async_remote_copy(
            src_ref=data_ref.at[12:16],
            dst_ref=top_ref,
            send_sem=row_send.at[0],
            recv_sem=row_recv.at[0],
            device_id=at(1, 0),
            device_id_type=MESH,
        ),
        pltpu.make_async_remote_copy(
            src_ref=data_ref.at[0:4],
            dst_ref=bottom_ref,
            send_sem=row_send.at[1],
            recv_sem=row_recv.at[1],
            device_id=at(-1, 0),
            device_id_type=MESH,
        ),
    ]
    for copy in row_copies:
        copy.start()

    def data_row(row, block, half):
        rows = slice(8 * block, 8 * block + 8)
        lanes = slice(LANES * half, LANES * (half + 1))
        if row < 4:
            return top_ref[row, rows, lanes]
        if row < 20:
            return data_ref[row - 4, rows, lanes]
        return bottom_ref[row - 20, rows, lanes]

    def make_strip(strip):
        first = lane_iota((8, LANES)) < 4
        for block in range(8):
            at_rows = slice(8 * block, 8 * block + 8)
            low = [pltpu.roll(data_row(8 * strip + y, block, 0), 4, 1) for y in range(8)]
            high = [pltpu.roll(data_row(8 * strip + y, block, 1), 4, 1) for y in range(8)]
            for k, tile in enumerate(block_transpose(low)):
                home_ref[k, strip, at_rows] = tile
            mixed = [jnp.where(first, a, b) for a, b in zip(low, high)]
            for k, tile in enumerate(block_transpose(mixed)):
                home_ref[8 + k, strip, at_rows] = tile
            last = high[0]
            group = lane_iota((8, LANES)) // 16
            for y in range(1, 8):
                last = jnp.where(group == y, pltpu.roll(high[y], 16 * y, 1), last)
            home_ref[16, strip, at_rows] = last

    def strip_copies(strip):
        copies = []
        for d in range(1, npat):
            to = lax.rem(q + d, npat)
            copies.append(
                pltpu.make_async_remote_copy(
                    src_ref=home_ref.at[pl.ds(4 * to, 5), strip],
                    dst_ref=data_tiles.at[q, :, strip],
                    send_sem=pat_send.at[strip, d - 1],
                    recv_sem=pat_recv.at[strip, d - 1],
                    device_id=peer(d),
                    device_id_type=MESH,
                )
            )
        return copies

    def edge_copies():
        return [
            pltpu.make_async_remote_copy(
                src_ref=home_ref.at[16],
                dst_ref=left_ref.at[q],
                send_sem=edge_send.at[0],
                recv_sem=left_recv.at[q],
                device_id={"ty": ty, "tx": lax.rem(tx + 1, ntx), "pat": 0},
                device_id_type=MESH,
            ),
            pltpu.make_async_remote_copy(
                src_ref=home_ref.at[0],
                dst_ref=right_ref.at[q],
                send_sem=edge_send.at[1],
                recv_sem=right_recv.at[q],
                device_id={"ty": ty, "tx": lax.rem(tx + ntx - 1, ntx), "pat": npat - 1},
                device_id_type=MESH,
            ),
        ]

    make_strip(1)
    for copy in strip_copies(1):
        copy.start()

    lane = lane_iota((LANES, LANES))
    line = row_iota((LANES, LANES))
    for backward in (False, True):
        target = adjoint_ref if backward else forward_ref
        target[...] = jnp.zeros_like(target)
        for block in range(2):
            row_gap = 8 * block + line // 16 - lane // 16
            for step in range(2):
                col_gap = 16 * step + lax.rem(line, 16) - lax.rem(lane, 16)
                total = jnp.zeros((LANES, LANES), jnp.float32)
                for i in range(TAPS):
                    here = jnp.zeros((LANES, LANES), jnp.float32)
                    for j in range(TAPS):
                        ki, kj = (TAPS - 1 - i, TAPS - 1 - j) if backward else (i, j)
                        tap = jnp.where(abs(kj - 4) <= radius_ref[ki], taps_ref[ki, kj], 0.0)
                        here = jnp.where(col_gap == j, tap, here)
                    total = jnp.where(row_gap == i, here, total)
                values = total.astype(jnp.bfloat16)
                for out_chunk in range(2):
                    start = 256 * (out_chunk + step) + LANES * block
                    target[start : start + LANES, LANES * out_chunk : LANES * (out_chunk + 1)] = values

    spread = (row_iota((256, 32)) % 32 == lane_iota((256, 32))).astype(jnp.bfloat16)
    axial_b = axial_ref[...].astype(jnp.bfloat16)
    same = row_iota((256, 256)) // 32 == lane_iota((256, 256)) // 32
    nt = (((1,), (1,)), ((), ()))
    right_fwd = lax.dot_general(axial_b, spread, nt, preferred_element_type=jnp.float32)
    full = jnp.dot(spread, right_fwd.astype(jnp.bfloat16), preferred_element_type=jnp.float32)
    axial_fwd[...] = jnp.where(same, full, 0.0).astype(jnp.bfloat16)
    left_adj = lax.dot_general(spread, axial_b, nt, preferred_element_type=jnp.float32)
    full = lax.dot_general(left_adj.astype(jnp.bfloat16), spread, nt, preferred_element_type=jnp.float32)
    axial_adj[...] = jnp.where(same, full, 0.0).astype(jnp.bfloat16)

    plane = row_iota((32, LANES)).astype(jnp.float32)
    planes_ref[...] = jnp.cos(plane * (2.0 * math.pi * 3.0 / 32.0))

    def positions(tile, strips, offset):
        spot = lane_iota(tile.shape)
        chunk, strip = tile // strips, tile % strips
        y = ty * 16 + 8 * strip - offset + spot // 16
        x = column * 64 + 16 * chunk - offset + spot % 16
        return y, x

    def waves(count, strips, offset):
        shape = (count * NPAT, LANES)
        index = row_iota(shape)
        y, x = positions(index // NPAT, strips, offset)
        pattern = index % NPAT
        angle = jnp.zeros(shape, jnp.int32)
        phase = jnp.zeros(shape, jnp.int32)
        for p in range(NPAT):
            angle = jnp.where(pattern == p, codes_ref[0, p], angle)
            phase = jnp.where(pattern == p, codes_ref[1, p], phase)
        cx = jnp.where(angle == 0, 2, -1)
        cy = jnp.where(angle == 0, 0, jnp.where(angle == 1, 2, -2))
        value = cx * x + cy * y + phase
        wide = value.astype(jnp.float32)
        m = wide - 5.0 * jnp.floor((wide + 0.5) * 0.2)
        wave = jnp.full(shape, COSINES[0], jnp.float32)
        for k in range(1, 5):
            wave = jnp.where(m == float(k), COSINES[k], wave)
        return 0.7 * wave

    wave_ext[...] = waves(20, 4, 8)
    wave_in[...] = waves(8, 2, 0)

    def inside(shape, strips, offset):
        y, x = positions(row_iota(shape), strips, offset)
        return (y >= 0) & (y < full_rows) & (x >= 0) & (x < full_cols)

    mask_ext[...] = inside((24, LANES), 4, 8).astype(jnp.float32)
    tile15 = (16, LANES)
    valid = inside(tile15, 3, 4) & ((row_iota(tile15) < 12) | (lane_iota(tile15) % 16 < 8))
    valid_ref[...] = valid.astype(jnp.float32)

    for copy in row_copies:
        copy.wait_recv()
    make_strip(0)
    make_strip(2)
    for copy in strip_copies(0) + strip_copies(2) + edge_copies():
        copy.start()
    data_tiles[q] = home_ref[pl.ds(4 * q, 5)]

    column_sum = lax.dot_general(
        axial_b, jnp.ones((32, LANES), jnp.bfloat16), (((0,), (0,)), ((), ())),
        preferred_element_type=jnp.float32,
    )
    cover_in = [
        jnp.broadcast_to(valid_ref[k : k + 1, :], (16, LANES)).astype(jnp.bfloat16)
        for k in range(15)
    ]
    plane_wave = planes_ref[...]
    for strip in range(2):
        for chunk in (0, 2):
            window = jnp.concatenate(
                [cover_in[3 * (chunk + k) + strip + a] for k in range(3) for a in range(2)], axis=1
            )
            cover = jnp.dot(window, adjoint_ref[...], preferred_element_type=jnp.float32)
            cover = cover.astype(jnp.bfloat16).astype(jnp.float32)
            for k in range(2):
                tile = 2 * (chunk + k) + strip
                row = cover[0:1, LANES * k : LANES * (k + 1)]
                light = jnp.zeros((32, LANES), jnp.float32)
                for p in range(NPAT):
                    light = light + (1.0 + wave_in[NPAT * tile + p : NPAT * tile + p + 1, :] * plane_wave)
                norm_ref[tile] = light * (row * column_sum)

    own = lane_iota((8, LANES))
    own_col, own_row = own % 16, own // 16

    def inner_mask(tile):
        chunk, strip = tile // 3, tile % 3
        x, y = 16 * chunk + own_col, 8 * strip + own_row
        return (x >= 4) & (x < 68) & (y >= 4) & (y < 20)

    def predict(strip, chunk):
        tile = 4 * chunk + strip
        if chunk == 4:
            return jnp.dot(
                blur_ref[:, LANES * tile : LANES * (tile + 2)],
                forward_ref[0:256, 0:LANES],
                preferred_element_type=jnp.float32,
            )
        window = jnp.concatenate(
            [blur_ref[:, LANES * (tile + 4 * k) : LANES * (tile + 4 * k + 2)] for k in range(3)], axis=1
        )
        return jnp.dot(window, forward_ref[...], preferred_element_type=jnp.float32)

    def compare(strip, chunk, predicted, squares):
        for k in range(predicted.shape[1] // LANES):
            tile = 3 * (chunk + k) + strip
            ok = valid_ref[tile : tile + 1, :]
            filler = 1.0 - ok
            total = jnp.zeros((8, LANES), jnp.float32)
            for source in range(4):
                data = data_tiles[source, chunk + k, strip]
                guess = predicted[64 * source : 64 * (source + 1), LANES * k : LANES * (k + 1)]
                misfit = data - guess
                total = total + jnp.sum((misfit * misfit).reshape(8, 8, LANES), axis=0)
                quotient = (data * ok) / (guess + filler)
                quot_ref[64 * source : 64 * (source + 1), LANES * tile : LANES * (tile + 1)] = (
                    quotient.astype(jnp.bfloat16)
                )
            squares = squares + jnp.where(inner_mask(tile), total, 0.0)
        return squares

    def iteration(t, first, last=False):
        copies = halo_copies(t)
        for copy in copies:
            copy.wait_recv()
        wave_z = planes_ref[...]
        left_half = lane_iota((32, LANES)) % 16 < 8
        for chunk in range(5):
            for strip in range(4):
                tile = 4 * chunk + strip
                a, b = grid_ref[t, chunk, strip], grid_ref[t, chunk + 1, strip]
                value = jnp.where(left_half, pltpu.roll(a, LANES - 8, 1), pltpu.roll(b, 8, 1))
                value = value * mask_ext[tile : tile + 1, :]
                for p in range(NPAT):
                    light = 1.0 + wave_ext[NPAT * tile + p : NPAT * tile + p + 1, :] * wave_z
                    lit_ref[32 * p : 32 * (p + 1), LANES * tile : LANES * (tile + 1)] = (
                        light * value
                    ).astype(jnp.bfloat16)
        for pair in range(10):
            lanes = slice(256 * pair, 256 * (pair + 1))
            blur_ref[:, lanes] = jnp.dot(
                axial_fwd[...], lit_ref[:, lanes], preferred_element_type=jnp.float32
            ).astype(jnp.bfloat16)
        squares = jnp.zeros((8, LANES), jnp.float32)
        order = [(strip, chunk) for strip in range(3) for chunk in (0, 2, 4)]
        if first:
            for strip, chunk in order:
                width = LANES if chunk == 4 else 2 * LANES
                tile = 5 * strip + chunk
                pred_ref[:, LANES * tile : LANES * tile + width] = predict(strip, chunk)
            for strip in range(3):
                for copy in strip_copies(strip):
                    copy.wait_recv()

            @pl.when(q == 0)
            def _():
                for source in range(4):
                    edge_in(left_ref.at[source], left_recv.at[source])
                    keep = lane_iota((64, LANES)) % 16 < 4
                    for strip in range(3):
                        data_tiles[source, 0, strip] = jnp.where(
                            keep, left_ref[source, strip], data_tiles[source, 0, strip]
                        )

            @pl.when(q == npat - 1)
            def _():
                for source in range(4):
                    edge_in(right_ref.at[source], right_recv.at[source])
                    keep = lane_iota((64, LANES)) % 16 < 4
                    for strip in range(3):
                        data_tiles[source, 4, strip] = jnp.where(
                            keep, data_tiles[source, 4, strip], right_ref[source, strip]
                        )

            for strip, chunk in order:
                width = LANES if chunk == 4 else 2 * LANES
                tile = 5 * strip + chunk
                squares = compare(
                    strip, chunk, pred_ref[:, LANES * tile : LANES * tile + width], squares
                )
        else:
            for strip, chunk in order:
                squares = compare(strip, chunk, predict(strip, chunk), squares)
        squares_ref[t] = squares
        if last:
            share = jnp.zeros((8, LANES), jnp.float32)
            for k in range(ITERS):
                total = jnp.sum(squares_ref[k], axis=0, keepdims=True)
                share = jnp.where(row_iota((8, LANES)) == k, total, share)
            send_sums(0, share)
        updated = []
        for strip in range(2):
            for chunk in (0, 2):
                tile = 3 * chunk + strip
                window = jnp.concatenate(
                    [quot_ref[:, LANES * (tile + 3 * k) : LANES * (tile + 3 * k + 2)] for k in range(3)],
                    axis=1,
                )
                spread_back = jnp.dot(
                    window, adjoint_ref[...], preferred_element_type=jnp.float32
                ).astype(jnp.bfloat16)
                gathered = jnp.dot(
                    axial_adj[...], spread_back, preferred_element_type=jnp.float32
                )
                for k in range(2):
                    here = 2 * (chunk + k) + strip
                    summed = jnp.zeros((32, LANES), jnp.float32)
                    for p in range(NPAT):
                        light = 1.0 + wave_in[NPAT * here + p : NPAT * here + p + 1, :] * wave_z
                        summed = summed + light * gathered[
                            32 * p : 32 * (p + 1), LANES * k : LANES * (k + 1)
                        ]
                    current = grid_ref[t, 1 + chunk + k, 1 + strip]
                    updated.append((chunk + k, strip, current * summed / norm_ref[here]))
                if last and (strip, chunk) == (0, 2):
                    send_sums(1, gather_sums(0))
        return updated, copies

    stages = [
        (sums_pat, npat, q, lambda d: shifted(0, 0, d)),
        (sums_tx, ntx, tx, lambda d: shifted(0, d, 0)),
        (sums_ty, nty, ty, lambda d: shifted(d, 0, 0)),
    ]

    def sum_copies(stage):
        slots, count, me, device = stages[stage]
        return [
            pltpu.make_async_remote_copy(
                src_ref=slots.at[me],
                dst_ref=slots.at[me],
                send_sem=sum_send.at[stage, d - 1],
                recv_sem=sum_recv.at[stage, d - 1],
                device_id=device(d),
                device_id_type=MESH,
            )
            for d in range(1, count)
        ]

    def send_sums(stage, value):
        slots, _, me, _ = stages[stage]
        slots[me] = value
        for copy in sum_copies(stage):
            copy.start()

    def gather_sums(stage):
        for copy in sum_copies(stage):
            copy.wait()
        slots, count, _, _ = stages[stage]
        total = slots[0]
        for k in range(1, count):
            total = total + slots[k]
        return total

    def edge_in(ref, sem):
        pltpu.make_async_copy(ref, ref, sem).wait()

    def advance(t, first):
        updated, copies = iteration(t, first)
        for chunk, strip, value in updated:
            grid_ref[t + 1, 1 + chunk, 1 + strip] = value
        for copy in halo_copies(t + 1):
            copy.start()
        for copy in copies:
            copy.wait_send()

    advance(0, True)
    for copy in row_copies + strip_copies(0) + strip_copies(1) + strip_copies(2) + edge_copies():
        copy.wait_send()

    @pl.loop(1, ITERS - 1)
    def _(t):
        advance(t, False)

    updated, copies = iteration(ITERS - 1, False, True)
    for chunk, strip, value in updated:
        final_ref[q, chunk, strip] = value
    outs = [
        pltpu.make_async_remote_copy(
            src_ref=final_ref.at[q],
            dst_ref=final_ref.at[q],
            send_sem=out_send.at[d - 1],
            recv_sem=out_recv.at[d - 1],
            device_id=peer(d),
            device_id_type=MESH,
        )
        for d in range(1, npat)
    ]
    for copy in outs:
        copy.start()
    send_sums(2, gather_sums(1))
    for copy in copies:
        copy.wait_send()
    for copy in outs:
        copy.wait()
    for strip in range(2):
        for half in range(2):
            tiles = [final_ref[2 * half + k // 4, k % 4, strip] for k in range(8)]
            for y, row in enumerate(block_transpose(tiles)):
                out_ref[8 * strip + y, :, LANES * half : LANES * (half + 1)] = row
    total = jnp.sum(gather_sums(2), axis=1, keepdims=True)
    rms_ref[...] = jnp.broadcast_to(jnp.sqrt(total / cells), (8, LANES))


def per_device(estimate, data, axial, lateral_kernel, psf_radius, pattern_codes):
    planes, height, width = estimate.shape
    local = data.shape[0]
    full_rows = height * lax.axis_size("ty")
    full_cols = width * lax.axis_size("tx")
    est_rows = estimate.transpose(1, 0, 2)
    data_rows = data.transpose(2, 0, 1, 3).reshape(height, local * planes, width)
    vmem = pl.BlockSpec(memory_space=pltpu.VMEM)
    smem = pl.BlockSpec(memory_space=pltpu.SMEM)
    f32, bf16 = jnp.float32, jnp.bfloat16
    dma = pltpu.SemaphoreType.DMA
    cells = float(local * lax.axis_size("pat") * planes * full_rows * full_cols)
    rows, rms = pl.pallas_call(
        functools.partial(kernel, full_rows, full_cols, cells),
        name="deconvolve",
        out_shape=(
            jax.ShapeDtypeStruct((height, planes, width), f32),
            jax.ShapeDtypeStruct((8, LANES), f32),
        ),
        in_specs=[vmem, vmem, vmem, smem, smem, smem],
        out_specs=(vmem, vmem),
        scratch_shapes=[
            pltpu.VMEM((ITERS, 8, LANES), f32),
            pltpu.VMEM((lax.axis_size("pat"), 8, LANES), f32),
            pltpu.VMEM((lax.axis_size("tx"), 8, LANES), f32),
            pltpu.VMEM((lax.axis_size("ty"), 8, LANES), f32),
            pltpu.VMEM((ITERS, 6, 4, 32, LANES), f32),
            pltpu.VMEM((4, 4, 2, 32, LANES), f32),
            pltpu.VMEM((17, 3, 64, LANES), f32),
            pltpu.VMEM((4, 5, 3, 64, LANES), f32),
            pltpu.VMEM((4, 64, 256), f32),
            pltpu.VMEM((4, 64, 256), f32),
            pltpu.VMEM((4, 3, 64, LANES), f32),
            pltpu.VMEM((4, 3, 64, LANES), f32),
            pltpu.VMEM((256, 20 * LANES), bf16),
            pltpu.VMEM((256, 20 * LANES), bf16),
            pltpu.VMEM((256, 15 * LANES), f32),
            pltpu.VMEM((256, 15 * LANES), bf16),
            pltpu.VMEM((768, 256), bf16),
            pltpu.VMEM((768, 256), bf16),
            pltpu.VMEM((256, 256), bf16),
            pltpu.VMEM((256, 256), bf16),
            pltpu.VMEM((20 * NPAT, LANES), f32),
            pltpu.VMEM((8 * NPAT, LANES), f32),
            pltpu.VMEM((32, LANES), f32),
            pltpu.VMEM((24, LANES), f32),
            pltpu.VMEM((16, LANES), f32),
            pltpu.VMEM((8, 32, LANES), f32),
            dma((ITERS, 8)),
            dma((ITERS, 8)),
            dma((2,)),
            dma((2,)),
            dma((2,)),
            dma((4,)),
            dma((4,)),
            dma((3, 3)),
            dma((3, 3)),
            dma((3,)),
            dma((3,)),
            dma((3, 7)),
            dma((3, 7)),
        ],
        compiler_params=pltpu.CompilerParams(
            collective_id=0, has_side_effects=True, vmem_limit_bytes=56 * 1024 * 1024
        ),
    )(est_rows, data_rows, axial, lateral_kernel, psf_radius, pattern_codes)
    return rows.transpose(1, 0, 2), rms[:ITERS, 0]


def solution(mesh):
    in_specs = (P(None, "ty", "tx"), P("pat", None, "ty", "tx"), P(), P(), P(), P())
    out_specs = (P(None, "ty", "tx"), P())
    return jax.shard_map(
        per_device, mesh=mesh, in_specs=in_specs, out_specs=out_specs, check_vma=False
    )
```

```python
import functools
import math

import jax
import jax.numpy as jnp
from jax import lax
from jax.experimental import pallas as pl
from jax.experimental.pallas import tpu as pltpu
from jax.sharding import PartitionSpec as P

ITERS = 4
TAPS = 9
NPAT = 8
LANES = 128
COSINES = [math.cos(2.0 * math.pi * m / 5.0) for m in range(5)]
MESH = pl.DeviceIdType.MESH


def lane_iota(shape):
    return lax.broadcasted_iota(jnp.int32, shape, len(shape) - 1)


def row_iota(shape):
    return lax.broadcasted_iota(jnp.int32, shape, len(shape) - 2)


def block_transpose(tiles):
    group = lane_iota(tiles[0].shape) // 16
    tiles = list(tiles)
    for bit in (4, 2, 1):
        keep = (group & bit) == 0
        for k in range(8):
            if k & bit:
                continue
            low, high = tiles[k], tiles[k + bit]
            axis = low.ndim - 1
            tiles[k] = jnp.where(keep, low, pltpu.roll(high, 16 * bit, axis))
            tiles[k + bit] = jnp.where(keep, pltpu.roll(low, LANES - 16 * bit, axis), high)
    return tiles


def kernel(
    full_rows,
    full_cols,
    cells,
    est_ref,
    data_ref,
    axial_ref,
    taps_ref,
    radius_ref,
    codes_ref,
    out_ref,
    rms_ref,
    squares_ref,
    sums_row,
    sums_ty,
    grid_ref,
    final_ref,
    home_ref,
    data_tiles,
    top_ref,
    bottom_ref,
    left_ref,
    right_ref,
    lit_ref,
    blur_ref,
    pred_ref,
    quot_ref,
    forward_ref,
    adjoint_ref,
    axial_fwd,
    axial_adj,
    wave_ext,
    wave_in,
    planes_ref,
    mask_ext,
    valid_ref,
    norm_ref,
    halo_send,
    halo_recv,
    row_send,
    row_recv,
    edge_send,
    left_recv,
    right_recv,
    pat_send,
    pat_recv,
    out_send,
    out_recv,
    sum_send,
    sum_recv,
):
    ty, tx, q = lax.axis_index("ty"), lax.axis_index("tx"), lax.axis_index("pat")
    nty, ntx, npat = lax.axis_size("ty"), lax.axis_size("tx"), lax.axis_size("pat")
    ncol = ntx * npat

    def turned(tile, place):
        return jnp.where(lax.rem(tile, 2) == 0, place, npat - 1 - place)

    mine = turned(tx, q)
    column = tx * npat + mine

    def at(dty, dcol):
        c = lax.rem(column + dcol + ncol, ncol)
        tile = c // npat
        return {
            "ty": lax.rem(ty + dty + nty, nty),
            "tx": tile,
            "pat": turned(tile, lax.rem(c, npat)),
        }

    def shifted(dty, dtx, dq):
        return {
            "ty": lax.rem(ty + dty + nty, nty),
            "tx": lax.rem(tx + dtx + ntx, ntx),
            "pat": lax.rem(q + dq, npat),
        }

    def peer(d):
        return shifted(0, 0, d)

    barrier = pltpu.get_barrier_semaphore()
    greet = [(0, b, c) for b in range(ntx) for c in range(npat)]
    greet += [(a, b, c) for a in (-1, 1) for b in (-1, 0, 1) for c in range(npat)]
    greet += [(a, 0, 0) for a in range(2, nty - 1)]
    greet.remove((0, 0, 0))
    for move in greet:
        pl.semaphore_signal(
            barrier, inc=1, device_id=shifted(*move), device_id_type=MESH
        )

    for strip in range(2):
        for half in range(2):
            rows = [est_ref[8 * strip + y, :, LANES * half : LANES * (half + 1)] for y in range(8)]
            for k, tile in enumerate(block_transpose(rows)):
                final_ref[2 * half + k // 4, k % 4, strip] = tile
    grid_ref[0, 1:5, 1:3] = final_ref[mine]

    moves = [
        ((slice(1, 5), 1), (slice(1, 5), 3), -1, 0),
        ((slice(1, 5), 2), (slice(1, 5), 0), 1, 0),
        ((1, 1), (5, 1), 0, -1),
        ((4, 1), (0, 1), 0, 1),
        ((1, 2), (5, 2), 0, -1),
        ((4, 2), (0, 2), 0, 1),
        ((1, 1), (5, 3), -1, -1),
        ((4, 1), (0, 3), -1, 1),
        ((1, 2), (5, 0), 1, -1),
        ((4, 2), (0, 0), 1, 1),
    ]
    from_strip = ((2, 3, 0, 6, 7), (4, 5, 1, 8, 9))
    side_halo = (2, 3, 4, 5)
    row_halo = {0: (1, 8, 9), 3: (0, 6, 7)}

    def halo_copies(t, which):
        copies = []
        for k in which:
            source, target, dty, dcol = moves[k]
            copies.append(
                pltpu.make_async_remote_copy(
                    src_ref=grid_ref.at[(t, *source)],
                    dst_ref=grid_ref.at[(t, *target)],
                    send_sem=halo_send.at[t, k],
                    recv_sem=halo_recv.at[t, k],
                    device_id=at(dty, dcol),
                    device_id_type=MESH,
                )
            )
        return copies

    row_copies = [
        pltpu.make_async_remote_copy(
            src_ref=data_ref.at[12:16],
            dst_ref=top_ref,
            send_sem=row_send.at[0],
            recv_sem=row_recv.at[0],
            device_id=at(1, 0),
            device_id_type=MESH,
        ),
        pltpu.make_async_remote_copy(
            src_ref=data_ref.at[0:4],
            dst_ref=bottom_ref,
            send_sem=row_send.at[1],
            recv_sem=row_recv.at[1],
            device_id=at(-1, 0),
            device_id_type=MESH,
        ),
    ]
    def data_row(row, block, half):
        rows = slice(8 * block, 8 * block + 8)
        lanes = slice(LANES * half, LANES * (half + 1))
        if row < 4:
            return top_ref[row, rows, lanes]
        if row < 20:
            return data_ref[row - 4, rows, lanes]
        return bottom_ref[row - 20, rows, lanes]

    def make_strip(strip):
        first = lane_iota((8, LANES)) < 4
        for block in range(8):
            at_rows = slice(8 * block, 8 * block + 8)
            low = [pltpu.roll(data_row(8 * strip + y, block, 0), 4, 1) for y in range(8)]
            high = [pltpu.roll(data_row(8 * strip + y, block, 1), 4, 1) for y in range(8)]
            for k, tile in enumerate(block_transpose(low)):
                home_ref[k, strip, at_rows] = tile
            mixed = [jnp.where(first, a, b) for a, b in zip(low, high)]
            for k, tile in enumerate(block_transpose(mixed)):
                home_ref[8 + k, strip, at_rows] = tile
            last = high[0]
            group = lane_iota((8, LANES)) // 16
            for y in range(1, 8):
                last = jnp.where(group == y, pltpu.roll(high[y], 16 * y, 1), last)
            home_ref[16, strip, at_rows] = last

    def strip_copies(strip):
        copies = []
        for d in range(1, npat):
            to = turned(tx, lax.rem(q + d, npat))
            copies.append(
                pltpu.make_async_remote_copy(
                    src_ref=home_ref.at[pl.ds(4 * to, 5), strip],
                    dst_ref=data_tiles.at[q, :, strip],
                    send_sem=pat_send.at[strip, d - 1],
                    recv_sem=pat_recv.at[strip, d - 1],
                    device_id=peer(d),
                    device_id_type=MESH,
                )
            )
        return copies

    def edge_copies(strip):
        after, before = lax.rem(tx + 1, ntx), lax.rem(tx + ntx - 1, ntx)
        return [
            pltpu.make_async_remote_copy(
                src_ref=home_ref.at[16, strip],
                dst_ref=left_ref.at[q, strip],
                send_sem=edge_send.at[0, strip],
                recv_sem=left_recv.at[q, strip],
                device_id={"ty": ty, "tx": after, "pat": turned(after, 0)},
                device_id_type=MESH,
            ),
            pltpu.make_async_remote_copy(
                src_ref=home_ref.at[0, strip],
                dst_ref=right_ref.at[q, strip],
                send_sem=edge_send.at[1, strip],
                recv_sem=right_recv.at[q, strip],
                device_id={"ty": ty, "tx": before, "pat": turned(before, npat - 1)},
                device_id_type=MESH,
            ),
        ]

    make_strip(1)
    pl.semaphore_wait(barrier, len(greet))
    for copy in row_copies + halo_copies(0, side_halo):
        copy.start()
    for copy in strip_copies(1) + edge_copies(1):
        copy.start()
    for copy in halo_copies(0, row_halo[0] + row_halo[3]):
        copy.start()

    taps = [
        [jnp.where(abs(j - 4) <= radius_ref[i], taps_ref[i, j], 0.0) for j in range(TAPS)]
        for i in range(TAPS)
    ]
    narrow = (16, LANES)
    group = lane_iota(narrow) // 16
    for backward in (False, True):
        target = adjoint_ref if backward else forward_ref
        target[0:256, LANES:] = jnp.zeros((256, LANES), jnp.bfloat16)
        target[512:768, 0:LANES] = jnp.zeros((256, LANES), jnp.bfloat16)

        def tap(i, j):
            return taps[TAPS - 1 - i][TAPS - 1 - j] if backward else taps[i][j]

        for step in range(2):
            gap = 16 * step + row_iota(narrow) - lane_iota(narrow) % 16
            low = jnp.zeros(narrow, jnp.float32)
            high = jnp.zeros(narrow, jnp.float32)
            for j in range(TAPS):
                values = jnp.zeros(narrow, jnp.float32)
                for g in range(8):
                    values = jnp.where(group == g, tap(7 - g, j), values)
                high = jnp.where(gap == j, values, high)
                low = jnp.where((gap == j) & (group == 7), tap(8, j), low)
            for block in range(2):
                for y in range(8):
                    if block:
                        first = 7 - y
                        left, right = low, high
                    else:
                        first = 7 - y
                        left, right = high, None
                    turn = (LANES - 16 * first) % LANES
                    left = pltpu.roll(left, turn, 1) if turn else left
                    if right is None:
                        right = jnp.zeros(narrow, jnp.float32)
                    else:
                        right = pltpu.roll(right, turn, 1) if turn else right
                    values = jnp.where(group < 8 - first, left, right).astype(jnp.bfloat16)
                    for out_chunk in range(2):
                        start = 256 * (out_chunk + step) + LANES * block + 16 * y
                        target[start : start + 16, LANES * out_chunk : LANES * (out_chunk + 1)] = values

    spread = (row_iota((256, 32)) % 32 == lane_iota((256, 32))).astype(jnp.bfloat16)
    axial_b = axial_ref[...].astype(jnp.bfloat16)
    same = row_iota((256, 256)) // 32 == lane_iota((256, 256)) // 32
    nt = (((1,), (1,)), ((), ()))
    right_fwd = lax.dot_general(axial_b, spread, nt, preferred_element_type=jnp.float32)
    full = jnp.dot(spread, right_fwd.astype(jnp.bfloat16), preferred_element_type=jnp.float32)
    axial_fwd[...] = jnp.where(same, full, 0.0).astype(jnp.bfloat16)
    left_adj = lax.dot_general(spread, axial_b, nt, preferred_element_type=jnp.float32)
    full = lax.dot_general(left_adj.astype(jnp.bfloat16), spread, nt, preferred_element_type=jnp.float32)
    axial_adj[...] = jnp.where(same, full, 0.0).astype(jnp.bfloat16)

    for copy in row_copies:
        copy.wait_recv()
    for strip in (2, 0):
        make_strip(strip)
        for copy in strip_copies(strip) + edge_copies(strip):
            copy.start()
    data_tiles[q] = home_ref[pl.ds(4 * mine, 5)]

    plane = row_iota((32, LANES)).astype(jnp.float32)
    planes_ref[...] = jnp.cos(plane * (2.0 * math.pi * 3.0 / 32.0))

    def positions(tile, strips, offset):
        spot = lane_iota(tile.shape)
        chunk, strip = tile // strips, tile % strips
        y = ty * 16 + 8 * strip - offset + spot // 16
        x = column * 64 + 16 * chunk - offset + spot % 16
        return y, x

    def waves(count, strips, offset):
        shape = (count * NPAT, LANES)
        index = row_iota(shape)
        y, x = positions(index // NPAT, strips, offset)
        pattern = index % NPAT
        angle = jnp.zeros(shape, jnp.int32)
        phase = jnp.zeros(shape, jnp.int32)
        for p in range(NPAT):
            angle = jnp.where(pattern == p, codes_ref[0, p], angle)
            phase = jnp.where(pattern == p, codes_ref[1, p], phase)
        cx = jnp.where(angle == 0, 2, -1)
        cy = jnp.where(angle == 0, 0, jnp.where(angle == 1, 2, -2))
        value = cx * x + cy * y + phase
        wide = value.astype(jnp.float32)
        m = wide - 5.0 * jnp.floor((wide + 0.5) * 0.2)
        wave = jnp.full(shape, COSINES[0], jnp.float32)
        for k in range(1, 5):
            wave = jnp.where(m == float(k), COSINES[k], wave)
        return 0.7 * wave

    wave_ext[...] = waves(20, 4, 8)
    wave_in[...] = waves(8, 2, 0)

    def inside(shape, strips, offset):
        y, x = positions(row_iota(shape), strips, offset)
        return (y >= 0) & (y < full_rows) & (x >= 0) & (x < full_cols)

    mask_ext[...] = inside((24, LANES), 4, 8).astype(jnp.float32)
    tile15 = (16, LANES)
    valid = inside(tile15, 3, 4) & ((row_iota(tile15) < 12) | (lane_iota(tile15) % 16 < 8))
    valid_ref[...] = valid.astype(jnp.float32)

    column_sum = lax.dot_general(
        axial_b, jnp.ones((32, LANES), jnp.bfloat16), (((0,), (0,)), ((), ())),
        preferred_element_type=jnp.float32,
    )
    cover_in = [
        jnp.broadcast_to(valid_ref[k : k + 1, :], (16, LANES)).astype(jnp.bfloat16)
        for k in range(15)
    ]
    plane_wave = planes_ref[...]
    for strip in range(2):
        for chunk in (0, 2):
            window = jnp.concatenate(
                [cover_in[3 * (chunk + k) + strip + a] for k in range(3) for a in range(2)], axis=1
            )
            cover = jnp.dot(window, adjoint_ref[...], preferred_element_type=jnp.float32)
            cover = cover.astype(jnp.bfloat16).astype(jnp.float32)
            for k in range(2):
                tile = 2 * (chunk + k) + strip
                row = cover[0:1, LANES * k : LANES * (k + 1)]
                light = jnp.zeros((32, LANES), jnp.float32)
                for p in range(NPAT):
                    light = light + (1.0 + wave_in[NPAT * tile + p : NPAT * tile + p + 1, :] * plane_wave)
                norm_ref[tile] = light * (row * column_sum)

    own = lane_iota((8, LANES))
    own_col, own_row = own % 16, own // 16

    def inner_mask(tile):
        chunk, strip = tile // 3, tile % 3
        x, y = 16 * chunk + own_col, 8 * strip + own_row
        return (x >= 4) & (x < 68) & (y >= 4) & (y < 20)

    def predict(strip, chunk):
        tile = 4 * chunk + strip
        if chunk == 4:
            return jnp.dot(
                blur_ref[:, LANES * tile : LANES * (tile + 2)],
                forward_ref[0:256, 0:LANES],
                preferred_element_type=jnp.float32,
            )
        window = jnp.concatenate(
            [blur_ref[:, LANES * (tile + 4 * k) : LANES * (tile + 4 * k + 2)] for k in range(3)], axis=1
        )
        return jnp.dot(window, forward_ref[...], preferred_element_type=jnp.float32)

    def compare(strip, chunk, predicted, squares):
        for k in range(predicted.shape[1] // LANES):
            tile = 3 * (chunk + k) + strip
            ok = valid_ref[tile : tile + 1, :]
            filler = 1.0 - ok
            total = jnp.zeros((8, LANES), jnp.float32)
            for source in range(4):
                data = data_tiles[source, chunk + k, strip]
                guess = predicted[64 * source : 64 * (source + 1), LANES * k : LANES * (k + 1)]
                misfit = data - guess
                total = total + jnp.sum((misfit * misfit).reshape(8, 8, LANES), axis=0)
                quotient = (data * ok) / (guess + filler)
                quot_ref[64 * source : 64 * (source + 1), LANES * tile : LANES * (tile + 1)] = (
                    quotient.astype(jnp.bfloat16)
                )
            squares = squares + jnp.where(inner_mask(tile), total, 0.0)
        return squares

    stages = [
        (sums_row, ncol, tx * npat + q, lambda d: shifted(0, d // npat, d % npat)),
        (sums_ty, nty, ty, lambda d: shifted(d, 0, 0)),
    ]

    def sum_copies(stage):
        slots, count, me, device = stages[stage]
        return [
            pltpu.make_async_remote_copy(
                src_ref=slots.at[me],
                dst_ref=slots.at[me],
                send_sem=sum_send.at[stage, d - 1],
                recv_sem=sum_recv.at[stage, d - 1],
                device_id=device(d),
                device_id_type=MESH,
            )
            for d in range(1, count)
        ]

    def send_sums(stage, value):
        slots, _, me, _ = stages[stage]
        slots[me] = value
        for copy in sum_copies(stage):
            copy.start()

    def gather_sums(stage):
        for copy in sum_copies(stage):
            copy.wait()
        slots, count, _, _ = stages[stage]
        total = slots[0]
        for k in range(1, count):
            total = total + slots[k]
        return total

    def lit_tiles(t, strips):
        wave_z = planes_ref[...]
        left_half = lane_iota((32, LANES)) % 16 < 8
        for chunk in range(5):
            for strip in strips:
                tile = 4 * chunk + strip
                a, b = grid_ref[t, chunk, strip], grid_ref[t, chunk + 1, strip]
                value = jnp.where(left_half, pltpu.roll(a, LANES - 8, 1), pltpu.roll(b, 8, 1))
                value = value * mask_ext[tile : tile + 1, :]
                for p in range(NPAT):
                    light = 1.0 + wave_ext[NPAT * tile + p : NPAT * tile + p + 1, :] * wave_z
                    lit_ref[32 * p : 32 * (p + 1), LANES * tile : LANES * (tile + 1)] = (
                        light * value
                    ).astype(jnp.bfloat16)
        tiles = [4 * chunk + strip for chunk in range(5) for strip in strips]
        for k in range(0, len(tiles), 2):
            pair = [slice(LANES * tile, LANES * (tile + 1)) for tile in tiles[k : k + 2]]
            lit = jnp.concatenate([lit_ref[:, lanes] for lanes in pair], axis=1)
            blurred = jnp.dot(axial_fwd[...], lit, preferred_element_type=jnp.float32)
            for n, lanes in enumerate(pair):
                blur_ref[:, lanes] = blurred[:, LANES * n : LANES * (n + 1)].astype(jnp.bfloat16)

    def wait_halo(t, which):
        for copy in halo_copies(t, which):
            copy.wait_recv()

    def wait_data(strip):
        for copy in strip_copies(strip):
            copy.wait_recv()
        keep = lane_iota((64, LANES)) % 16 < 4

        @pl.when(mine == 0)
        def _():
            for source in range(4):
                arrived(left_ref.at[source, strip], left_recv.at[source, strip])
                data_tiles[source, 0, strip] = jnp.where(
                    keep, left_ref[source, strip], data_tiles[source, 0, strip]
                )

        @pl.when(mine == npat - 1)
        def _():
            for source in range(4):
                arrived(right_ref.at[source, strip], right_recv.at[source, strip])
                data_tiles[source, 4, strip] = jnp.where(
                    keep, data_tiles[source, 4, strip], right_ref[source, strip]
                )

    def arrived(ref, sem):
        pltpu.make_async_copy(ref, ref, sem).wait()

    def back_project(t, strip):
        wave_z = planes_ref[...]
        updated = []
        for chunk in (0, 2):
            tile = 3 * chunk + strip
            window = jnp.concatenate(
                [quot_ref[:, LANES * (tile + 3 * k) : LANES * (tile + 3 * k + 2)] for k in range(3)],
                axis=1,
            )
            spread_back = jnp.dot(
                window, adjoint_ref[...], preferred_element_type=jnp.float32
            ).astype(jnp.bfloat16)
            gathered = jnp.dot(axial_adj[...], spread_back, preferred_element_type=jnp.float32)
            for k in range(2):
                here = 2 * (chunk + k) + strip
                summed = jnp.zeros((32, LANES), jnp.float32)
                for p in range(NPAT):
                    light = 1.0 + wave_in[NPAT * here + p : NPAT * here + p + 1, :] * wave_z
                    summed = summed + light * gathered[
                        32 * p : 32 * (p + 1), LANES * k : LANES * (k + 1)
                    ]
                current = grid_ref[t, 1 + chunk + k, 1 + strip]
                updated.append((chunk + k, current * summed / norm_ref[here]))
        return updated

    def out_copies(strip):
        return [
            pltpu.make_async_remote_copy(
                src_ref=final_ref.at[mine, :, strip],
                dst_ref=final_ref.at[mine, :, strip],
                send_sem=out_send.at[strip, d - 1],
                recv_sem=out_recv.at[strip, d - 1],
                device_id=peer(d),
                device_id_type=MESH,
            )
            for d in range(1, npat)
        ]

    def compare_strip(t, strip, squares):
        for chunk in (0, 2, 4):
            if t == 0:
                width = LANES if chunk == 4 else 2 * LANES
                tile = 5 * strip + chunk
                predicted = pred_ref[:, LANES * tile : LANES * tile + width]
            else:
                predicted = predict(strip, chunk)
            squares = compare(strip, chunk, predicted, squares)
        return squares

    def finish_strip(t, strip):
        for chunk, value in back_project(t, strip):
            if t == ITERS - 1:
                final_ref[mine, chunk, strip] = value
            else:
                grid_ref[t + 1, 1 + chunk, 1 + strip] = value
        if t == ITERS - 1:
            copies = out_copies(strip)
        else:
            copies = halo_copies(t + 1, from_strip[strip])
        for copy in copies:
            copy.start()

    for t in range(ITERS):
        early = 1 - t % 2
        near, far = (2, 0) if early == 1 else (0, 2)
        near_halo, far_halo = (3, 0) if early == 1 else (0, 3)
        squares = jnp.zeros((8, LANES), jnp.float32)
        wait_halo(t, side_halo)
        lit_tiles(t, (1, 2))
        if t == 0:
            wait_halo(t, row_halo[0] + row_halo[3])
            lit_tiles(t, (0, 3))
            for strip in range(3):
                for chunk in (0, 2, 4):
                    width = LANES if chunk == 4 else 2 * LANES
                    tile = 5 * strip + chunk
                    pred_ref[:, LANES * tile : LANES * tile + width] = predict(strip, chunk)
            wait_data(1)
        squares = compare_strip(t, 1, squares)
        if t == 0:
            wait_data(near)
        else:
            wait_halo(t, row_halo[near_halo])
            lit_tiles(t, (near_halo,))
        squares = compare_strip(t, near, squares)
        finish_strip(t, early)
        if t == 0:
            wait_data(far)
        else:
            wait_halo(t, row_halo[far_halo])
            lit_tiles(t, (far_halo,))
        squares = compare_strip(t, far, squares)
        squares_ref[t] = squares
        if t == ITERS - 1:
            share = jnp.zeros((8, LANES), jnp.float32)
            for k in range(ITERS):
                total = jnp.sum(squares_ref[k], axis=0, keepdims=True)
                share = jnp.where(row_iota((8, LANES)) == k, total, share)
            send_sums(0, share)
        finish_strip(t, 1 - early)

    send_sums(1, gather_sums(0))
    for copy in row_copies:
        copy.wait_send()
    for strip in range(3):
        for copy in strip_copies(strip) + edge_copies(strip):
            copy.wait_send()
    for t in range(ITERS):
        for copy in halo_copies(t, range(len(moves))):
            copy.wait_send()
    for strip in (early, 1 - early):
        for copy in out_copies(strip):
            copy.wait()
        for half in range(2):
            tiles = [final_ref[2 * half + k // 4, k % 4, strip] for k in range(8)]
            for y, row in enumerate(block_transpose(tiles)):
                out_ref[8 * strip + y, :, LANES * half : LANES * (half + 1)] = row
    total = jnp.sum(gather_sums(1), axis=1, keepdims=True)
    rms_ref[...] = jnp.broadcast_to(jnp.sqrt(total / cells), (8, LANES))


def per_device(estimate, data, axial, lateral_kernel, psf_radius, pattern_codes):
    planes, height, width = estimate.shape
    local = data.shape[0]
    full_rows = height * lax.axis_size("ty")
    full_cols = width * lax.axis_size("tx")
    est_rows = estimate.transpose(1, 0, 2)
    data_rows = data.transpose(2, 0, 1, 3).reshape(height, local * planes, width)
    vmem = pl.BlockSpec(memory_space=pltpu.VMEM)
    smem = pl.BlockSpec(memory_space=pltpu.SMEM)
    f32, bf16 = jnp.float32, jnp.bfloat16
    dma = pltpu.SemaphoreType.DMA
    cells = float(local * lax.axis_size("pat") * planes * full_rows * full_cols)
    rows, rms = pl.pallas_call(
        functools.partial(kernel, full_rows, full_cols, cells),
        name="deconvolve",
        out_shape=(
            jax.ShapeDtypeStruct((height, planes, width), f32),
            jax.ShapeDtypeStruct((8, LANES), f32),
        ),
        in_specs=[vmem, vmem, vmem, smem, smem, smem],
        out_specs=(vmem, vmem),
        scratch_shapes=[
            pltpu.VMEM((ITERS, 8, LANES), f32),
            pltpu.VMEM((lax.axis_size(("tx", "pat")), 8, LANES), f32),
            pltpu.VMEM((lax.axis_size("ty"), 8, LANES), f32),
            pltpu.VMEM((ITERS, 6, 4, 32, LANES), f32),
            pltpu.VMEM((4, 4, 2, 32, LANES), f32),
            pltpu.VMEM((17, 3, 64, LANES), f32),
            pltpu.VMEM((4, 5, 3, 64, LANES), f32),
            pltpu.VMEM((4, 64, 256), f32),
            pltpu.VMEM((4, 64, 256), f32),
            pltpu.VMEM((4, 3, 64, LANES), f32),
            pltpu.VMEM((4, 3, 64, LANES), f32),
            pltpu.VMEM((256, 20 * LANES), bf16),
            pltpu.VMEM((256, 20 * LANES), bf16),
            pltpu.VMEM((256, 15 * LANES), f32),
            pltpu.VMEM((256, 15 * LANES), bf16),
            pltpu.VMEM((768, 256), bf16),
            pltpu.VMEM((768, 256), bf16),
            pltpu.VMEM((256, 256), bf16),
            pltpu.VMEM((256, 256), bf16),
            pltpu.VMEM((20 * NPAT, LANES), f32),
            pltpu.VMEM((8 * NPAT, LANES), f32),
            pltpu.VMEM((32, LANES), f32),
            pltpu.VMEM((24, LANES), f32),
            pltpu.VMEM((16, LANES), f32),
            pltpu.VMEM((8, 32, LANES), f32),
            dma((ITERS, 10)),
            dma((ITERS, 10)),
            dma((2,)),
            dma((2,)),
            dma((2, 3)),
            dma((4, 3)),
            dma((4, 3)),
            dma((3, 3)),
            dma((3, 3)),
            dma((2, 3)),
            dma((2, 3)),
            dma((2, 15)),
            dma((2, 15)),
        ],
        compiler_params=pltpu.CompilerParams(
            collective_id=0, has_side_effects=True, vmem_limit_bytes=56 * 1024 * 1024
        ),
    )(est_rows, data_rows, axial, lateral_kernel, psf_radius, pattern_codes)
    return rows.transpose(1, 0, 2), rms[:ITERS, 0]


def solution(mesh):
    in_specs = (P(None, "ty", "tx"), P("pat", None, "ty", "tx"), P(), P(), P(), P())
    out_specs = (P(None, "ty", "tx"), P())
    return jax.shard_map(
        per_device, mesh=mesh, in_specs=in_specs, out_specs=out_specs, check_vma=False
    )
```

```python
import functools
import math

import jax
import jax.numpy as jnp
from jax import lax
from jax.experimental import pallas as pl
from jax.experimental.pallas import tpu as pltpu
from jax.sharding import PartitionSpec as P

ITERS = 4
TAPS = 9
NPAT = 8
LANES = 128
COSINES = [math.cos(2.0 * math.pi * m / 5.0) for m in range(5)]
MESH = pl.DeviceIdType.MESH


def lane_iota(shape):
    return lax.broadcasted_iota(jnp.int32, shape, len(shape) - 1)


def row_iota(shape):
    return lax.broadcasted_iota(jnp.int32, shape, len(shape) - 2)


def block_transpose(tiles):
    group = lane_iota(tiles[0].shape) // 16
    tiles = list(tiles)
    for bit in (4, 2, 1):
        keep = (group & bit) == 0
        for k in range(8):
            if k & bit:
                continue
            low, high = tiles[k], tiles[k + bit]
            axis = low.ndim - 1
            tiles[k] = jnp.where(keep, low, pltpu.roll(high, 16 * bit, axis))
            tiles[k + bit] = jnp.where(keep, pltpu.roll(low, LANES - 16 * bit, axis), high)
    return tiles


def kernel(
    full_rows,
    full_cols,
    cells,
    est_ref,
    data_ref,
    axial_ref,
    taps_ref,
    radius_ref,
    codes_ref,
    out_ref,
    rms_ref,
    squares_ref,
    sums_row,
    sums_ty,
    est_rows,
    data_rows,
    out_rows,
    load_sem,
    store_sem,
    grid_ref,
    final_ref,
    home_ref,
    data_in,
    data_mid,
    relay_out,
    relay_in,
    left_ref,
    right_ref,
    lit_ref,
    blur_ref,
    pred_ref,
    quot_ref,
    forward_ref,
    adjoint_ref,
    axial_fwd,
    axial_adj,
    wave_ext,
    wave_in,
    planes_ref,
    mask_ext,
    valid_ref,
    norm_ref,
    halo_send,
    halo_recv,
    relay_send,
    relay_recv,
    edge_send,
    left_recv,
    right_recv,
    pat_send,
    pat_recv,
    out_send,
    out_recv,
    sum_send,
    sum_recv,
):
    ty, tx, q = lax.axis_index("ty"), lax.axis_index("tx"), lax.axis_index("pat")
    nty, ntx, npat = lax.axis_size("ty"), lax.axis_size("tx"), lax.axis_size("pat")
    ncol = ntx * npat
    loads = [
        pltpu.make_async_copy(
            source.at[:, LANES * half : LANES * (half + 1)], target.at[half], load_sem.at[k, half]
        )
        for k, (source, target) in enumerate(((est_ref, est_rows), (data_ref, data_rows)))
        for half in range(2)
    ]
    for copy in loads:
        copy.start()

    def turned(tile, place):
        return jnp.where(lax.rem(tile, 2) == 0, place, npat - 1 - place)

    mine = turned(tx, q)
    column = tx * npat + mine

    def at(dty, dcol):
        c = lax.rem(column + dcol + ncol, ncol)
        tile = c // npat
        return {
            "ty": lax.rem(ty + dty + nty, nty),
            "tx": tile,
            "pat": turned(tile, lax.rem(c, npat)),
        }

    def shifted(dty, dtx, dq):
        return {
            "ty": lax.rem(ty + dty + nty, nty),
            "tx": lax.rem(tx + dtx + ntx, ntx),
            "pat": lax.rem(q + dq, npat),
        }

    def peer(d):
        return shifted(0, 0, d)

    barrier = pltpu.get_barrier_semaphore()
    greet = [(0, b, c) for b in range(ntx) for c in range(npat)]
    greet += [(a, b, c) for a in (-1, 1) for b in (-1, 0, 1) for c in range(npat)]
    greet += [(a, 0, 0) for a in range(2, nty - 1)]
    greet.remove((0, 0, 0))
    for move in greet:
        pl.semaphore_signal(
            barrier, inc=1, device_id=shifted(*move), device_id_type=MESH
        )

    for half in range(2):
        loads[half].wait()
    for strip in range(2):
        for half in range(2):
            rows = [est_rows[half, pl.ds(8 * strip + y, 32, stride=16)] for y in range(8)]
            for k, tile in enumerate(block_transpose(rows)):
                final_ref[2 * half + k // 4, k % 4, strip] = tile
    grid_ref[0, 1:5, 1:3] = final_ref[mine]

    moves = [
        ((slice(1, 5), 1), (slice(1, 5), 3), -1, 0),
        ((slice(1, 5), 2), (slice(1, 5), 0), 1, 0),
        ((1, 1), (5, 1), 0, -1),
        ((4, 1), (0, 1), 0, 1),
        ((1, 2), (5, 2), 0, -1),
        ((4, 2), (0, 2), 0, 1),
        ((1, 1), (5, 3), -1, -1),
        ((4, 1), (0, 3), -1, 1),
        ((1, 2), (5, 0), 1, -1),
        ((4, 2), (0, 0), 1, 1),
    ]
    from_strip = ((2, 3, 0, 6, 7), (4, 5, 1, 8, 9))
    side_halo = (2, 3, 4, 5)
    row_halo = {0: (1, 8, 9), 3: (0, 6, 7)}

    def halo_copies(t, which):
        copies = []
        for k in which:
            source, target, dty, dcol = moves[k]
            copies.append(
                pltpu.make_async_remote_copy(
                    src_ref=grid_ref.at[(t, *source)],
                    dst_ref=grid_ref.at[(t, *target)],
                    send_sem=halo_send.at[t, k],
                    recv_sem=halo_recv.at[t, k],
                    device_id=at(dty, dcol),
                    device_id_type=MESH,
                )
            )
        return copies

    kind_rows = (range(4, 12), (12, 13, 14, 15, 0, 1, 2, 3))

    def make_strip(kind):
        first = lane_iota((8, LANES)) < 4
        group = lane_iota((8, LANES)) // 16
        for block in range(8):
            at_rows = slice(8 * block, 8 * block + 8)

            def rows_of(half):
                return [
                    pltpu.roll(data_rows[half, pl.ds(128 * block + y, 8, stride=16)], 4, 1)
                    for y in kind_rows[kind]
                ]

            low, high = rows_of(0), rows_of(1)
            for k, tile in enumerate(block_transpose(low)):
                home_ref[k, kind, at_rows] = tile
            mixed = [jnp.where(first, a, b) for a, b in zip(low, high)]
            for k, tile in enumerate(block_transpose(mixed)):
                home_ref[8 + k, kind, at_rows] = tile
            last = high[0]
            for y in range(1, 8):
                last = jnp.where(group == y, pltpu.roll(high[y], 16 * y, 1), last)
            home_ref[16, kind, at_rows] = last

    def strip_copy(kind, d):
        to = turned(tx, lax.rem(q + d, npat))
        return pltpu.make_async_remote_copy(
            src_ref=home_ref.at[pl.ds(4 * to, 5), kind],
            dst_ref=data_in.at[q, :, kind],
            send_sem=pat_send.at[kind, d - 1],
            recv_sem=pat_recv.at[kind, d - 1],
            device_id=peer(d),
            device_id_type=MESH,
        )

    def edge_copies(kind):
        after, before = lax.rem(tx + 1, ntx), lax.rem(tx + ntx - 1, ntx)
        return [
            pltpu.make_async_remote_copy(
                src_ref=home_ref.at[16, kind],
                dst_ref=left_ref.at[q, kind],
                send_sem=edge_send.at[0, kind],
                recv_sem=left_recv.at[q, kind],
                device_id={"ty": ty, "tx": after, "pat": turned(after, 0)},
                device_id_type=MESH,
            ),
            pltpu.make_async_remote_copy(
                src_ref=home_ref.at[0, kind],
                dst_ref=right_ref.at[q, kind],
                send_sem=edge_send.at[1, kind],
                recv_sem=right_recv.at[q, kind],
                device_id={"ty": ty, "tx": before, "pat": turned(before, npat - 1)},
                device_id_type=MESH,
            ),
        ]

    hops = (1, 3, 2)
    for copy in loads[2:]:
        copy.wait()
    make_strip(1)
    pl.semaphore_wait(barrier, len(greet))
    for copy in halo_copies(0, side_halo) + [strip_copy(1, d) for d in hops] + edge_copies(1):
        copy.start()
    for copy in halo_copies(0, row_halo[0] + row_halo[3]):
        copy.start()
    make_strip(0)
    for copy in [strip_copy(0, d) for d in hops] + edge_copies(0):
        copy.start()
    data_in[q] = home_ref[pl.ds(4 * mine, 5)]

    def arrived(ref, sem):
        pltpu.make_async_copy(ref, ref, sem).wait()

    def receive(kind, d):
        source = lax.rem(q - d + npat, npat)
        if d:
            strip_copy(kind, d).wait_recv()
        keep = lane_iota((64, LANES)) % 16 < 4

        @pl.when(mine == 0)
        def _():
            arrived(left_ref.at[source, kind], left_recv.at[source, kind])
            data_in[source, 0, kind] = jnp.where(
                keep, left_ref[source, kind], data_in[source, 0, kind]
            )

        @pl.when(mine == npat - 1)
        def _():
            arrived(right_ref.at[source, kind], right_recv.at[source, kind])
            data_in[source, 4, kind] = jnp.where(
                keep, data_in[source, 4, kind], right_ref[source, kind]
            )

    lower = lane_iota((64, LANES)) < 64

    def relay_copies(d):
        source = lax.rem(q - d + npat, npat)
        return [
            pltpu.make_async_remote_copy(
                src_ref=relay_out.at[way, d],
                dst_ref=relay_in.at[way, source],
                send_sem=relay_send.at[way, d],
                recv_sem=relay_recv.at[way, d],
                device_id=at(1 - 2 * way, 0),
                device_id_type=MESH,
            )
            for way in range(2)
        ]

    def relay(d):
        source = lax.rem(q - d + npat, npat)
        receive(1, d)
        for k in range(2):
            a, b = data_in[source, 2 * k, 1], data_in[source, 2 * k + 1, 1]
            relay_out[0, d, k] = jnp.where(lower, a, pltpu.roll(b, 64, 1))
            relay_out[1, d, k] = jnp.where(lower, pltpu.roll(a, 64, 1), b)
        for way in range(2):
            relay_out[way, d, 2] = data_in[source, 4, 1]
        for copy in relay_copies(d):
            copy.start()

    def outer_strips(d):
        source = lax.rem(q - d + npat, npat)
        for copy in relay_copies(d):
            copy.wait_recv()
        for chunk in range(5):
            own = data_in[source, chunk, 1]
            above, below = relay_in[0, source, chunk // 2], relay_in[1, source, chunk // 2]
            if chunk % 2:
                above = pltpu.roll(above, 64, 1)
            elif chunk < 4:
                below = pltpu.roll(below, 64, 1)
            data_mid[source, chunk, 0] = jnp.where(lower, above, own)
            data_mid[source, chunk, 1] = jnp.where(lower, own, below)

    taps = [
        [jnp.where(abs(j - 4) <= radius_ref[i], taps_ref[i, j], 0.0) for j in range(TAPS)]
        for i in range(TAPS)
    ]
    narrow = (16, LANES)
    group = lane_iota(narrow) // 16
    for backward in (False, True):
        target = adjoint_ref if backward else forward_ref
        target[0:256, LANES:] = jnp.zeros((256, LANES), jnp.bfloat16)
        target[512:768, 0:LANES] = jnp.zeros((256, LANES), jnp.bfloat16)

        def tap(i, j):
            return taps[TAPS - 1 - i][TAPS - 1 - j] if backward else taps[i][j]

        for step in range(2):
            gap = 16 * step + row_iota(narrow) - lane_iota(narrow) % 16
            low = jnp.zeros(narrow, jnp.float32)
            high = jnp.zeros(narrow, jnp.float32)
            for j in range(TAPS):
                values = jnp.zeros(narrow, jnp.float32)
                for g in range(8):
                    values = jnp.where(group == g, tap(7 - g, j), values)
                high = jnp.where(gap == j, values, high)
                low = jnp.where((gap == j) & (group == 7), tap(8, j), low)
            for block in range(2):
                for y in range(8):
                    if block:
                        first = 7 - y
                        left, right = low, high
                    else:
                        first = 7 - y
                        left, right = high, None
                    turn = (LANES - 16 * first) % LANES
                    left = pltpu.roll(left, turn, 1) if turn else left
                    if right is None:
                        right = jnp.zeros(narrow, jnp.float32)
                    else:
                        right = pltpu.roll(right, turn, 1) if turn else right
                    values = jnp.where(group < 8 - first, left, right).astype(jnp.bfloat16)
                    for out_chunk in range(2):
                        start = 256 * (out_chunk + step) + LANES * block + 16 * y
                        target[start : start + 16, LANES * out_chunk : LANES * (out_chunk + 1)] = values

    spread = (row_iota((256, 32)) % 32 == lane_iota((256, 32))).astype(jnp.bfloat16)
    axial_b = axial_ref[...].astype(jnp.bfloat16)
    same = row_iota((256, 256)) // 32 == lane_iota((256, 256)) // 32
    nt = (((1,), (1,)), ((), ()))
    right_fwd = lax.dot_general(axial_b, spread, nt, preferred_element_type=jnp.float32)
    full = jnp.dot(spread, right_fwd.astype(jnp.bfloat16), preferred_element_type=jnp.float32)
    axial_fwd[...] = jnp.where(same, full, 0.0).astype(jnp.bfloat16)
    left_adj = lax.dot_general(spread, axial_b, nt, preferred_element_type=jnp.float32)
    full = lax.dot_general(left_adj.astype(jnp.bfloat16), spread, nt, preferred_element_type=jnp.float32)
    axial_adj[...] = jnp.where(same, full, 0.0).astype(jnp.bfloat16)

    relay(0)

    plane = row_iota((32, LANES)).astype(jnp.float32)
    planes_ref[...] = jnp.cos(plane * (2.0 * math.pi * 3.0 / 32.0))

    def positions(tile, strips, offset):
        spot = lane_iota(tile.shape)
        chunk, strip = tile // strips, tile % strips
        y = ty * 16 + 8 * strip - offset + spot // 16
        x = column * 64 + 16 * chunk - offset + spot % 16
        return y, x

    def waves(count, strips, offset):
        shape = (count * NPAT, LANES)
        index = row_iota(shape)
        y, x = positions(index // NPAT, strips, offset)
        pattern = index % NPAT
        angle = jnp.zeros(shape, jnp.int32)
        phase = jnp.zeros(shape, jnp.int32)
        for p in range(NPAT):
            angle = jnp.where(pattern == p, codes_ref[0, p], angle)
            phase = jnp.where(pattern == p, codes_ref[1, p], phase)
        cx = jnp.where(angle == 0, 2, -1)
        cy = jnp.where(angle == 0, 0, jnp.where(angle == 1, 2, -2))
        value = cx * x + cy * y + phase
        wide = value.astype(jnp.float32)
        m = wide - 5.0 * jnp.floor((wide + 0.5) * 0.2)
        wave = jnp.full(shape, COSINES[0], jnp.float32)
        for k in range(1, 5):
            wave = jnp.where(m == float(k), COSINES[k], wave)
        return 0.7 * wave

    wave_ext[...] = waves(20, 4, 8)
    wave_in[...] = waves(8, 2, 0)

    def inside(shape, strips, offset):
        y, x = positions(row_iota(shape), strips, offset)
        return (y >= 0) & (y < full_rows) & (x >= 0) & (x < full_cols)

    mask_ext[...] = inside((24, LANES), 4, 8).astype(jnp.float32)
    tile15 = (16, LANES)
    valid = inside(tile15, 3, 4) & ((row_iota(tile15) < 12) | (lane_iota(tile15) % 16 < 8))
    valid_ref[...] = valid.astype(jnp.float32)

    column_sum = lax.dot_general(
        axial_b, jnp.ones((32, LANES), jnp.bfloat16), (((0,), (0,)), ((), ())),
        preferred_element_type=jnp.float32,
    )
    cover_in = [
        jnp.broadcast_to(valid_ref[k : k + 1, :], (16, LANES)).astype(jnp.bfloat16)
        for k in range(15)
    ]
    plane_wave = planes_ref[...]
    for strip in range(2):
        for chunk in (0, 2):
            window = jnp.concatenate(
                [cover_in[3 * (chunk + k) + strip + a] for k in range(3) for a in range(2)], axis=1
            )
            cover = jnp.dot(window, adjoint_ref[...], preferred_element_type=jnp.float32)
            cover = cover.astype(jnp.bfloat16).astype(jnp.float32)
            for k in range(2):
                tile = 2 * (chunk + k) + strip
                row = cover[0:1, LANES * k : LANES * (k + 1)]
                light = jnp.zeros((32, LANES), jnp.float32)
                for p in range(NPAT):
                    light = light + (1.0 + wave_in[NPAT * tile + p : NPAT * tile + p + 1, :] * plane_wave)
                norm_ref[tile] = light * (row * column_sum)

    own = lane_iota((8, LANES))
    own_col, own_row = own % 16, own // 16

    def inner_mask(tile):
        chunk, strip = tile // 3, tile % 3
        x, y = 16 * chunk + own_col, 8 * strip + own_row
        return (x >= 4) & (x < 68) & (y >= 4) & (y < 20)

    blocks = ((1, 2), (0, 1), (3, 2))

    def predict(strip, chunk, width):
        count = min(width + 1, 5 - chunk)
        window = jnp.concatenate(
            [
                blur_ref[:, LANES * (4 * (chunk + k) + strip) : LANES * (4 * (chunk + k) + strip + 2)]
                for k in range(count)
            ],
            axis=1,
        )
        return jnp.dot(
            window,
            forward_ref[0 : 256 * count, 0 : LANES * width],
            preferred_element_type=jnp.float32,
        )

    def compare(strip, chunk, predicted, squares):
        for k in range(predicted.shape[1] // LANES):
            tile = 3 * (chunk + k) + strip
            ok = valid_ref[tile : tile + 1, :]
            filler = 1.0 - ok
            total = jnp.zeros((8, LANES), jnp.float32)
            for source in range(4):
                if strip == 1:
                    data = data_in[source, chunk + k, 0]
                else:
                    data = data_mid[source, chunk + k, strip // 2]
                guess = predicted[64 * source : 64 * (source + 1), LANES * k : LANES * (k + 1)]
                misfit = data - guess
                total = total + jnp.sum((misfit * misfit).reshape(8, 8, LANES), axis=0)
                quotient = (data * ok) / (guess + filler)
                quot_ref[64 * source : 64 * (source + 1), LANES * tile : LANES * (tile + 1)] = (
                    quotient.astype(jnp.bfloat16)
                )
            squares = squares + jnp.where(inner_mask(tile), total, 0.0)
        return squares

    stages = [
        (sums_row, ncol, tx * npat + q, lambda d: shifted(0, d // npat, d % npat)),
        (sums_ty, nty, ty, lambda d: shifted(d, 0, 0)),
    ]

    def sum_copies(stage):
        slots, count, me, device = stages[stage]
        return [
            pltpu.make_async_remote_copy(
                src_ref=slots.at[me],
                dst_ref=slots.at[me],
                send_sem=sum_send.at[stage, d - 1],
                recv_sem=sum_recv.at[stage, d - 1],
                device_id=device(d),
                device_id_type=MESH,
            )
            for d in range(1, count)
        ]

    def send_sums(stage, value):
        slots, _, me, _ = stages[stage]
        slots[me] = value
        for copy in sum_copies(stage):
            copy.start()

    def gather_sums(stage):
        for copy in sum_copies(stage):
            copy.wait()
        slots, count, _, _ = stages[stage]
        total = slots[0]
        for k in range(1, count):
            total = total + slots[k]
        return total

    def lit_tiles(t, strips, chunks=range(5)):
        wave_z = planes_ref[...]
        left_half = lane_iota((32, LANES)) % 16 < 8
        for chunk in chunks:
            for strip in strips:
                tile = 4 * chunk + strip
                a, b = grid_ref[t, chunk, strip], grid_ref[t, chunk + 1, strip]
                value = jnp.where(left_half, pltpu.roll(a, LANES - 8, 1), pltpu.roll(b, 8, 1))
                value = value * mask_ext[tile : tile + 1, :]
                for p in range(NPAT):
                    light = 1.0 + wave_ext[NPAT * tile + p : NPAT * tile + p + 1, :] * wave_z
                    lit_ref[32 * p : 32 * (p + 1), LANES * tile : LANES * (tile + 1)] = (
                        light * value
                    ).astype(jnp.bfloat16)
        tiles = [4 * chunk + strip for chunk in chunks for strip in strips]
        for k in range(0, len(tiles), 2):
            pair = [slice(LANES * tile, LANES * (tile + 1)) for tile in tiles[k : k + 2]]
            lit = jnp.concatenate([lit_ref[:, lanes] for lanes in pair], axis=1)
            blurred = jnp.dot(axial_fwd[...], lit, preferred_element_type=jnp.float32)
            for n, lanes in enumerate(pair):
                blur_ref[:, lanes] = blurred[:, LANES * n : LANES * (n + 1)].astype(jnp.bfloat16)

    def wait_halo(t, which):
        for copy in halo_copies(t, which):
            copy.wait_recv()

    def back_project(t, strip):
        wave_z = planes_ref[...]
        updated = []
        for chunk in (0, 2):
            tile = 3 * chunk + strip
            window = jnp.concatenate(
                [quot_ref[:, LANES * (tile + 3 * k) : LANES * (tile + 3 * k + 2)] for k in range(3)],
                axis=1,
            )
            spread_back = jnp.dot(
                window, adjoint_ref[...], preferred_element_type=jnp.float32
            ).astype(jnp.bfloat16)
            gathered = jnp.dot(axial_adj[...], spread_back, preferred_element_type=jnp.float32)
            for k in range(2):
                here = 2 * (chunk + k) + strip
                summed = jnp.zeros((32, LANES), jnp.float32)
                for p in range(NPAT):
                    light = 1.0 + wave_in[NPAT * here + p : NPAT * here + p + 1, :] * wave_z
                    summed = summed + light * gathered[
                        32 * p : 32 * (p + 1), LANES * k : LANES * (k + 1)
                    ]
                current = grid_ref[t, 1 + chunk + k, 1 + strip]
                updated.append((chunk + k, current * summed / norm_ref[here]))
        return updated

    def out_copies(strip):
        return [
            pltpu.make_async_remote_copy(
                src_ref=final_ref.at[mine, :, strip],
                dst_ref=final_ref.at[mine, :, strip],
                send_sem=out_send.at[strip, d - 1],
                recv_sem=out_recv.at[strip, d - 1],
                device_id=peer(d),
                device_id_type=MESH,
            )
            for d in range(1, npat)
        ]

    def compare_strip(t, strip, squares, some=blocks):
        for chunk, width in some:
            if t == 0:
                tile = 5 * strip + chunk
                predicted = pred_ref[:, LANES * tile : LANES * (tile + width)]
            else:
                predicted = predict(strip, chunk, width)
            squares = compare(strip, chunk, predicted, squares)
        return squares

    def finish_strip(t, strip):
        for chunk, value in back_project(t, strip):
            if t == ITERS - 1:
                final_ref[mine, chunk, strip] = value
            else:
                grid_ref[t + 1, 1 + chunk, 1 + strip] = value
        if t == ITERS - 1:
            copies = out_copies(strip)
        else:
            copies = halo_copies(t + 1, from_strip[strip])
        for copy in copies:
            copy.start()

    for t in range(ITERS):
        early = 1 - t % 2
        near, far = (2, 0) if early == 1 else (0, 2)
        near_halo, far_halo = (3, 0) if early == 1 else (0, 3)
        squares = jnp.zeros((8, LANES), jnp.float32)
        lit_tiles(t, (1, 2), (1, 2, 3))
        if t == 0:
            wait_halo(t, side_halo)
            lit_tiles(t, (1, 2), (0, 4))
            wait_halo(t, row_halo[0] + row_halo[3])
            lit_tiles(t, (0, 3))
            for strip in range(3):
                for chunk, width in blocks:
                    tile = 5 * strip + chunk
                    pred_ref[:, LANES * tile : LANES * (tile + width)] = predict(
                        strip, chunk, width
                    )
            for d in hops:
                relay(d)
            for d in (0, *hops):
                outer_strips(d)
            squares = compare_strip(t, near, squares)
            squares = compare_strip(t, far, squares)
            for d in (0, *hops):
                receive(0, d)
            squares = compare_strip(t, 1, squares)
            finish_strip(t, early)
        else:
            squares = compare_strip(t, 1, squares, blocks[:1])
            wait_halo(t, side_halo)
            lit_tiles(t, (1, 2), (0, 4))
            squares = compare_strip(t, 1, squares, blocks[1:])
            wait_halo(t, row_halo[near_halo])
            lit_tiles(t, (near_halo,))
            squares = compare_strip(t, near, squares)
            finish_strip(t, early)
            wait_halo(t, row_halo[far_halo])
            lit_tiles(t, (far_halo,))
            squares = compare_strip(t, far, squares)
        squares_ref[t] = squares
        if t == ITERS - 1:
            share = jnp.zeros((8, LANES), jnp.float32)
            for k in range(ITERS):
                total = jnp.sum(squares_ref[k], axis=0, keepdims=True)
                share = jnp.where(row_iota((8, LANES)) == k, total, share)
            send_sums(0, share)
        finish_strip(t, 1 - early)

    send_sums(1, gather_sums(0))
    for kind in range(2):
        for copy in [strip_copy(kind, d) for d in hops] + edge_copies(kind):
            copy.wait_send()
    for d in range(npat):
        for copy in relay_copies(d):
            copy.wait_send()
    for t in range(ITERS):
        for copy in halo_copies(t, range(len(moves))):
            copy.wait_send()
    for strip in (early, 1 - early):
        for copy in out_copies(strip):
            copy.wait()
        for half in range(2):
            tiles = [final_ref[2 * half + k // 4, k % 4, strip] for k in range(8)]
            for y, row in enumerate(block_transpose(tiles)):
                out_rows[half, pl.ds(8 * strip + y, 32, stride=16)] = row
    stores = [
        pltpu.make_async_copy(
            out_rows.at[half], out_ref.at[:, LANES * half : LANES * (half + 1)], store_sem.at[half]
        )
        for half in range(2)
    ]
    for copy in stores:
        copy.start()
    total = jnp.sum(gather_sums(1), axis=1, keepdims=True)
    rms_ref[...] = jnp.broadcast_to(jnp.sqrt(total / cells), (8, LANES))
    for copy in stores:
        copy.wait()


def per_device(estimate, data, axial, lateral_kernel, psf_radius, pattern_codes):
    planes, height, width = estimate.shape
    local = data.shape[0]
    full_rows = height * lax.axis_size("ty")
    full_cols = width * lax.axis_size("tx")
    est_rows = estimate.reshape(planes * height, width)
    data_rows = data.reshape(local * planes * height, width)
    vmem = pl.BlockSpec(memory_space=pltpu.VMEM)
    hbm = pl.BlockSpec(memory_space=pltpu.HBM)
    smem = pl.BlockSpec(memory_space=pltpu.SMEM)
    f32, bf16 = jnp.float32, jnp.bfloat16
    dma = pltpu.SemaphoreType.DMA
    cells = float(local * lax.axis_size("pat") * planes * full_rows * full_cols)
    rows, rms = pl.pallas_call(
        functools.partial(kernel, full_rows, full_cols, cells),
        name="deconvolve",
        out_shape=(
            jax.ShapeDtypeStruct((planes * height, width), f32),
            jax.ShapeDtypeStruct((8, LANES), f32),
        ),
        in_specs=[hbm, hbm, vmem, smem, smem, smem],
        out_specs=(hbm, vmem),
        scratch_shapes=[
            pltpu.VMEM((ITERS, 8, LANES), f32),
            pltpu.VMEM((lax.axis_size(("tx", "pat")), 8, LANES), f32),
            pltpu.VMEM((lax.axis_size("ty"), 8, LANES), f32),
            pltpu.VMEM((2, planes * height, LANES), f32),
            pltpu.VMEM((2, local * planes * height, LANES), f32),
            pltpu.VMEM((2, planes * height, LANES), f32),
            dma((2, 2)),
            dma((2,)),
            pltpu.VMEM((ITERS, 6, 4, 32, LANES), f32),
            pltpu.VMEM((4, 4, 2, 32, LANES), f32),
            pltpu.VMEM((17, 2, 64, LANES), f32),
            pltpu.VMEM((4, 5, 2, 64, LANES), f32),
            pltpu.VMEM((4, 5, 2, 64, LANES), f32),
            pltpu.VMEM((2, 4, 3, 64, LANES), f32),
            pltpu.VMEM((2, 4, 3, 64, LANES), f32),
            pltpu.VMEM((4, 2, 64, LANES), f32),
            pltpu.VMEM((4, 2, 64, LANES), f32),
            pltpu.VMEM((256, 20 * LANES), bf16),
            pltpu.VMEM((256, 20 * LANES), bf16),
            pltpu.VMEM((256, 15 * LANES), f32),
            pltpu.VMEM((256, 15 * LANES), bf16),
            pltpu.VMEM((768, 256), bf16),
            pltpu.VMEM((768, 256), bf16),
            pltpu.VMEM((256, 256), bf16),
            pltpu.VMEM((256, 256), bf16),
            pltpu.VMEM((20 * NPAT, LANES), f32),
            pltpu.VMEM((8 * NPAT, LANES), f32),
            pltpu.VMEM((32, LANES), f32),
            pltpu.VMEM((24, LANES), f32),
            pltpu.VMEM((16, LANES), f32),
            pltpu.VMEM((8, 32, LANES), f32),
            dma((ITERS, 10)),
            dma((ITERS, 10)),
            dma((2, 4)),
            dma((2, 4)),
            dma((2, 2)),
            dma((4, 2)),
            dma((4, 2)),
            dma((2, 3)),
            dma((2, 3)),
            dma((2, 3)),
            dma((2, 3)),
            dma((2, 15)),
            dma((2, 15)),
        ],
        compiler_params=pltpu.CompilerParams(
            collective_id=0, has_side_effects=True, vmem_limit_bytes=56 * 1024 * 1024
        ),
    )(est_rows, data_rows, axial, lateral_kernel, psf_radius, pattern_codes)
    return rows.reshape(planes, height, width), rms[:ITERS, 0]


def solution(mesh):
    in_specs = (P(None, "ty", "tx"), P("pat", None, "ty", "tx"), P(), P(), P(), P())
    out_specs = (P(None, "ty", "tx"), P())
    return jax.shard_map(
        per_device, mesh=mesh, in_specs=in_specs, out_specs=out_specs, check_vma=False
    )
```

```python
import functools
import math

import jax
import jax.numpy as jnp
from jax import lax
from jax.experimental import pallas as pl
from jax.experimental.pallas import tpu as pltpu
from jax.sharding import PartitionSpec as P

ITERS = 4
TAPS = 9
NPAT = 8
LANES = 128
COSINES = [math.cos(2.0 * math.pi * m / 5.0) for m in range(5)]
MESH = pl.DeviceIdType.MESH


def lane_iota(shape):
    return lax.broadcasted_iota(jnp.int32, shape, len(shape) - 1)


def row_iota(shape):
    return lax.broadcasted_iota(jnp.int32, shape, len(shape) - 2)


def block_transpose(tiles):
    group = lane_iota(tiles[0].shape) // 16
    tiles = list(tiles)
    for bit in (4, 2, 1):
        keep = (group & bit) == 0
        for k in range(8):
            if k & bit:
                continue
            low, high = tiles[k], tiles[k + bit]
            axis = low.ndim - 1
            tiles[k] = jnp.where(keep, low, pltpu.roll(high, 16 * bit, axis))
            tiles[k + bit] = jnp.where(keep, pltpu.roll(low, LANES - 16 * bit, axis), high)
    return tiles


def kernel(
    full_rows,
    full_cols,
    cells,
    est_ref,
    data_ref,
    axial_ref,
    taps_ref,
    radius_ref,
    codes_ref,
    out_ref,
    rms_ref,
    squares_ref,
    sums_row,
    sums_ty,
    est_rows,
    data_rows,
    out_rows,
    load_sem,
    store_sem,
    grid_ref,
    final_ref,
    home_ref,
    data_in,
    data_mid,
    relay_out,
    relay_in,
    left_ref,
    right_ref,
    lit_ref,
    blur_ref,
    pred_ref,
    quot_ref,
    forward_ref,
    adjoint_ref,
    axial_fwd,
    axial_adj,
    wave_ext,
    wave_in,
    planes_ref,
    mask_ext,
    valid_ref,
    norm_ref,
    halo_send,
    halo_recv,
    relay_send,
    relay_recv,
    edge_send,
    left_recv,
    right_recv,
    pat_send,
    pat_recv,
    out_send,
    out_recv,
    sum_send,
    sum_recv,
):
    ty, tx, q = lax.axis_index("ty"), lax.axis_index("tx"), lax.axis_index("pat")
    nty, ntx, npat = lax.axis_size("ty"), lax.axis_size("tx"), lax.axis_size("pat")
    ncol = ntx * npat
    loads = [
        pltpu.make_async_copy(
            source.at[:, LANES * half : LANES * (half + 1)], target.at[half], load_sem.at[k, half]
        )
        for k, (source, target) in enumerate(((est_ref, est_rows), (data_ref, data_rows)))
        for half in range(2)
    ]
    for copy in loads:
        copy.start()

    def turned(tile, place):
        return jnp.where(lax.rem(tile, 2) == 0, place, npat - 1 - place)

    mine = turned(tx, q)
    column = tx * npat + mine

    def at(dty, dcol):
        c = lax.rem(column + dcol + ncol, ncol)
        tile = c // npat
        return {
            "ty": lax.rem(ty + dty + nty, nty),
            "tx": tile,
            "pat": turned(tile, lax.rem(c, npat)),
        }

    def shifted(dty, dtx, dq):
        return {
            "ty": lax.rem(ty + dty + nty, nty),
            "tx": lax.rem(tx + dtx + ntx, ntx),
            "pat": lax.rem(q + dq, npat),
        }

    def peer(d):
        return shifted(0, 0, d)

    barrier = pltpu.get_barrier_semaphore()
    greet = [(0, b, c) for b in range(ntx) for c in range(npat)]
    greet += [(a, b, c) for a in (-1, 1) for b in (-1, 0, 1) for c in range(npat)]
    greet += [(a, 0, 0) for a in range(2, nty - 1)]
    greet.remove((0, 0, 0))
    for move in greet:
        pl.semaphore_signal(
            barrier, inc=1, device_id=shifted(*move), device_id_type=MESH
        )

    for half in range(2):
        loads[half].wait()
    for strip in range(2):
        for half in range(2):
            rows = [est_rows[half, pl.ds(8 * strip + y, 32, stride=16)] for y in range(8)]
            for k, tile in enumerate(block_transpose(rows)):
                final_ref[2 * half + k // 4, k % 4, strip] = tile
    grid_ref[0, 1:5, 1:3] = final_ref[mine]

    moves = [
        ((slice(1, 5), 1), (slice(1, 5), 3), -1, 0),
        ((slice(1, 5), 2), (slice(1, 5), 0), 1, 0),
        ((1, 1), (5, 1), 0, -1),
        ((4, 1), (0, 1), 0, 1),
        ((1, 2), (5, 2), 0, -1),
        ((4, 2), (0, 2), 0, 1),
        ((1, 1), (5, 3), -1, -1),
        ((4, 1), (0, 3), -1, 1),
        ((1, 2), (5, 0), 1, -1),
        ((4, 2), (0, 0), 1, 1),
    ]
    from_strip = ((2, 3, 0, 6, 7), (4, 5, 1, 8, 9))
    side_halo = (2, 3, 4, 5)
    row_halo = {0: (1, 8, 9), 3: (0, 6, 7)}

    def halo_copies(t, which):
        copies = []
        for k in which:
            source, target, dty, dcol = moves[k]
            copies.append(
                pltpu.make_async_remote_copy(
                    src_ref=grid_ref.at[(t, *source)],
                    dst_ref=grid_ref.at[(t, *target)],
                    send_sem=halo_send.at[t, k],
                    recv_sem=halo_recv.at[t, k],
                    device_id=at(dty, dcol),
                    device_id_type=MESH,
                )
            )
        return copies

    kind_rows = (range(4, 12), (12, 13, 14, 15, 0, 1, 2, 3))

    def make_strip(kind):
        first = lane_iota((8, LANES)) < 4
        group = lane_iota((8, LANES)) // 16
        for block in range(8):
            at_rows = slice(8 * block, 8 * block + 8)

            def rows_of(half):
                return [
                    pltpu.roll(data_rows[half, pl.ds(128 * block + y, 8, stride=16)], 4, 1)
                    for y in kind_rows[kind]
                ]

            low, high = rows_of(0), rows_of(1)
            for k, tile in enumerate(block_transpose(low)):
                home_ref[k, kind, at_rows] = tile
            mixed = [jnp.where(first, a, b) for a, b in zip(low, high)]
            for k, tile in enumerate(block_transpose(mixed)):
                home_ref[8 + k, kind, at_rows] = tile
            last = high[0]
            for y in range(1, 8):
                last = jnp.where(group == y, pltpu.roll(high[y], 16 * y, 1), last)
            home_ref[16, kind, at_rows] = last

    def strip_copy(kind, d):
        to = turned(tx, lax.rem(q + d, npat))
        return pltpu.make_async_remote_copy(
            src_ref=home_ref.at[pl.ds(4 * to, 5), kind],
            dst_ref=data_in.at[q, :, kind],
            send_sem=pat_send.at[kind, d - 1],
            recv_sem=pat_recv.at[kind, d - 1],
            device_id=peer(d),
            device_id_type=MESH,
        )

    def edge_copies(kind):
        after, before = lax.rem(tx + 1, ntx), lax.rem(tx + ntx - 1, ntx)
        return [
            pltpu.make_async_remote_copy(
                src_ref=home_ref.at[16, kind],
                dst_ref=left_ref.at[q, kind],
                send_sem=edge_send.at[0, kind],
                recv_sem=left_recv.at[q, kind],
                device_id={"ty": ty, "tx": after, "pat": turned(after, 0)},
                device_id_type=MESH,
            ),
            pltpu.make_async_remote_copy(
                src_ref=home_ref.at[0, kind],
                dst_ref=right_ref.at[q, kind],
                send_sem=edge_send.at[1, kind],
                recv_sem=right_recv.at[q, kind],
                device_id={"ty": ty, "tx": before, "pat": turned(before, npat - 1)},
                device_id_type=MESH,
            ),
        ]

    hops = (1, 3, 2)
    for copy in loads[2:]:
        copy.wait()
    make_strip(1)
    pl.semaphore_wait(barrier, len(greet))
    for copy in halo_copies(0, side_halo + row_halo[0] + row_halo[3]):
        copy.start()
    for copy in [strip_copy(1, d) for d in hops] + edge_copies(1):
        copy.start()
    make_strip(0)
    for copy in [strip_copy(0, d) for d in hops] + edge_copies(0):
        copy.start()
    data_in[q] = home_ref[pl.ds(4 * mine, 5)]

    def arrived(ref, sem):
        pltpu.make_async_copy(ref, ref, sem).wait()

    def receive(kind, d):
        source = lax.rem(q - d + npat, npat)
        if d:
            strip_copy(kind, d).wait_recv()
        keep = lane_iota((64, LANES)) % 16 < 4

        @pl.when(mine == 0)
        def _():
            arrived(left_ref.at[source, kind], left_recv.at[source, kind])
            data_in[source, 0, kind] = jnp.where(
                keep, left_ref[source, kind], data_in[source, 0, kind]
            )

        @pl.when(mine == npat - 1)
        def _():
            arrived(right_ref.at[source, kind], right_recv.at[source, kind])
            data_in[source, 4, kind] = jnp.where(
                keep, data_in[source, 4, kind], right_ref[source, kind]
            )

    lower = lane_iota((64, LANES)) < 64

    def relay_copies(d):
        source = lax.rem(q - d + npat, npat)
        return [
            pltpu.make_async_remote_copy(
                src_ref=relay_out.at[way, d],
                dst_ref=relay_in.at[way, source],
                send_sem=relay_send.at[way, d],
                recv_sem=relay_recv.at[way, d],
                device_id=at(1 - 2 * way, 0),
                device_id_type=MESH,
            )
            for way in range(2)
        ]

    def relay(d):
        source = lax.rem(q - d + npat, npat)
        receive(1, d)
        for k in range(2):
            a, b = data_in[source, 2 * k, 1], data_in[source, 2 * k + 1, 1]
            relay_out[0, d, k] = jnp.where(lower, a, pltpu.roll(b, 64, 1))
            relay_out[1, d, k] = jnp.where(lower, pltpu.roll(a, 64, 1), b)
        for way in range(2):
            relay_out[way, d, 2] = data_in[source, 4, 1]
        for copy in relay_copies(d):
            copy.start()

    def outer_strips(d):
        source = lax.rem(q - d + npat, npat)
        for copy in relay_copies(d):
            copy.wait_recv()
        for chunk in range(5):
            own = data_in[source, chunk, 1]
            above, below = relay_in[0, source, chunk // 2], relay_in[1, source, chunk // 2]
            if chunk % 2:
                above = pltpu.roll(above, 64, 1)
            elif chunk < 4:
                below = pltpu.roll(below, 64, 1)
            data_mid[source, chunk, 0] = jnp.where(lower, above, own)
            data_mid[source, chunk, 1] = jnp.where(lower, own, below)

    taps = [
        [jnp.where(abs(j - 4) <= radius_ref[i], taps_ref[i, j], 0.0) for j in range(TAPS)]
        for i in range(TAPS)
    ]
    narrow = (16, LANES)
    group = lane_iota(narrow) // 16
    for backward in (False, True):
        target = adjoint_ref if backward else forward_ref
        target[0:256, LANES:] = jnp.zeros((256, LANES), jnp.bfloat16)
        target[512:768, 0:LANES] = jnp.zeros((256, LANES), jnp.bfloat16)

        def tap(i, j):
            return taps[TAPS - 1 - i][TAPS - 1 - j] if backward else taps[i][j]

        for step in range(2):
            gap = 16 * step + row_iota(narrow) - lane_iota(narrow) % 16
            low = jnp.zeros(narrow, jnp.float32)
            high = jnp.zeros(narrow, jnp.float32)
            for j in range(TAPS):
                values = jnp.zeros(narrow, jnp.float32)
                for g in range(8):
                    values = jnp.where(group == g, tap(7 - g, j), values)
                high = jnp.where(gap == j, values, high)
                low = jnp.where((gap == j) & (group == 7), tap(8, j), low)
            for block in range(2):
                for y in range(8):
                    if block:
                        first = 7 - y
                        left, right = low, high
                    else:
                        first = 7 - y
                        left, right = high, None
                    turn = (LANES - 16 * first) % LANES
                    left = pltpu.roll(left, turn, 1) if turn else left
                    if right is None:
                        right = jnp.zeros(narrow, jnp.float32)
                    else:
                        right = pltpu.roll(right, turn, 1) if turn else right
                    values = jnp.where(group < 8 - first, left, right).astype(jnp.bfloat16)
                    for out_chunk in range(2):
                        start = 256 * (out_chunk + step) + LANES * block + 16 * y
                        target[start : start + 16, LANES * out_chunk : LANES * (out_chunk + 1)] = values

    spread = (row_iota((256, 32)) % 32 == lane_iota((256, 32))).astype(jnp.bfloat16)
    axial_b = axial_ref[...].astype(jnp.bfloat16)
    same = row_iota((256, 256)) // 32 == lane_iota((256, 256)) // 32
    nt = (((1,), (1,)), ((), ()))
    right_fwd = lax.dot_general(axial_b, spread, nt, preferred_element_type=jnp.float32)
    full = jnp.dot(spread, right_fwd.astype(jnp.bfloat16), preferred_element_type=jnp.float32)
    axial_fwd[...] = jnp.where(same, full, 0.0).astype(jnp.bfloat16)
    left_adj = lax.dot_general(spread, axial_b, nt, preferred_element_type=jnp.float32)
    full = lax.dot_general(left_adj.astype(jnp.bfloat16), spread, nt, preferred_element_type=jnp.float32)
    axial_adj[...] = jnp.where(same, full, 0.0).astype(jnp.bfloat16)

    relay(0)

    plane = row_iota((32, LANES)).astype(jnp.float32)
    planes_ref[...] = jnp.cos(plane * (2.0 * math.pi * 3.0 / 32.0))

    def positions(tile, strips, offset):
        spot = lane_iota(tile.shape)
        chunk, strip = tile // strips, tile % strips
        y = ty * 16 + 8 * strip - offset + spot // 16
        x = column * 64 + 16 * chunk - offset + spot % 16
        return y, x

    def waves(count, strips, offset):
        shape = (count * NPAT, LANES)
        index = row_iota(shape)
        y, x = positions(index // NPAT, strips, offset)
        pattern = index % NPAT
        angle = jnp.zeros(shape, jnp.int32)
        phase = jnp.zeros(shape, jnp.int32)
        for p in range(NPAT):
            angle = jnp.where(pattern == p, codes_ref[0, p], angle)
            phase = jnp.where(pattern == p, codes_ref[1, p], phase)
        cx = jnp.where(angle == 0, 2, -1)
        cy = jnp.where(angle == 0, 0, jnp.where(angle == 1, 2, -2))
        value = cx * x + cy * y + phase
        wide = value.astype(jnp.float32)
        m = wide - 5.0 * jnp.floor((wide + 0.5) * 0.2)
        wave = jnp.full(shape, COSINES[0], jnp.float32)
        for k in range(1, 5):
            wave = jnp.where(m == float(k), COSINES[k], wave)
        return 0.7 * wave

    wave_ext[...] = waves(20, 4, 8)
    wave_in[...] = waves(8, 2, 0)

    def inside(shape, strips, offset):
        y, x = positions(row_iota(shape), strips, offset)
        return (y >= 0) & (y < full_rows) & (x >= 0) & (x < full_cols)

    mask_ext[...] = inside((24, LANES), 4, 8).astype(jnp.float32)
    tile15 = (16, LANES)
    valid = inside(tile15, 3, 4) & ((row_iota(tile15) < 12) | (lane_iota(tile15) % 16 < 8))
    valid_ref[...] = valid.astype(jnp.float32)

    column_sum = lax.dot_general(
        axial_b, jnp.ones((32, LANES), jnp.bfloat16), (((0,), (0,)), ((), ())),
        preferred_element_type=jnp.float32,
    )
    cover_in = [
        jnp.broadcast_to(valid_ref[k : k + 1, :], (16, LANES)).astype(jnp.bfloat16)
        for k in range(15)
    ]
    plane_wave = planes_ref[...]
    for strip in range(2):
        for chunk in (0, 2):
            window = jnp.concatenate(
                [cover_in[3 * (chunk + k) + strip + a] for k in range(3) for a in range(2)], axis=1
            )
            cover = jnp.dot(window, adjoint_ref[...], preferred_element_type=jnp.float32)
            cover = cover.astype(jnp.bfloat16).astype(jnp.float32)
            for k in range(2):
                tile = 2 * (chunk + k) + strip
                row = cover[0:1, LANES * k : LANES * (k + 1)]
                light = jnp.zeros((32, LANES), jnp.float32)
                for p in range(NPAT):
                    light = light + (1.0 + wave_in[NPAT * tile + p : NPAT * tile + p + 1, :] * plane_wave)
                norm_ref[tile] = light * (row * column_sum)

    own = lane_iota((8, LANES))
    own_col, own_row = own % 16, own // 16

    def inner_mask(tile):
        chunk, strip = tile // 3, tile % 3
        x, y = 16 * chunk + own_col, 8 * strip + own_row
        return (x >= 4) & (x < 68) & (y >= 4) & (y < 20)

    blocks = ((1, 2), (0, 1), (3, 2))

    def predict(strip, chunk, width):
        count = min(width + 1, 5 - chunk)
        window = jnp.concatenate(
            [
                blur_ref[:, LANES * (4 * (chunk + k) + strip) : LANES * (4 * (chunk + k) + strip + 2)]
                for k in range(count)
            ],
            axis=1,
        )
        return jnp.dot(
            window,
            forward_ref[0 : 256 * count, 0 : LANES * width],
            preferred_element_type=jnp.float32,
        )

    def compare_rows(strip, tile_chunk, source, guess):
        tile = 3 * tile_chunk + strip
        ok = valid_ref[tile : tile + 1, :]
        if strip == 1:
            data = data_in[source, tile_chunk, 0]
        else:
            data = data_mid[source, tile_chunk, strip // 2]
        misfit = data - guess
        quotient = (data * ok) / (guess + (1.0 - ok))
        return jnp.sum((misfit * misfit).reshape(8, 8, LANES), axis=0), quotient.astype(jnp.bfloat16)

    def compare(strip, chunk, predicted, squares):
        for k in range(predicted.shape[1] // LANES):
            tile = 3 * (chunk + k) + strip
            total = jnp.zeros((8, LANES), jnp.float32)
            for source in range(4):
                rows = slice(64 * source, 64 * (source + 1))
                part, quotient = compare_rows(
                    strip, chunk + k, source, predicted[rows, LANES * k : LANES * (k + 1)]
                )
                quot_ref[rows, LANES * tile : LANES * (tile + 1)] = quotient
                total = total + part
            squares = squares + jnp.where(inner_mask(tile), total, 0.0)
        return squares

    def compare_source(source, squares):
        rows = pl.ds(pl.multiple_of(64 * source, 64), 64)
        for strip in range(3):
            for chunk in range(5):
                tile, place = 3 * chunk + strip, 5 * strip + chunk
                part, quotient = compare_rows(
                    strip, chunk, source, pred_ref[rows, LANES * place : LANES * (place + 1)]
                )
                quot_ref[rows, LANES * tile : LANES * (tile + 1)] = quotient
                squares = squares + jnp.where(inner_mask(tile), part, 0.0)
        return squares

    stages = [
        (sums_row, ncol, tx * npat + q, lambda d: shifted(0, d // npat, d % npat)),
        (sums_ty, nty, ty, lambda d: shifted(d, 0, 0)),
    ]

    def sum_copies(stage):
        slots, count, me, device = stages[stage]
        return [
            pltpu.make_async_remote_copy(
                src_ref=slots.at[me],
                dst_ref=slots.at[me],
                send_sem=sum_send.at[stage, d - 1],
                recv_sem=sum_recv.at[stage, d - 1],
                device_id=device(d),
                device_id_type=MESH,
            )
            for d in range(1, count)
        ]

    def send_sums(stage, value):
        slots, _, me, _ = stages[stage]
        slots[me] = value
        for copy in sum_copies(stage):
            copy.start()

    def gather_sums(stage):
        for copy in sum_copies(stage):
            copy.wait()
        slots, count, _, _ = stages[stage]
        total = slots[0]
        for k in range(1, count):
            total = total + slots[k]
        return total

    def lit_tiles(t, strips, chunks=range(5)):
        wave_z = planes_ref[...]
        left_half = lane_iota((32, LANES)) % 16 < 8

        def light(tile):
            chunk, strip = tile // 4, tile % 4
            a, b = grid_ref[t, chunk, strip], grid_ref[t, chunk + 1, strip]
            value = jnp.where(left_half, pltpu.roll(a, LANES - 8, 1), pltpu.roll(b, 8, 1))
            value = value * mask_ext[tile : tile + 1, :]
            for p in range(NPAT):
                wave = 1.0 + wave_ext[NPAT * tile + p : NPAT * tile + p + 1, :] * wave_z
                lit_ref[32 * p : 32 * (p + 1), LANES * tile : LANES * (tile + 1)] = (
                    wave * value
                ).astype(jnp.bfloat16)

        def blur(pair):
            pair = [slice(LANES * tile, LANES * (tile + 1)) for tile in pair]
            lit = jnp.concatenate([lit_ref[:, lanes] for lanes in pair], axis=1)
            blurred = jnp.dot(axial_fwd[...], lit, preferred_element_type=jnp.float32)
            for n, lanes in enumerate(pair):
                blur_ref[:, lanes] = blurred[:, LANES * n : LANES * (n + 1)].astype(jnp.bfloat16)

        tiles = [4 * chunk + strip for chunk in chunks for strip in strips]
        pairs = [tiles[k : k + 2] for k in range(0, len(tiles), 2)]
        for k, pair in enumerate(pairs):
            for tile in pair:
                light(tile)
            if k:
                blur(pairs[k - 1])
        blur(pairs[-1])

    def wait_halo(t, which):
        for copy in halo_copies(t, which):
            copy.wait_recv()

    def back_project(t, strip):
        wave_z = planes_ref[...]
        updated = []
        for chunk in (0, 2):
            tile = 3 * chunk + strip
            window = jnp.concatenate(
                [quot_ref[:, LANES * (tile + 3 * k) : LANES * (tile + 3 * k + 2)] for k in range(3)],
                axis=1,
            )
            spread_back = jnp.dot(
                window, adjoint_ref[...], preferred_element_type=jnp.float32
            ).astype(jnp.bfloat16)
            gathered = jnp.dot(axial_adj[...], spread_back, preferred_element_type=jnp.float32)
            for k in range(2):
                here = 2 * (chunk + k) + strip
                summed = jnp.zeros((32, LANES), jnp.float32)
                for p in range(NPAT):
                    light = 1.0 + wave_in[NPAT * here + p : NPAT * here + p + 1, :] * wave_z
                    summed = summed + light * gathered[
                        32 * p : 32 * (p + 1), LANES * k : LANES * (k + 1)
                    ]
                current = grid_ref[t, 1 + chunk + k, 1 + strip]
                updated.append((chunk + k, current * summed / norm_ref[here]))
        return updated

    def out_copies(strip):
        return [
            pltpu.make_async_remote_copy(
                src_ref=final_ref.at[mine, :, strip],
                dst_ref=final_ref.at[mine, :, strip],
                send_sem=out_send.at[strip, d - 1],
                recv_sem=out_recv.at[strip, d - 1],
                device_id=peer(d),
                device_id_type=MESH,
            )
            for d in range(1, npat)
        ]

    def compare_strip(strip, squares, some=blocks):
        waiting = None
        for chunk, width in some:
            predicted = predict(strip, chunk, width)
            if waiting is not None:
                squares = compare(strip, *waiting, squares)
            waiting = chunk, predicted
        return compare(strip, *waiting, squares)

    def finish_strip(t, strip):
        for chunk, value in back_project(t, strip):
            if t == ITERS - 1:
                final_ref[mine, chunk, strip] = value
            else:
                grid_ref[t + 1, 1 + chunk, 1 + strip] = value
        if t == ITERS - 1:
            copies = out_copies(strip)
        else:
            copies = halo_copies(t + 1, from_strip[strip])
        for copy in copies:
            copy.start()

    for t in range(ITERS):
        early = 1 - t % 2
        near, far = (2, 0) if early == 1 else (0, 2)
        near_halo, far_halo = (3, 0) if early == 1 else (0, 3)
        squares = jnp.zeros((8, LANES), jnp.float32)
        lit_tiles(t, (1, 2), (1, 2, 3))
        if t == 0:
            wait_halo(t, side_halo)
            lit_tiles(t, (1, 2), (0, 4))
            wait_halo(t, row_halo[0] + row_halo[3])
            lit_tiles(t, (0, 3))
            for strip in range(3):
                for chunk, width in blocks:
                    tile = 5 * strip + chunk
                    pred_ref[:, LANES * tile : LANES * (tile + width)] = predict(
                        strip, chunk, width
                    )
            for d in hops:
                relay(d)
            for d in (0, *hops):
                outer_strips(d)
                receive(0, d)
                squares = compare_source(lax.rem(q - d + npat, npat), squares)
            finish_strip(t, early)
        else:
            squares = compare_strip(1, squares, blocks[:1])
            wait_halo(t, row_halo[near_halo][:1])
            lit_tiles(t, (near_halo,), (1, 2, 3))
            squares = compare_strip(near, squares, blocks[:1])
            wait_halo(t, side_halo)
            lit_tiles(t, (1, 2), (0, 4))
            squares = compare_strip(1, squares, blocks[1:])
            wait_halo(t, row_halo[near_halo][1:])
            lit_tiles(t, (near_halo,), (0, 4))
            squares = compare_strip(near, squares, blocks[1:])
            finish_strip(t, early)
            wait_halo(t, row_halo[far_halo])
            lit_tiles(t, (far_halo,))
            squares = compare_strip(far, squares)
        squares_ref[t] = squares
        if t == ITERS - 1:
            share = jnp.zeros((8, LANES), jnp.float32)
            for k in range(ITERS):
                total = jnp.sum(squares_ref[k], axis=0, keepdims=True)
                share = jnp.where(row_iota((8, LANES)) == k, total, share)
            send_sums(0, share)
        finish_strip(t, 1 - early)

    send_sums(1, gather_sums(0))
    for kind in range(2):
        for copy in [strip_copy(kind, d) for d in hops] + edge_copies(kind):
            copy.wait_send()
    for d in range(npat):
        for copy in relay_copies(d):
            copy.wait_send()
    for t in range(ITERS):
        for copy in halo_copies(t, range(len(moves))):
            copy.wait_send()
    for strip in (early, 1 - early):
        for copy in out_copies(strip):
            copy.wait()
        for half in range(2):
            tiles = [final_ref[2 * half + k // 4, k % 4, strip] for k in range(8)]
            for y, row in enumerate(block_transpose(tiles)):
                out_rows[half, pl.ds(8 * strip + y, 32, stride=16)] = row
    stores = [
        pltpu.make_async_copy(
            out_rows.at[half], out_ref.at[:, LANES * half : LANES * (half + 1)], store_sem.at[half]
        )
        for half in range(2)
    ]
    for copy in stores:
        copy.start()
    total = jnp.sum(gather_sums(1), axis=1, keepdims=True)
    rms_ref[...] = jnp.broadcast_to(jnp.sqrt(total / cells), (8, LANES))
    for copy in stores:
        copy.wait()


def per_device(estimate, data, axial, lateral_kernel, psf_radius, pattern_codes):
    planes, height, width = estimate.shape
    local = data.shape[0]
    full_rows = height * lax.axis_size("ty")
    full_cols = width * lax.axis_size("tx")
    est_rows = estimate.reshape(planes * height, width)
    data_rows = data.reshape(local * planes * height, width)
    vmem = pl.BlockSpec(memory_space=pltpu.VMEM)
    hbm = pl.BlockSpec(memory_space=pltpu.HBM)
    smem = pl.BlockSpec(memory_space=pltpu.SMEM)
    f32, bf16 = jnp.float32, jnp.bfloat16
    dma = pltpu.SemaphoreType.DMA
    cells = float(local * lax.axis_size("pat") * planes * full_rows * full_cols)
    rows, rms = pl.pallas_call(
        functools.partial(kernel, full_rows, full_cols, cells),
        name="deconvolve",
        out_shape=(
            jax.ShapeDtypeStruct((planes * height, width), f32),
            jax.ShapeDtypeStruct((8, LANES), f32),
        ),
        in_specs=[hbm, hbm, vmem, smem, smem, smem],
        out_specs=(hbm, vmem),
        scratch_shapes=[
            pltpu.VMEM((ITERS, 8, LANES), f32),
            pltpu.VMEM((lax.axis_size(("tx", "pat")), 8, LANES), f32),
            pltpu.VMEM((lax.axis_size("ty"), 8, LANES), f32),
            pltpu.VMEM((2, planes * height, LANES), f32),
            pltpu.VMEM((2, local * planes * height, LANES), f32),
            pltpu.VMEM((2, planes * height, LANES), f32),
            dma((2, 2)),
            dma((2,)),
            pltpu.VMEM((ITERS, 6, 4, 32, LANES), f32),
            pltpu.VMEM((4, 4, 2, 32, LANES), f32),
            pltpu.VMEM((17, 2, 64, LANES), f32),
            pltpu.VMEM((4, 5, 2, 64, LANES), f32),
            pltpu.VMEM((4, 5, 2, 64, LANES), f32),
            pltpu.VMEM((2, 4, 3, 64, LANES), f32),
            pltpu.VMEM((2, 4, 3, 64, LANES), f32),
            pltpu.VMEM((4, 2, 64, LANES), f32),
            pltpu.VMEM((4, 2, 64, LANES), f32),
            pltpu.VMEM((256, 20 * LANES), bf16),
            pltpu.VMEM((256, 20 * LANES), bf16),
            pltpu.VMEM((256, 15 * LANES), f32),
            pltpu.VMEM((256, 15 * LANES), bf16),
            pltpu.VMEM((768, 256), bf16),
            pltpu.VMEM((768, 256), bf16),
            pltpu.VMEM((256, 256), bf16),
            pltpu.VMEM((256, 256), bf16),
            pltpu.VMEM((20 * NPAT, LANES), f32),
            pltpu.VMEM((8 * NPAT, LANES), f32),
            pltpu.VMEM((32, LANES), f32),
            pltpu.VMEM((24, LANES), f32),
            pltpu.VMEM((16, LANES), f32),
            pltpu.VMEM((8, 32, LANES), f32),
            dma((ITERS, 10)),
            dma((ITERS, 10)),
            dma((2, 4)),
            dma((2, 4)),
            dma((2, 2)),
            dma((4, 2)),
            dma((4, 2)),
            dma((2, 3)),
            dma((2, 3)),
            dma((2, 3)),
            dma((2, 3)),
            dma((2, 15)),
            dma((2, 15)),
        ],
        compiler_params=pltpu.CompilerParams(
            collective_id=0, has_side_effects=True, vmem_limit_bytes=56 * 1024 * 1024
        ),
    )(est_rows, data_rows, axial, lateral_kernel, psf_radius, pattern_codes)
    return rows.reshape(planes, height, width), rms[:ITERS, 0]


def solution(mesh):
    in_specs = (P(None, "ty", "tx"), P("pat", None, "ty", "tx"), P(), P(), P(), P())
    out_specs = (P(None, "ty", "tx"), P())
    return jax.shard_map(
        per_device, mesh=mesh, in_specs=in_specs, out_specs=out_specs, check_vma=False
    )
```

```python
import functools
import math

import jax
import jax.numpy as jnp
from jax import lax
from jax.experimental import pallas as pl
from jax.experimental.pallas import tpu as pltpu
from jax.sharding import PartitionSpec as P

ITERS = 4
TAPS = 9
NPAT = 8
LANES = 128
COSINES = [math.cos(2.0 * math.pi * m / 5.0) for m in range(5)]
MESH = pl.DeviceIdType.MESH


def lane_iota(shape):
    return lax.broadcasted_iota(jnp.int32, shape, len(shape) - 1)


def row_iota(shape):
    return lax.broadcasted_iota(jnp.int32, shape, len(shape) - 2)


def block_transpose(tiles):
    group = lane_iota(tiles[0].shape) // 16
    tiles = list(tiles)
    for bit in (4, 2, 1):
        keep = (group & bit) == 0
        for k in range(8):
            if k & bit:
                continue
            low, high = tiles[k], tiles[k + bit]
            axis = low.ndim - 1
            tiles[k] = jnp.where(keep, low, pltpu.roll(high, 16 * bit, axis))
            tiles[k + bit] = jnp.where(keep, pltpu.roll(low, LANES - 16 * bit, axis), high)
    return tiles


def kernel(
    full_rows,
    full_cols,
    cells,
    est_ref,
    data_ref,
    axial_ref,
    taps_ref,
    radius_ref,
    codes_ref,
    out_ref,
    rms_ref,
    squares_ref,
    sums_row,
    sums_ty,
    est_rows,
    data_rows,
    out_rows,
    load_sem,
    store_sem,
    grid_ref,
    final_ref,
    home_ref,
    data_in,
    data_mid,
    relay_out,
    relay_in,
    left_ref,
    right_ref,
    lit_ref,
    blur_ref,
    pred_ref,
    quot_ref,
    forward_ref,
    adjoint_ref,
    axial_fwd,
    axial_adj,
    wave_ext,
    wave_in,
    planes_ref,
    mask_ext,
    valid_ref,
    norm_ref,
    halo_send,
    halo_recv,
    relay_send,
    relay_recv,
    edge_send,
    left_recv,
    right_recv,
    pat_send,
    pat_recv,
    out_send,
    out_recv,
    sum_send,
    sum_recv,
):
    ty, tx, q = lax.axis_index("ty"), lax.axis_index("tx"), lax.axis_index("pat")
    nty, ntx, npat = lax.axis_size("ty"), lax.axis_size("tx"), lax.axis_size("pat")
    ncol = ntx * npat
    loads = [
        pltpu.make_async_copy(
            source.at[:, LANES * half : LANES * (half + 1)], target.at[half], load_sem.at[k, half]
        )
        for k, (source, target) in enumerate(((est_ref, est_rows), (data_ref, data_rows)))
        for half in range(2)
    ]
    for copy in loads:
        copy.start()

    def turned(tile, place):
        return jnp.where(lax.rem(tile, 2) == 0, place, npat - 1 - place)

    mine = turned(tx, q)
    column = tx * npat + mine

    def at(dty, dcol):
        c = lax.rem(column + dcol + ncol, ncol)
        tile = c // npat
        return {
            "ty": lax.rem(ty + dty + nty, nty),
            "tx": tile,
            "pat": turned(tile, lax.rem(c, npat)),
        }

    def shifted(dty, dtx, dq):
        return {
            "ty": lax.rem(ty + dty + nty, nty),
            "tx": lax.rem(tx + dtx + ntx, ntx),
            "pat": lax.rem(q + dq, npat),
        }

    def peer(d):
        return shifted(0, 0, d)

    barrier = pltpu.get_barrier_semaphore()
    greet = [(0, b, c) for b in range(ntx) for c in range(npat)]
    greet += [(a, b, c) for a in (-1, 1) for b in (-1, 0, 1) for c in range(npat)]
    greet += [(a, 0, 0) for a in range(2, nty - 1)]
    greet.remove((0, 0, 0))
    for move in greet:
        pl.semaphore_signal(
            barrier, inc=1, device_id=shifted(*move), device_id_type=MESH
        )

    for half in range(2):
        loads[half].wait()
    for strip in range(2):
        for half in range(2):
            rows = [est_rows[half, pl.ds(8 * strip + y, 32, stride=16)] for y in range(8)]
            for k, tile in enumerate(block_transpose(rows)):
                final_ref[2 * half + k // 4, k % 4, strip] = tile
    grid_ref[0, 1:5, 1:3] = final_ref[mine]

    moves = [
        ((slice(1, 3), 1), (slice(1, 3), 3), -1, 0),
        ((slice(3, 5), 1), (slice(3, 5), 3), -1, 0),
        ((slice(1, 3), 2), (slice(1, 3), 0), 1, 0),
        ((slice(3, 5), 2), (slice(3, 5), 0), 1, 0),
        ((1, 1), (5, 1), 0, -1),
        ((4, 1), (0, 1), 0, 1),
        ((1, 2), (5, 2), 0, -1),
        ((4, 2), (0, 2), 0, 1),
        ((1, 1), (5, 3), -1, -1),
        ((4, 1), (0, 3), -1, 1),
        ((1, 2), (5, 0), 1, -1),
        ((4, 2), (0, 0), 1, 1),
    ]
    from_strip = (((8, 4, 0), (9, 5, 1)), ((10, 6, 2), (11, 7, 3)))
    side_halo = (4, 5, 6, 7)
    row_halo = {0: (2, 3), 3: (0, 1)}
    corner_halo = {0: (10, 11), 3: (8, 9)}
    all_halo = (8, 9, 10, 11, 4, 5, 6, 7, 0, 1, 2, 3)

    def halo_copies(t, which):
        copies = []
        for k in which:
            source, target, dty, dcol = moves[k]
            copies.append(
                pltpu.make_async_remote_copy(
                    src_ref=grid_ref.at[(t, *source)],
                    dst_ref=grid_ref.at[(t, *target)],
                    send_sem=halo_send.at[t, k],
                    recv_sem=halo_recv.at[t, k],
                    device_id=at(dty, dcol),
                    device_id_type=MESH,
                )
            )
        return copies

    kind_rows = (range(4, 12), (12, 13, 14, 15, 0, 1, 2, 3))

    def make_strip(kind):
        first = lane_iota((8, LANES)) < 4
        group = lane_iota((8, LANES)) // 16
        for block in range(8):
            at_rows = slice(8 * block, 8 * block + 8)

            def rows_of(half):
                return [
                    pltpu.roll(data_rows[half, pl.ds(128 * block + y, 8, stride=16)], 4, 1)
                    for y in kind_rows[kind]
                ]

            low, high = rows_of(0), rows_of(1)
            for k, tile in enumerate(block_transpose(low)):
                home_ref[k, kind, at_rows] = tile
            mixed = [jnp.where(first, a, b) for a, b in zip(low, high)]
            for k, tile in enumerate(block_transpose(mixed)):
                home_ref[8 + k, kind, at_rows] = tile
            last = high[0]
            for y in range(1, 8):
                last = jnp.where(group == y, pltpu.roll(high[y], 16 * y, 1), last)
            home_ref[16, kind, at_rows] = last

    def strip_copy(kind, d):
        to = turned(tx, lax.rem(q + d, npat))
        return pltpu.make_async_remote_copy(
            src_ref=home_ref.at[pl.ds(4 * to, 5), kind],
            dst_ref=data_in.at[q, :, kind],
            send_sem=pat_send.at[kind, d - 1],
            recv_sem=pat_recv.at[kind, d - 1],
            device_id=peer(d),
            device_id_type=MESH,
        )

    def edge_copies(kind):
        after, before = lax.rem(tx + 1, ntx), lax.rem(tx + ntx - 1, ntx)
        return [
            pltpu.make_async_remote_copy(
                src_ref=home_ref.at[16, kind],
                dst_ref=left_ref.at[q, kind],
                send_sem=edge_send.at[0, kind],
                recv_sem=left_recv.at[q, kind],
                device_id={"ty": ty, "tx": after, "pat": turned(after, 0)},
                device_id_type=MESH,
            ),
            pltpu.make_async_remote_copy(
                src_ref=home_ref.at[0, kind],
                dst_ref=right_ref.at[q, kind],
                send_sem=edge_send.at[1, kind],
                recv_sem=right_recv.at[q, kind],
                device_id={"ty": ty, "tx": before, "pat": turned(before, npat - 1)},
                device_id_type=MESH,
            ),
        ]

    hops = (1, 3, 2)
    for copy in loads[2:]:
        copy.wait()
    make_strip(1)
    pl.semaphore_wait(barrier, len(greet))
    for copy in halo_copies(0, all_halo):
        copy.start()
    for copy in [strip_copy(1, d) for d in hops] + edge_copies(1):
        copy.start()
    make_strip(0)
    for copy in [strip_copy(0, d) for d in hops] + edge_copies(0):
        copy.start()
    data_in[q] = home_ref[pl.ds(4 * mine, 5)]

    def arrived(ref, sem):
        pltpu.make_async_copy(ref, ref, sem).wait()

    def receive(kind, d):
        source = lax.rem(q - d + npat, npat)
        if d:
            strip_copy(kind, d).wait_recv()
        keep = lane_iota((64, LANES)) % 16 < 4

        @pl.when(mine == 0)
        def _():
            arrived(left_ref.at[source, kind], left_recv.at[source, kind])
            data_in[source, 0, kind] = jnp.where(
                keep, left_ref[source, kind], data_in[source, 0, kind]
            )

        @pl.when(mine == npat - 1)
        def _():
            arrived(right_ref.at[source, kind], right_recv.at[source, kind])
            data_in[source, 4, kind] = jnp.where(
                keep, data_in[source, 4, kind], right_ref[source, kind]
            )

    lower = lane_iota((64, LANES)) < 64

    def relay_copies(d):
        source = lax.rem(q - d + npat, npat)
        return [
            pltpu.make_async_remote_copy(
                src_ref=relay_out.at[way, d],
                dst_ref=relay_in.at[way, source],
                send_sem=relay_send.at[way, d],
                recv_sem=relay_recv.at[way, d],
                device_id=at(1 - 2 * way, 0),
                device_id_type=MESH,
            )
            for way in range(2)
        ]

    def relay(d):
        source = lax.rem(q - d + npat, npat)
        receive(1, d)
        for k in range(2):
            a, b = data_in[source, 2 * k, 1], data_in[source, 2 * k + 1, 1]
            relay_out[0, d, k] = jnp.where(lower, a, pltpu.roll(b, 64, 1))
            relay_out[1, d, k] = jnp.where(lower, pltpu.roll(a, 64, 1), b)
        for way in range(2):
            relay_out[way, d, 2] = data_in[source, 4, 1]
        for copy in relay_copies(d):
            copy.start()

    def outer_strips(d):
        source = lax.rem(q - d + npat, npat)
        for copy in relay_copies(d):
            copy.wait_recv()
        for chunk in range(5):
            own = data_in[source, chunk, 1]
            above, below = relay_in[0, source, chunk // 2], relay_in[1, source, chunk // 2]
            if chunk % 2:
                above = pltpu.roll(above, 64, 1)
            elif chunk < 4:
                below = pltpu.roll(below, 64, 1)
            data_mid[source, chunk, 0] = jnp.where(lower, above, own)
            data_mid[source, chunk, 1] = jnp.where(lower, own, below)

    taps = [
        [jnp.where(abs(j - 4) <= radius_ref[i], taps_ref[i, j], 0.0) for j in range(TAPS)]
        for i in range(TAPS)
    ]
    narrow = (16, LANES)
    group = lane_iota(narrow) // 16
    for backward in (False, True):
        target = adjoint_ref if backward else forward_ref
        target[0:256, LANES:] = jnp.zeros((256, LANES), jnp.bfloat16)
        target[512:768, 0:LANES] = jnp.zeros((256, LANES), jnp.bfloat16)

        def tap(i, j):
            return taps[TAPS - 1 - i][TAPS - 1 - j] if backward else taps[i][j]

        for step in range(2):
            gap = 16 * step + row_iota(narrow) - lane_iota(narrow) % 16
            low = jnp.zeros(narrow, jnp.float32)
            high = jnp.zeros(narrow, jnp.float32)
            for j in range(TAPS):
                values = jnp.zeros(narrow, jnp.float32)
                for g in range(8):
                    values = jnp.where(group == g, tap(7 - g, j), values)
                high = jnp.where(gap == j, values, high)
                low = jnp.where((gap == j) & (group == 7), tap(8, j), low)
            for block in range(2):
                for y in range(8):
                    if block:
                        first = 7 - y
                        left, right = low, high
                    else:
                        first = 7 - y
                        left, right = high, None
                    turn = (LANES - 16 * first) % LANES
                    left = pltpu.roll(left, turn, 1) if turn else left
                    if right is None:
                        right = jnp.zeros(narrow, jnp.float32)
                    else:
                        right = pltpu.roll(right, turn, 1) if turn else right
                    values = jnp.where(group < 8 - first, left, right).astype(jnp.bfloat16)
                    for out_chunk in range(2):
                        start = 256 * (out_chunk + step) + LANES * block + 16 * y
                        target[start : start + 16, LANES * out_chunk : LANES * (out_chunk + 1)] = values

    spread = (row_iota((256, 32)) % 32 == lane_iota((256, 32))).astype(jnp.bfloat16)
    axial_b = axial_ref[...].astype(jnp.bfloat16)
    same = row_iota((256, 256)) // 32 == lane_iota((256, 256)) // 32
    nt = (((1,), (1,)), ((), ()))
    right_fwd = lax.dot_general(axial_b, spread, nt, preferred_element_type=jnp.float32)
    full = jnp.dot(spread, right_fwd.astype(jnp.bfloat16), preferred_element_type=jnp.float32)
    axial_fwd[...] = jnp.where(same, full, 0.0).astype(jnp.bfloat16)
    left_adj = lax.dot_general(spread, axial_b, nt, preferred_element_type=jnp.float32)
    full = lax.dot_general(left_adj.astype(jnp.bfloat16), spread, nt, preferred_element_type=jnp.float32)
    axial_adj[...] = jnp.where(same, full, 0.0).astype(jnp.bfloat16)

    relay(0)

    plane = row_iota((32, LANES)).astype(jnp.float32)
    planes_ref[...] = jnp.cos(plane * (2.0 * math.pi * 3.0 / 32.0))

    def positions(tile, strips, offset):
        spot = lane_iota(tile.shape)
        chunk, strip = tile // strips, tile % strips
        y = ty * 16 + 8 * strip - offset + spot // 16
        x = column * 64 + 16 * chunk - offset + spot % 16
        return y, x

    def waves(count, strips, offset):
        shape = (count * NPAT, LANES)
        index = row_iota(shape)
        y, x = positions(index // NPAT, strips, offset)
        pattern = index % NPAT
        angle = jnp.zeros(shape, jnp.int32)
        phase = jnp.zeros(shape, jnp.int32)
        for p in range(NPAT):
            angle = jnp.where(pattern == p, codes_ref[0, p], angle)
            phase = jnp.where(pattern == p, codes_ref[1, p], phase)
        cx = jnp.where(angle == 0, 2, -1)
        cy = jnp.where(angle == 0, 0, jnp.where(angle == 1, 2, -2))
        value = cx * x + cy * y + phase
        wide = value.astype(jnp.float32)
        m = wide - 5.0 * jnp.floor((wide + 0.5) * 0.2)
        wave = jnp.full(shape, COSINES[0], jnp.float32)
        for k in range(1, 5):
            wave = jnp.where(m == float(k), COSINES[k], wave)
        return 0.7 * wave

    wave_ext[...] = waves(20, 4, 8)
    wave_in[...] = waves(8, 2, 0)

    def inside(shape, strips, offset):
        y, x = positions(row_iota(shape), strips, offset)
        return (y >= 0) & (y < full_rows) & (x >= 0) & (x < full_cols)

    mask_ext[...] = inside((24, LANES), 4, 8).astype(jnp.float32)
    tile15 = (16, LANES)
    valid = inside(tile15, 3, 4) & ((row_iota(tile15) < 12) | (lane_iota(tile15) % 16 < 8))
    valid_ref[...] = valid.astype(jnp.float32)

    column_sum = lax.dot_general(
        axial_b, jnp.ones((32, LANES), jnp.bfloat16), (((0,), (0,)), ((), ())),
        preferred_element_type=jnp.float32,
    )
    cover_in = [
        jnp.broadcast_to(valid_ref[k : k + 1, :], (16, LANES)).astype(jnp.bfloat16)
        for k in range(15)
    ]
    plane_wave = planes_ref[...]
    for strip in range(2):
        for chunk in (0, 2):
            window = jnp.concatenate(
                [cover_in[3 * (chunk + k) + strip + a] for k in range(3) for a in range(2)], axis=1
            )
            cover = jnp.dot(window, adjoint_ref[...], preferred_element_type=jnp.float32)
            cover = cover.astype(jnp.bfloat16).astype(jnp.float32)
            for k in range(2):
                tile = 2 * (chunk + k) + strip
                row = cover[0:1, LANES * k : LANES * (k + 1)]
                light = jnp.zeros((32, LANES), jnp.float32)
                for p in range(NPAT):
                    light = light + (1.0 + wave_in[NPAT * tile + p : NPAT * tile + p + 1, :] * plane_wave)
                norm_ref[tile] = light * (row * column_sum)

    own = lane_iota((8, LANES))
    own_col, own_row = own % 16, own // 16

    def inner_mask(tile):
        chunk, strip = tile // 3, tile % 3
        x, y = 16 * chunk + own_col, 8 * strip + own_row
        return (x >= 4) & (x < 68) & (y >= 4) & (y < 20)

    blocks = ((1, 2), (0, 1), (3, 2))

    def predict(strip, chunk, width):
        count = min(width + 1, 5 - chunk)
        window = jnp.concatenate(
            [
                blur_ref[:, LANES * (4 * (chunk + k) + strip) : LANES * (4 * (chunk + k) + strip + 2)]
                for k in range(count)
            ],
            axis=1,
        )
        return jnp.dot(
            window,
            forward_ref[0 : 256 * count, 0 : LANES * width],
            preferred_element_type=jnp.float32,
        )

    def compare_rows(strip, tile_chunk, source, guess):
        tile = 3 * tile_chunk + strip
        ok = valid_ref[tile : tile + 1, :]
        if strip == 1:
            data = data_in[source, tile_chunk, 0]
        else:
            data = data_mid[source, tile_chunk, strip // 2]
        misfit = data - guess
        quotient = (data * ok) / (guess + (1.0 - ok))
        return jnp.sum((misfit * misfit).reshape(8, 8, LANES), axis=0), quotient.astype(jnp.bfloat16)

    def compare(strip, chunk, predicted, squares):
        for k in range(predicted.shape[1] // LANES):
            tile = 3 * (chunk + k) + strip
            total = jnp.zeros((8, LANES), jnp.float32)
            for source in range(4):
                rows = slice(64 * source, 64 * (source + 1))
                part, quotient = compare_rows(
                    strip, chunk + k, source, predicted[rows, LANES * k : LANES * (k + 1)]
                )
                quot_ref[rows, LANES * tile : LANES * (tile + 1)] = quotient
                total = total + part
            squares = squares + jnp.where(inner_mask(tile), total, 0.0)
        return squares

    def compare_source(source, squares):
        rows = pl.ds(pl.multiple_of(64 * source, 64), 64)
        for strip in range(3):
            for chunk in range(5):
                tile, place = 3 * chunk + strip, 5 * strip + chunk
                part, quotient = compare_rows(
                    strip, chunk, source, pred_ref[rows, LANES * place : LANES * (place + 1)]
                )
                quot_ref[rows, LANES * tile : LANES * (tile + 1)] = quotient
                squares = squares + jnp.where(inner_mask(tile), part, 0.0)
        return squares

    stages = [
        (sums_row, ncol, tx * npat + q, lambda d: shifted(0, d // npat, d % npat)),
        (sums_ty, nty, ty, lambda d: shifted(d, 0, 0)),
    ]

    def sum_copies(stage):
        slots, count, me, device = stages[stage]
        return [
            pltpu.make_async_remote_copy(
                src_ref=slots.at[me],
                dst_ref=slots.at[me],
                send_sem=sum_send.at[stage, d - 1],
                recv_sem=sum_recv.at[stage, d - 1],
                device_id=device(d),
                device_id_type=MESH,
            )
            for d in range(1, count)
        ]

    def send_sums(stage, value):
        slots, _, me, _ = stages[stage]
        slots[me] = value
        for copy in sum_copies(stage):
            copy.start()

    def gather_sums(stage):
        for copy in sum_copies(stage):
            copy.wait()
        slots, count, _, _ = stages[stage]
        total = slots[0]
        for k in range(1, count):
            total = total + slots[k]
        return total

    def lit_tiles(t, strips, chunks=range(5)):
        wave_z = planes_ref[...]
        left_half = lane_iota((32, LANES)) % 16 < 8

        def light(tile):
            chunk, strip = tile // 4, tile % 4
            a, b = grid_ref[t, chunk, strip], grid_ref[t, chunk + 1, strip]
            value = jnp.where(left_half, pltpu.roll(a, LANES - 8, 1), pltpu.roll(b, 8, 1))
            value = value * mask_ext[tile : tile + 1, :]
            for p in range(NPAT):
                wave = 1.0 + wave_ext[NPAT * tile + p : NPAT * tile + p + 1, :] * wave_z
                lit_ref[32 * p : 32 * (p + 1), LANES * tile : LANES * (tile + 1)] = (
                    wave * value
                ).astype(jnp.bfloat16)

        def blur(pair):
            pair = [slice(LANES * tile, LANES * (tile + 1)) for tile in pair]
            lit = jnp.concatenate([lit_ref[:, lanes] for lanes in pair], axis=1)
            blurred = jnp.dot(axial_fwd[...], lit, preferred_element_type=jnp.float32)
            for n, lanes in enumerate(pair):
                blur_ref[:, lanes] = blurred[:, LANES * n : LANES * (n + 1)].astype(jnp.bfloat16)

        tiles = [4 * chunk + strip for chunk in chunks for strip in strips]
        pairs = [tiles[k : k + 2] for k in range(0, len(tiles), 2)]
        for k, pair in enumerate(pairs):
            for tile in pair:
                light(tile)
            if k:
                blur(pairs[k - 1])
        blur(pairs[-1])

    def wait_halo(t, which):
        for copy in halo_copies(t, which):
            copy.wait_recv()

    def back_project(t, strip, chunk):
        wave_z = planes_ref[...]
        updated = []
        tile = 3 * chunk + strip
        window = jnp.concatenate(
            [quot_ref[:, LANES * (tile + 3 * k) : LANES * (tile + 3 * k + 2)] for k in range(3)],
            axis=1,
        )
        spread_back = jnp.dot(
            window, adjoint_ref[...], preferred_element_type=jnp.float32
        ).astype(jnp.bfloat16)
        gathered = jnp.dot(axial_adj[...], spread_back, preferred_element_type=jnp.float32)
        for k in range(2):
            here = 2 * (chunk + k) + strip
            summed = jnp.zeros((32, LANES), jnp.float32)
            for p in range(NPAT):
                light = 1.0 + wave_in[NPAT * here + p : NPAT * here + p + 1, :] * wave_z
                summed = summed + light * gathered[
                    32 * p : 32 * (p + 1), LANES * k : LANES * (k + 1)
                ]
            current = grid_ref[t, 1 + chunk + k, 1 + strip]
            updated.append((chunk + k, current * summed / norm_ref[here]))
        return updated

    def out_copies(strip):
        return [
            pltpu.make_async_remote_copy(
                src_ref=final_ref.at[mine, :, strip],
                dst_ref=final_ref.at[mine, :, strip],
                send_sem=out_send.at[strip, d - 1],
                recv_sem=out_recv.at[strip, d - 1],
                device_id=peer(d),
                device_id_type=MESH,
            )
            for d in range(1, npat)
        ]

    def compare_strip(strip, squares, some=blocks):
        waiting = None
        for chunk, width in some:
            predicted = predict(strip, chunk, width)
            if waiting is not None:
                squares = compare(strip, *waiting, squares)
            waiting = chunk, predicted
        return compare(strip, *waiting, squares)

    def finish_strip(t, strip):
        last = t == ITERS - 1
        for block in range(2):
            for chunk, value in back_project(t, strip, 2 * block):
                if last:
                    final_ref[mine, chunk, strip] = value
                else:
                    grid_ref[t + 1, 1 + chunk, 1 + strip] = value
            if not last:
                for copy in halo_copies(t + 1, from_strip[strip][block]):
                    copy.start()
        if last:
            for copy in out_copies(strip):
                copy.start()

    def share_squares():
        share = jnp.zeros((8, LANES), jnp.float32)
        for k in range(ITERS):
            total = jnp.sum(squares_ref[k], axis=0, keepdims=True)
            share = jnp.where(row_iota((8, LANES)) == k, total, share)
        send_sums(0, share)

    for t in range(ITERS):
        early = 1 - t % 2
        near, far = (2, 0) if early == 1 else (0, 2)
        near_halo, far_halo = (3, 0) if early == 1 else (0, 3)
        squares = jnp.zeros((8, LANES), jnp.float32)
        lit_tiles(t, (1, 2), (1, 2, 3))
        if t == 0:
            wait_halo(t, side_halo)
            lit_tiles(t, (1, 2), (0, 4))
            wait_halo(t, all_halo[:4] + all_halo[8:])
            lit_tiles(t, (0, 3))
            for strip in range(3):
                for chunk, width in blocks:
                    tile = 5 * strip + chunk
                    pred_ref[:, LANES * tile : LANES * (tile + width)] = predict(
                        strip, chunk, width
                    )
            for d in hops:
                relay(d)
            for d in (0, *hops):
                outer_strips(d)
                receive(0, d)
                squares = compare_source(lax.rem(q - d + npat, npat), squares)
        else:
            squares = compare_strip(1, squares, blocks[:1])
            wait_halo(t, row_halo[near_halo])
            lit_tiles(t, (near_halo,), (1, 2, 3))
            squares = compare_strip(near, squares, blocks[:1])
            wait_halo(t, side_halo)
            lit_tiles(t, (1, 2), (0, 4))
            squares = compare_strip(1, squares, blocks[1:])
            wait_halo(t, corner_halo[near_halo])
            lit_tiles(t, (near_halo,), (0, 4))
            squares = compare_strip(near, squares, blocks[1:])
            if t < ITERS - 1:
                finish_strip(t, early)
            wait_halo(t, row_halo[far_halo])
            lit_tiles(t, (far_halo,), (1, 2, 3))
            squares = compare_strip(far, squares, blocks[:1])
            wait_halo(t, corner_halo[far_halo])
            lit_tiles(t, (far_halo,), (0, 4))
            squares = compare_strip(far, squares, blocks[1:])
        squares_ref[t] = squares
        if t == ITERS - 1:
            share_squares()
        if t == 0 or t == ITERS - 1:
            finish_strip(t, early)
        finish_strip(t, 1 - early)

    send_sums(1, gather_sums(0))
    for kind in range(2):
        for copy in [strip_copy(kind, d) for d in hops] + edge_copies(kind):
            copy.wait_send()
    for d in range(npat):
        for copy in relay_copies(d):
            copy.wait_send()
    for t in range(ITERS):
        for copy in halo_copies(t, all_halo):
            copy.wait_send()
    for strip in (early, 1 - early):
        for copy in out_copies(strip):
            copy.wait()
        for half in range(2):
            tiles = [final_ref[2 * half + k // 4, k % 4, strip] for k in range(8)]
            for y, row in enumerate(block_transpose(tiles)):
                out_rows[half, pl.ds(8 * strip + y, 32, stride=16)] = row
    stores = [
        pltpu.make_async_copy(
            out_rows.at[half], out_ref.at[:, LANES * half : LANES * (half + 1)], store_sem.at[half]
        )
        for half in range(2)
    ]
    for copy in stores:
        copy.start()
    total = jnp.sum(gather_sums(1), axis=1, keepdims=True)
    rms = jnp.sqrt(total / cells)
    for k in range(ITERS):
        rms_ref[k] = rms[k, 0]
    for copy in stores:
        copy.wait()


def per_device(estimate, data, axial, lateral_kernel, psf_radius, pattern_codes):
    planes, height, width = estimate.shape
    local = data.shape[0]
    full_rows = height * lax.axis_size("ty")
    full_cols = width * lax.axis_size("tx")
    est_rows = estimate.reshape(planes * height, width)
    data_rows = data.reshape(local * planes * height, width)
    vmem = pl.BlockSpec(memory_space=pltpu.VMEM)
    hbm = pl.BlockSpec(memory_space=pltpu.HBM)
    smem = pl.BlockSpec(memory_space=pltpu.SMEM)
    f32, bf16 = jnp.float32, jnp.bfloat16
    dma = pltpu.SemaphoreType.DMA
    cells = float(local * lax.axis_size("pat") * planes * full_rows * full_cols)
    rows, rms = pl.pallas_call(
        functools.partial(kernel, full_rows, full_cols, cells),
        name="deconvolve",
        out_shape=(
            jax.ShapeDtypeStruct((planes * height, width), f32),
            jax.ShapeDtypeStruct((ITERS,), f32),
        ),
        in_specs=[hbm, hbm, vmem, smem, smem, smem],
        out_specs=(hbm, smem),
        scratch_shapes=[
            pltpu.VMEM((ITERS, 8, LANES), f32),
            pltpu.VMEM((lax.axis_size(("tx", "pat")), 8, LANES), f32),
            pltpu.VMEM((lax.axis_size("ty"), 8, LANES), f32),
            pltpu.VMEM((2, planes * height, LANES), f32),
            pltpu.VMEM((2, local * planes * height, LANES), f32),
            pltpu.VMEM((2, planes * height, LANES), f32),
            dma((2, 2)),
            dma((2,)),
            pltpu.VMEM((ITERS, 6, 4, 32, LANES), f32),
            pltpu.VMEM((4, 4, 2, 32, LANES), f32),
            pltpu.VMEM((17, 2, 64, LANES), f32),
            pltpu.VMEM((4, 5, 2, 64, LANES), f32),
            pltpu.VMEM((4, 5, 2, 64, LANES), f32),
            pltpu.VMEM((2, 4, 3, 64, LANES), f32),
            pltpu.VMEM((2, 4, 3, 64, LANES), f32),
            pltpu.VMEM((4, 2, 64, LANES), f32),
            pltpu.VMEM((4, 2, 64, LANES), f32),
            pltpu.VMEM((256, 20 * LANES), bf16),
            pltpu.VMEM((256, 20 * LANES), bf16),
            pltpu.VMEM((256, 15 * LANES), f32),
            pltpu.VMEM((256, 15 * LANES), bf16),
            pltpu.VMEM((768, 256), bf16),
            pltpu.VMEM((768, 256), bf16),
            pltpu.VMEM((256, 256), bf16),
            pltpu.VMEM((256, 256), bf16),
            pltpu.VMEM((20 * NPAT, LANES), f32),
            pltpu.VMEM((8 * NPAT, LANES), f32),
            pltpu.VMEM((32, LANES), f32),
            pltpu.VMEM((24, LANES), f32),
            pltpu.VMEM((16, LANES), f32),
            pltpu.VMEM((8, 32, LANES), f32),
            dma((ITERS, 12)),
            dma((ITERS, 12)),
            dma((2, 4)),
            dma((2, 4)),
            dma((2, 2)),
            dma((4, 2)),
            dma((4, 2)),
            dma((2, 3)),
            dma((2, 3)),
            dma((2, 3)),
            dma((2, 3)),
            dma((2, 15)),
            dma((2, 15)),
        ],
        compiler_params=pltpu.CompilerParams(
            collective_id=0, has_side_effects=True, vmem_limit_bytes=56 * 1024 * 1024
        ),
    )(est_rows, data_rows, axial, lateral_kernel, psf_radius, pattern_codes)
    return rows.reshape(planes, height, width), rms


def solution(mesh):
    in_specs = (P(None, "ty", "tx"), P("pat", None, "ty", "tx"), P(), P(), P(), P())
    out_specs = (P(None, "ty", "tx"), P())
    return jax.shard_map(
        per_device, mesh=mesh, in_specs=in_specs, out_specs=out_specs, check_vma=False
    )
```

```python
import functools
import math

import jax
import jax.numpy as jnp
from jax import lax
from jax.experimental import pallas as pl
from jax.experimental.pallas import tpu as pltpu
from jax.sharding import PartitionSpec as P

ITERS = 4
TAPS = 9
NPAT = 8
LANES = 128
COSINES = [math.cos(2.0 * math.pi * m / 5.0) for m in range(5)]
MESH = pl.DeviceIdType.MESH


def lane_iota(shape):
    return lax.broadcasted_iota(jnp.int32, shape, len(shape) - 1)


def row_iota(shape):
    return lax.broadcasted_iota(jnp.int32, shape, len(shape) - 2)


def block_transpose(tiles):
    group = lane_iota(tiles[0].shape) // 16
    tiles = list(tiles)
    for bit in (4, 2, 1):
        keep = (group & bit) == 0
        for k in range(8):
            if k & bit:
                continue
            low, high = tiles[k], tiles[k + bit]
            axis = low.ndim - 1
            tiles[k] = jnp.where(keep, low, pltpu.roll(high, 16 * bit, axis))
            tiles[k + bit] = jnp.where(keep, pltpu.roll(low, LANES - 16 * bit, axis), high)
    return tiles


def kernel(
    full_rows,
    full_cols,
    cells,
    est_ref,
    data_ref,
    axial_ref,
    taps_ref,
    radius_ref,
    codes_ref,
    out_ref,
    rms_ref,
    squares_ref,
    sums_row,
    sums_ty,
    est_rows,
    data_rows,
    out_rows,
    load_sem,
    store_sem,
    grid_ref,
    final_ref,
    home_ref,
    data_in,
    data_mid,
    relay_out,
    relay_in,
    left_ref,
    right_ref,
    lit_ref,
    blur_ref,
    pred_ref,
    quot_ref,
    forward_ref,
    adjoint_ref,
    axial_fwd,
    axial_adj,
    wave_ext,
    wave_in,
    planes_ref,
    mask_ext,
    valid_ref,
    norm_ref,
    halo_send,
    halo_recv,
    relay_send,
    relay_recv,
    edge_send,
    left_recv,
    right_recv,
    pat_send,
    pat_recv,
    out_send,
    out_recv,
    sum_send,
    sum_recv,
):
    ty, tx, q = lax.axis_index("ty"), lax.axis_index("tx"), lax.axis_index("pat")
    nty, ntx, npat = lax.axis_size("ty"), lax.axis_size("tx"), lax.axis_size("pat")
    ncol = ntx * npat
    loads = [
        pltpu.make_async_copy(
            source.at[:, LANES * half : LANES * (half + 1)], target.at[half], load_sem.at[k, half]
        )
        for k, (source, target) in enumerate(((est_ref, est_rows), (data_ref, data_rows)))
        for half in range(2)
    ]
    for copy in loads:
        copy.start()

    def turned(tile, place):
        return jnp.where(lax.rem(tile, 2) == 0, place, npat - 1 - place)

    mine = turned(tx, q)
    column = tx * npat + mine

    def at(dty, dcol):
        c = lax.rem(column + dcol + ncol, ncol)
        tile = c // npat
        return {
            "ty": lax.rem(ty + dty + nty, nty),
            "tx": tile,
            "pat": turned(tile, lax.rem(c, npat)),
        }

    def shifted(dty, dtx, dq):
        return {
            "ty": lax.rem(ty + dty + nty, nty),
            "tx": lax.rem(tx + dtx + ntx, ntx),
            "pat": lax.rem(q + dq, npat),
        }

    def peer(d):
        return shifted(0, 0, d)

    barrier = pltpu.get_barrier_semaphore()
    greet = [(0, b, c) for b in range(ntx) for c in range(npat)]
    greet += [(a, b, c) for a in (-1, 1) for b in (-1, 0, 1) for c in range(npat)]
    greet += [(a, 0, 0) for a in range(2, nty - 1)]
    greet.remove((0, 0, 0))
    for move in greet:
        pl.semaphore_signal(
            barrier, inc=1, device_id=shifted(*move), device_id_type=MESH
        )

    for half in range(2):
        loads[half].wait()
    for strip in range(2):
        for half in range(2):
            rows = [est_rows[half, pl.ds(8 * strip + y, 32, stride=16)] for y in range(8)]
            for k, tile in enumerate(block_transpose(rows)):
                final_ref[2 * half + k // 4, k % 4, strip] = tile
    grid_ref[0, 1:5, 1:3] = final_ref[mine]

    moves = [
        ((slice(1, 3), 1), (slice(1, 3), 3), -1, 0),
        ((slice(3, 5), 1), (slice(3, 5), 3), -1, 0),
        ((slice(1, 3), 2), (slice(1, 3), 0), 1, 0),
        ((slice(3, 5), 2), (slice(3, 5), 0), 1, 0),
        ((1, 1), (5, 1), 0, -1),
        ((4, 1), (0, 1), 0, 1),
        ((1, 2), (5, 2), 0, -1),
        ((4, 2), (0, 2), 0, 1),
        ((1, 1), (5, 3), -1, -1),
        ((4, 1), (0, 3), -1, 1),
        ((1, 2), (5, 0), 1, -1),
        ((4, 2), (0, 0), 1, 1),
    ]
    from_strip = (((8, 4, 0), (9, 5, 1)), ((10, 6, 2), (11, 7, 3)))
    side_halo = (4, 5, 6, 7)
    row_halo = {0: (2, 3), 3: (0, 1)}
    corner_halo = {0: (10, 11), 3: (8, 9)}
    all_halo = (8, 9, 10, 11, 4, 5, 6, 7, 0, 1, 2, 3)

    def halo_copies(t, which):
        copies = []
        for k in which:
            source, target, dty, dcol = moves[k]
            copies.append(
                pltpu.make_async_remote_copy(
                    src_ref=grid_ref.at[(t, *source)],
                    dst_ref=grid_ref.at[(t, *target)],
                    send_sem=halo_send.at[t, k],
                    recv_sem=halo_recv.at[t, k],
                    device_id=at(dty, dcol),
                    device_id_type=MESH,
                )
            )
        return copies

    kind_rows = (range(4, 12), (12, 13, 14, 15, 0, 1, 2, 3))

    def make_strip(kind):
        first = lane_iota((8, LANES)) < 4
        group = lane_iota((8, LANES)) // 16
        for block in range(8):
            at_rows = slice(8 * block, 8 * block + 8)

            def rows_of(half):
                return [
                    pltpu.roll(data_rows[half, pl.ds(128 * block + y, 8, stride=16)], 4, 1)
                    for y in kind_rows[kind]
                ]

            low, high = rows_of(0), rows_of(1)
            for k, tile in enumerate(block_transpose(low)):
                home_ref[k, kind, at_rows] = tile
            mixed = [jnp.where(first, a, b) for a, b in zip(low, high)]
            for k, tile in enumerate(block_transpose(mixed)):
                home_ref[8 + k, kind, at_rows] = tile
            last = high[0]
            for y in range(1, 8):
                last = jnp.where(group == y, pltpu.roll(high[y], 16 * y, 1), last)
            home_ref[16, kind, at_rows] = last

    def strip_copy(kind, d):
        to = turned(tx, lax.rem(q + d, npat))
        return pltpu.make_async_remote_copy(
            src_ref=home_ref.at[pl.ds(4 * to, 5), kind],
            dst_ref=data_in.at[q, :, kind],
            send_sem=pat_send.at[kind, d - 1],
            recv_sem=pat_recv.at[kind, d - 1],
            device_id=peer(d),
            device_id_type=MESH,
        )

    def edge_copies(kind):
        after, before = lax.rem(tx + 1, ntx), lax.rem(tx + ntx - 1, ntx)
        return [
            pltpu.make_async_remote_copy(
                src_ref=home_ref.at[16, kind],
                dst_ref=left_ref.at[q, kind],
                send_sem=edge_send.at[0, kind],
                recv_sem=left_recv.at[q, kind],
                device_id={"ty": ty, "tx": after, "pat": turned(after, 0)},
                device_id_type=MESH,
            ),
            pltpu.make_async_remote_copy(
                src_ref=home_ref.at[0, kind],
                dst_ref=right_ref.at[q, kind],
                send_sem=edge_send.at[1, kind],
                recv_sem=right_recv.at[q, kind],
                device_id={"ty": ty, "tx": before, "pat": turned(before, npat - 1)},
                device_id_type=MESH,
            ),
        ]

    hops = (1, 3, 2)
    for copy in loads[2:]:
        copy.wait()
    make_strip(1)
    pl.semaphore_wait(barrier, len(greet))
    for copy in halo_copies(0, all_halo):
        copy.start()
    for copy in [strip_copy(1, d) for d in hops] + edge_copies(1):
        copy.start()
    make_strip(0)
    for copy in [strip_copy(0, d) for d in hops] + edge_copies(0):
        copy.start()
    data_in[q] = home_ref[pl.ds(4 * mine, 5)]

    def arrived(ref, sem):
        pltpu.make_async_copy(ref, ref, sem).wait()

    def receive(kind, d):
        source = lax.rem(q - d + npat, npat)
        if d:
            strip_copy(kind, d).wait_recv()
        keep = lane_iota((64, LANES)) % 16 < 4

        @pl.when(mine == 0)
        def _():
            arrived(left_ref.at[source, kind], left_recv.at[source, kind])
            data_in[source, 0, kind] = jnp.where(
                keep, left_ref[source, kind], data_in[source, 0, kind]
            )

        @pl.when(mine == npat - 1)
        def _():
            arrived(right_ref.at[source, kind], right_recv.at[source, kind])
            data_in[source, 4, kind] = jnp.where(
                keep, data_in[source, 4, kind], right_ref[source, kind]
            )

    lower = lane_iota((64, LANES)) < 64

    def relay_copies(d):
        source = lax.rem(q - d + npat, npat)
        return [
            pltpu.make_async_remote_copy(
                src_ref=relay_out.at[way, d],
                dst_ref=relay_in.at[way, source],
                send_sem=relay_send.at[way, d],
                recv_sem=relay_recv.at[way, d],
                device_id=at(1 - 2 * way, 0),
                device_id_type=MESH,
            )
            for way in range(2)
        ]

    def relay(d):
        source = lax.rem(q - d + npat, npat)
        receive(1, d)
        for k in range(2):
            a, b = data_in[source, 2 * k, 1], data_in[source, 2 * k + 1, 1]
            relay_out[0, d, k] = jnp.where(lower, a, pltpu.roll(b, 64, 1))
            relay_out[1, d, k] = jnp.where(lower, pltpu.roll(a, 64, 1), b)
        for way in range(2):
            relay_out[way, d, 2] = data_in[source, 4, 1]
        for copy in relay_copies(d):
            copy.start()

    def outer_strips(d):
        source = lax.rem(q - d + npat, npat)
        for copy in relay_copies(d):
            copy.wait_recv()
        for chunk in range(5):
            own = data_in[source, chunk, 1]
            above, below = relay_in[0, source, chunk // 2], relay_in[1, source, chunk // 2]
            if chunk % 2:
                above = pltpu.roll(above, 64, 1)
            elif chunk < 4:
                below = pltpu.roll(below, 64, 1)
            data_mid[source, chunk, 0] = jnp.where(lower, above, own)
            data_mid[source, chunk, 1] = jnp.where(lower, own, below)

    taps = [
        [jnp.where(abs(j - 4) <= radius_ref[i], taps_ref[i, j], 0.0) for j in range(TAPS)]
        for i in range(TAPS)
    ]
    narrow = (16, LANES)
    group = lane_iota(narrow) // 16
    for backward in (False, True):
        target = adjoint_ref if backward else forward_ref
        target[0:256, LANES:] = jnp.zeros((256, LANES), jnp.bfloat16)
        target[512:768, 0:LANES] = jnp.zeros((256, LANES), jnp.bfloat16)

        def tap(i, j):
            return taps[TAPS - 1 - i][TAPS - 1 - j] if backward else taps[i][j]

        for step in range(2):
            gap = 16 * step + row_iota(narrow) - lane_iota(narrow) % 16
            low = jnp.zeros(narrow, jnp.float32)
            high = jnp.zeros(narrow, jnp.float32)
            for j in range(TAPS):
                values = jnp.zeros(narrow, jnp.float32)
                for g in range(8):
                    values = jnp.where(group == g, tap(7 - g, j), values)
                high = jnp.where(gap == j, values, high)
                low = jnp.where((gap == j) & (group == 7), tap(8, j), low)
            for block in range(2):
                for y in range(8):
                    if block:
                        first = 7 - y
                        left, right = low, high
                    else:
                        first = 7 - y
                        left, right = high, None
                    turn = (LANES - 16 * first) % LANES
                    left = pltpu.roll(left, turn, 1) if turn else left
                    if right is None:
                        right = jnp.zeros(narrow, jnp.float32)
                    else:
                        right = pltpu.roll(right, turn, 1) if turn else right
                    values = jnp.where(group < 8 - first, left, right).astype(jnp.bfloat16)
                    for out_chunk in range(2):
                        start = 256 * (out_chunk + step) + LANES * block + 16 * y
                        target[start : start + 16, LANES * out_chunk : LANES * (out_chunk + 1)] = values

    spread = (row_iota((256, 32)) % 32 == lane_iota((256, 32))).astype(jnp.bfloat16)
    axial_b = axial_ref[...].astype(jnp.bfloat16)
    same = row_iota((256, 256)) // 32 == lane_iota((256, 256)) // 32
    nt = (((1,), (1,)), ((), ()))
    right_fwd = lax.dot_general(axial_b, spread, nt, preferred_element_type=jnp.float32)
    full = jnp.dot(spread, right_fwd.astype(jnp.bfloat16), preferred_element_type=jnp.float32)
    axial_fwd[...] = jnp.where(same, full, 0.0).astype(jnp.bfloat16)
    left_adj = lax.dot_general(spread, axial_b, nt, preferred_element_type=jnp.float32)
    full = lax.dot_general(left_adj.astype(jnp.bfloat16), spread, nt, preferred_element_type=jnp.float32)
    axial_adj[...] = jnp.where(same, full, 0.0).astype(jnp.bfloat16)

    relay(0)

    plane = row_iota((32, LANES)).astype(jnp.float32)
    planes_ref[...] = jnp.cos(plane * (2.0 * math.pi * 3.0 / 32.0))

    def positions(tile, strips, offset):
        spot = lane_iota(tile.shape)
        chunk, strip = tile // strips, tile % strips
        y = ty * 16 + 8 * strip - offset + spot // 16
        x = column * 64 + 16 * chunk - offset + spot % 16
        return y, x

    def waves(count, strips, offset):
        shape = (count * NPAT, LANES)
        index = row_iota(shape)
        y, x = positions(index // NPAT, strips, offset)
        pattern = index % NPAT
        angle = jnp.zeros(shape, jnp.int32)
        phase = jnp.zeros(shape, jnp.int32)
        for p in range(NPAT):
            angle = jnp.where(pattern == p, codes_ref[0, p], angle)
            phase = jnp.where(pattern == p, codes_ref[1, p], phase)
        cx = jnp.where(angle == 0, 2, -1)
        cy = jnp.where(angle == 0, 0, jnp.where(angle == 1, 2, -2))
        value = cx * x + cy * y + phase
        wide = value.astype(jnp.float32)
        m = wide - 5.0 * jnp.floor((wide + 0.5) * 0.2)
        wave = jnp.full(shape, COSINES[0], jnp.float32)
        for k in range(1, 5):
            wave = jnp.where(m == float(k), COSINES[k], wave)
        return 0.7 * wave

    wave_ext[...] = waves(20, 4, 8)
    wave_in[...] = waves(8, 2, 0)

    def inside(shape, strips, offset):
        y, x = positions(row_iota(shape), strips, offset)
        return (y >= 0) & (y < full_rows) & (x >= 0) & (x < full_cols)

    mask_ext[...] = inside((24, LANES), 4, 8).astype(jnp.float32)
    tile15 = (16, LANES)
    valid = inside(tile15, 3, 4) & ((row_iota(tile15) < 12) | (lane_iota(tile15) % 16 < 8))
    valid_ref[...] = valid.astype(jnp.float32)

    column_sum = lax.dot_general(
        axial_b, jnp.ones((32, LANES), jnp.bfloat16), (((0,), (0,)), ((), ())),
        preferred_element_type=jnp.float32,
    )
    cover_in = [
        jnp.broadcast_to(valid_ref[k : k + 1, :], (16, LANES)).astype(jnp.bfloat16)
        for k in range(15)
    ]
    plane_wave = planes_ref[...]
    for strip in range(2):
        for chunk in (0, 2):
            window = jnp.concatenate(
                [cover_in[3 * (chunk + k) + strip + a] for k in range(3) for a in range(2)], axis=1
            )
            cover = jnp.dot(window, adjoint_ref[...], preferred_element_type=jnp.float32)
            cover = cover.astype(jnp.bfloat16).astype(jnp.float32)
            for k in range(2):
                tile = 2 * (chunk + k) + strip
                row = cover[0:1, LANES * k : LANES * (k + 1)]
                light = jnp.zeros((32, LANES), jnp.float32)
                for p in range(NPAT):
                    light = light + (1.0 + wave_in[NPAT * tile + p : NPAT * tile + p + 1, :] * plane_wave)
                norm_ref[tile] = light * (row * column_sum)

    own = lane_iota((8, LANES))
    own_col, own_row = own % 16, own // 16

    def inner_mask(tile):
        chunk, strip = tile // 3, tile % 3
        x, y = 16 * chunk + own_col, 8 * strip + own_row
        return (x >= 4) & (x < 68) & (y >= 4) & (y < 20)

    blocks = ((1, 2), (0, 1), (3, 2))

    def predict(strip, chunk, width):
        count = min(width + 1, 5 - chunk)
        window = jnp.concatenate(
            [
                blur_ref[:, LANES * (4 * (chunk + k) + strip) : LANES * (4 * (chunk + k) + strip + 2)]
                for k in range(count)
            ],
            axis=1,
        )
        return jnp.dot(
            window,
            forward_ref[0 : 256 * count, 0 : LANES * width],
            preferred_element_type=jnp.float32,
        )

    def compare_rows(strip, tile_chunk, source, guess):
        tile = 3 * tile_chunk + strip
        ok = valid_ref[tile : tile + 1, :]
        if strip == 1:
            data = data_in[source, tile_chunk, 0]
        else:
            data = data_mid[source, tile_chunk, strip // 2]
        misfit = data - guess
        quotient = (data * ok) / (guess + (1.0 - ok))
        return jnp.sum((misfit * misfit).reshape(8, 8, LANES), axis=0), quotient.astype(jnp.bfloat16)

    def compare(strip, chunk, predicted, squares):
        for k in range(predicted.shape[1] // LANES):
            tile = 3 * (chunk + k) + strip
            total = jnp.zeros((8, LANES), jnp.float32)
            for source in range(4):
                rows = slice(64 * source, 64 * (source + 1))
                part, quotient = compare_rows(
                    strip, chunk + k, source, predicted[rows, LANES * k : LANES * (k + 1)]
                )
                quot_ref[rows, LANES * tile : LANES * (tile + 1)] = quotient
                total = total + part
            squares = squares + jnp.where(inner_mask(tile), total, 0.0)
        return squares

    def compare_source(source, squares):
        rows = pl.ds(pl.multiple_of(64 * source, 64), 64)
        for strip in range(3):
            for chunk in range(5):
                tile, place = 3 * chunk + strip, 5 * strip + chunk
                part, quotient = compare_rows(
                    strip, chunk, source, pred_ref[rows, LANES * place : LANES * (place + 1)]
                )
                quot_ref[rows, LANES * tile : LANES * (tile + 1)] = quotient
                squares = squares + jnp.where(inner_mask(tile), part, 0.0)
        return squares

    stages = [
        (sums_row, ncol, tx * npat + q, lambda d: shifted(0, d // npat, d % npat)),
        (sums_ty, nty, ty, lambda d: shifted(d, 0, 0)),
    ]

    def sum_copies(stage):
        slots, count, me, device = stages[stage]
        return [
            pltpu.make_async_remote_copy(
                src_ref=slots.at[me],
                dst_ref=slots.at[me],
                send_sem=sum_send.at[stage, d - 1],
                recv_sem=sum_recv.at[stage, d - 1],
                device_id=device(d),
                device_id_type=MESH,
            )
            for d in range(1, count)
        ]

    def send_sums(stage, value):
        slots, _, me, _ = stages[stage]
        slots[me] = value
        for copy in sum_copies(stage):
            copy.start()

    def gather_sums(stage):
        for copy in sum_copies(stage):
            copy.wait()
        slots, count, _, _ = stages[stage]
        total = slots[0]
        for k in range(1, count):
            total = total + slots[k]
        return total

    def lit_tiles(t, strips, chunks=range(5)):
        wave_z = planes_ref[...]
        left_half = lane_iota((32, LANES)) % 16 < 8

        def light(tile):
            chunk, strip = tile // 4, tile % 4
            a, b = grid_ref[t, chunk, strip], grid_ref[t, chunk + 1, strip]
            value = jnp.where(left_half, pltpu.roll(a, LANES - 8, 1), pltpu.roll(b, 8, 1))
            value = value * mask_ext[tile : tile + 1, :]
            for p in range(NPAT):
                wave = 1.0 + wave_ext[NPAT * tile + p : NPAT * tile + p + 1, :] * wave_z
                lit_ref[32 * p : 32 * (p + 1), LANES * tile : LANES * (tile + 1)] = (
                    wave * value
                ).astype(jnp.bfloat16)

        def blur(pair):
            pair = [slice(LANES * tile, LANES * (tile + 1)) for tile in pair]
            lit = jnp.concatenate([lit_ref[:, lanes] for lanes in pair], axis=1)
            blurred = jnp.dot(axial_fwd[...], lit, preferred_element_type=jnp.float32)
            for n, lanes in enumerate(pair):
                blur_ref[:, lanes] = blurred[:, LANES * n : LANES * (n + 1)].astype(jnp.bfloat16)

        tiles = [4 * chunk + strip for chunk in chunks for strip in strips]
        pairs = [tiles[k : k + 2] for k in range(0, len(tiles), 2)]
        for k, pair in enumerate(pairs):
            for tile in pair:
                light(tile)
            if k:
                blur(pairs[k - 1])
        blur(pairs[-1])

    def wait_halo(t, which):
        for copy in halo_copies(t, which):
            copy.wait_recv()

    def back_project(t, strip, chunk):
        wave_z = planes_ref[...]
        updated = []
        tile = 3 * chunk + strip
        window = jnp.concatenate(
            [quot_ref[:, LANES * (tile + 3 * k) : LANES * (tile + 3 * k + 2)] for k in range(3)],
            axis=1,
        )
        spread_back = jnp.dot(
            window, adjoint_ref[...], preferred_element_type=jnp.float32
        ).astype(jnp.bfloat16)
        gathered = jnp.dot(axial_adj[...], spread_back, preferred_element_type=jnp.float32)
        for k in range(2):
            here = 2 * (chunk + k) + strip
            summed = jnp.zeros((32, LANES), jnp.float32)
            for p in range(NPAT):
                light = 1.0 + wave_in[NPAT * here + p : NPAT * here + p + 1, :] * wave_z
                summed = summed + light * gathered[
                    32 * p : 32 * (p + 1), LANES * k : LANES * (k + 1)
                ]
            current = grid_ref[t, 1 + chunk + k, 1 + strip]
            updated.append((chunk + k, current * summed / norm_ref[here]))
        return updated

    def out_copies(strip):
        return [
            pltpu.make_async_remote_copy(
                src_ref=final_ref.at[mine, :, strip],
                dst_ref=final_ref.at[mine, :, strip],
                send_sem=out_send.at[strip, d - 1],
                recv_sem=out_recv.at[strip, d - 1],
                device_id=peer(d),
                device_id_type=MESH,
            )
            for d in range(1, npat)
        ]

    def compare_strip(strip, squares, some=blocks):
        waiting = None
        for chunk, width in some:
            predicted = predict(strip, chunk, width)
            if waiting is not None:
                squares = compare(strip, *waiting, squares)
            waiting = chunk, predicted
        return compare(strip, *waiting, squares)

    def finish_strip(t, strip):
        last = t == ITERS - 1
        for block in range(2):
            for chunk, value in back_project(t, strip, 2 * block):
                if last:
                    final_ref[mine, chunk, strip] = value
                else:
                    grid_ref[t + 1, 1 + chunk, 1 + strip] = value
            if not last:
                for copy in halo_copies(t + 1, from_strip[strip][block]):
                    copy.start()
        if last:
            for copy in out_copies(strip):
                copy.start()

    def share_squares():
        share = jnp.zeros((8, LANES), jnp.float32)
        for k in range(ITERS):
            total = jnp.sum(squares_ref[k], axis=0, keepdims=True)
            share = jnp.where(row_iota((8, LANES)) == k, total, share)
        send_sums(0, share)

    for t in range(ITERS):
        early = 1 - t % 2
        near, far = (2, 0) if early == 1 else (0, 2)
        near_halo, far_halo = (3, 0) if early == 1 else (0, 3)
        squares = jnp.zeros((8, LANES), jnp.float32)
        lit_tiles(t, (1, 2), (1, 2, 3))
        if t == 0:
            wait_halo(t, side_halo)
            lit_tiles(t, (1, 2), (0, 4))
            wait_halo(t, all_halo[:4] + all_halo[8:])
            lit_tiles(t, (0, 3))
            for strip in range(3):
                for chunk, width in blocks:
                    tile = 5 * strip + chunk
                    pred_ref[:, LANES * tile : LANES * (tile + width)] = predict(
                        strip, chunk, width
                    )
            for d in hops:
                relay(d)
            for d in (0, *hops):
                outer_strips(d)
                receive(0, d)
                squares = compare_source(lax.rem(q - d + npat, npat), squares)
        else:
            squares = compare_strip(1, squares, blocks[:1])
            wait_halo(t, side_halo + row_halo[near_halo] + corner_halo[near_halo])
            lit_tiles(t, (1, 2), (0, 4))
            lit_tiles(t, (near_halo,))
            squares = compare_strip(1, squares, blocks[1:])
            squares = compare_strip(near, squares)
            if t < ITERS - 1:
                finish_strip(t, early)
            wait_halo(t, row_halo[far_halo] + corner_halo[far_halo])
            lit_tiles(t, (far_halo,))
            squares = compare_strip(far, squares)
        squares_ref[t] = squares
        if t == ITERS - 1:
            share_squares()
        if t == 0 or t == ITERS - 1:
            finish_strip(t, early)
        finish_strip(t, 1 - early)

    send_sums(1, gather_sums(0))
    for kind in range(2):
        for copy in [strip_copy(kind, d) for d in hops] + edge_copies(kind):
            copy.wait_send()
    for d in range(npat):
        for copy in relay_copies(d):
            copy.wait_send()
    for t in range(ITERS):
        for copy in halo_copies(t, all_halo):
            copy.wait_send()
    for strip in (early, 1 - early):
        for copy in out_copies(strip):
            copy.wait()
        for half in range(2):
            tiles = [final_ref[2 * half + k // 4, k % 4, strip] for k in range(8)]
            for y, row in enumerate(block_transpose(tiles)):
                out_rows[half, pl.ds(8 * strip + y, 32, stride=16)] = row
    stores = [
        pltpu.make_async_copy(
            out_rows.at[half], out_ref.at[:, LANES * half : LANES * (half + 1)], store_sem.at[half]
        )
        for half in range(2)
    ]
    for copy in stores:
        copy.start()
    total = jnp.sum(gather_sums(1), axis=1, keepdims=True)
    rms = jnp.sqrt(total / cells)
    for k in range(ITERS):
        rms_ref[k] = rms[k, 0]
    for copy in stores:
        copy.wait()


def per_device(estimate, data, axial, lateral_kernel, psf_radius, pattern_codes):
    planes, height, width = estimate.shape
    local = data.shape[0]
    full_rows = height * lax.axis_size("ty")
    full_cols = width * lax.axis_size("tx")
    est_rows = estimate.reshape(planes * height, width)
    data_rows = data.reshape(local * planes * height, width)
    vmem = pl.BlockSpec(memory_space=pltpu.VMEM)
    hbm = pl.BlockSpec(memory_space=pltpu.HBM)
    smem = pl.BlockSpec(memory_space=pltpu.SMEM)
    f32, bf16 = jnp.float32, jnp.bfloat16
    dma = pltpu.SemaphoreType.DMA
    cells = float(local * lax.axis_size("pat") * planes * full_rows * full_cols)
    rows, rms = pl.pallas_call(
        functools.partial(kernel, full_rows, full_cols, cells),
        name="deconvolve",
        out_shape=(
            jax.ShapeDtypeStruct((planes * height, width), f32),
            jax.ShapeDtypeStruct((ITERS,), f32),
        ),
        in_specs=[hbm, hbm, vmem, smem, smem, smem],
        out_specs=(hbm, smem),
        scratch_shapes=[
            pltpu.VMEM((ITERS, 8, LANES), f32),
            pltpu.VMEM((lax.axis_size(("tx", "pat")), 8, LANES), f32),
            pltpu.VMEM((lax.axis_size("ty"), 8, LANES), f32),
            pltpu.VMEM((2, planes * height, LANES), f32),
            pltpu.VMEM((2, local * planes * height, LANES), f32),
            pltpu.VMEM((2, planes * height, LANES), f32),
            dma((2, 2)),
            dma((2,)),
            pltpu.VMEM((ITERS, 6, 4, 32, LANES), f32),
            pltpu.VMEM((4, 4, 2, 32, LANES), f32),
            pltpu.VMEM((17, 2, 64, LANES), f32),
            pltpu.VMEM((4, 5, 2, 64, LANES), f32),
            pltpu.VMEM((4, 5, 2, 64, LANES), f32),
            pltpu.VMEM((2, 4, 3, 64, LANES), f32),
            pltpu.VMEM((2, 4, 3, 64, LANES), f32),
            pltpu.VMEM((4, 2, 64, LANES), f32),
            pltpu.VMEM((4, 2, 64, LANES), f32),
            pltpu.VMEM((256, 20 * LANES), bf16),
            pltpu.VMEM((256, 20 * LANES), bf16),
            pltpu.VMEM((256, 15 * LANES), f32),
            pltpu.VMEM((256, 15 * LANES), bf16),
            pltpu.VMEM((768, 256), bf16),
            pltpu.VMEM((768, 256), bf16),
            pltpu.VMEM((256, 256), bf16),
            pltpu.VMEM((256, 256), bf16),
            pltpu.VMEM((20 * NPAT, LANES), f32),
            pltpu.VMEM((8 * NPAT, LANES), f32),
            pltpu.VMEM((32, LANES), f32),
            pltpu.VMEM((24, LANES), f32),
            pltpu.VMEM((16, LANES), f32),
            pltpu.VMEM((8, 32, LANES), f32),
            dma((ITERS, 12)),
            dma((ITERS, 12)),
            dma((2, 4)),
            dma((2, 4)),
            dma((2, 2)),
            dma((4, 2)),
            dma((4, 2)),
            dma((2, 3)),
            dma((2, 3)),
            dma((2, 3)),
            dma((2, 3)),
            dma((2, 15)),
            dma((2, 15)),
        ],
        compiler_params=pltpu.CompilerParams(
            collective_id=0, has_side_effects=True, vmem_limit_bytes=56 * 1024 * 1024
        ),
    )(est_rows, data_rows, axial, lateral_kernel, psf_radius, pattern_codes)
    return rows.reshape(planes, height, width), rms


def solution(mesh):
    in_specs = (P(None, "ty", "tx"), P("pat", None, "ty", "tx"), P(), P(), P(), P())
    out_specs = (P(None, "ty", "tx"), P())
    return jax.shard_map(
        per_device, mesh=mesh, in_specs=in_specs, out_specs=out_specs, check_vma=False
    )
```

```python
import functools
import math

import jax
import jax.numpy as jnp
from jax import lax
from jax.experimental import pallas as pl
from jax.experimental.pallas import tpu as pltpu
from jax.sharding import PartitionSpec as P

ITERS = 4
TAPS = 9
NPAT = 8
LANES = 128
COSINES = [math.cos(2.0 * math.pi * m / 5.0) for m in range(5)]
MESH = pl.DeviceIdType.MESH


def lane_iota(shape):
    return lax.broadcasted_iota(jnp.int32, shape, len(shape) - 1)


def row_iota(shape):
    return lax.broadcasted_iota(jnp.int32, shape, len(shape) - 2)


def block_transpose(tiles):
    group = lane_iota(tiles[0].shape) // 16
    tiles = list(tiles)
    for bit in (4, 2, 1):
        keep = (group & bit) == 0
        for k in range(8):
            if k & bit:
                continue
            low, high = tiles[k], tiles[k + bit]
            axis = low.ndim - 1
            tiles[k] = jnp.where(keep, low, pltpu.roll(high, 16 * bit, axis))
            tiles[k + bit] = jnp.where(keep, pltpu.roll(low, LANES - 16 * bit, axis), high)
    return tiles


def kernel(
    full_rows,
    full_cols,
    cells,
    est_ref,
    data_ref,
    axial_ref,
    taps_ref,
    radius_ref,
    codes_ref,
    out_ref,
    rms_ref,
    squares_ref,
    sums_row,
    sums_ty,
    est_rows,
    data_rows,
    out_rows,
    load_sem,
    store_sem,
    grid_ref,
    final_ref,
    home_ref,
    data_in,
    data_mid,
    relay_out,
    relay_in,
    left_ref,
    right_ref,
    lit_ref,
    blur_ref,
    pred_ref,
    quot_ref,
    forward_ref,
    adjoint_ref,
    axial_fwd,
    axial_adj,
    wave_ext,
    wave_in,
    planes_ref,
    mask_ext,
    valid_ref,
    norm_ref,
    halo_send,
    halo_recv,
    relay_send,
    relay_recv,
    edge_send,
    left_recv,
    right_recv,
    pat_send,
    pat_recv,
    out_send,
    out_recv,
    sum_send,
    sum_recv,
):
    ty, tx, q = lax.axis_index("ty"), lax.axis_index("tx"), lax.axis_index("pat")
    nty, ntx, npat = lax.axis_size("ty"), lax.axis_size("tx"), lax.axis_size("pat")
    ncol = ntx * npat
    loads = [
        pltpu.make_async_copy(
            source.at[:, LANES * half : LANES * (half + 1)], target.at[half], load_sem.at[k, half]
        )
        for k, (source, target) in enumerate(((est_ref, est_rows), (data_ref, data_rows)))
        for half in range(2)
    ]
    for copy in loads:
        copy.start()

    def turned(tile, place):
        return jnp.where(lax.rem(tile, 2) == 0, place, npat - 1 - place)

    mine = turned(tx, q)
    column = tx * npat + mine

    def at(dty, dcol):
        c = lax.rem(column + dcol + ncol, ncol)
        tile = c // npat
        return {
            "ty": lax.rem(ty + dty + nty, nty),
            "tx": tile,
            "pat": turned(tile, lax.rem(c, npat)),
        }

    def shifted(dty, dtx, dq):
        return {
            "ty": lax.rem(ty + dty + nty, nty),
            "tx": lax.rem(tx + dtx + ntx, ntx),
            "pat": lax.rem(q + dq, npat),
        }

    def peer(d):
        return shifted(0, 0, d)

    barrier = pltpu.get_barrier_semaphore()
    greet = [(0, b, c) for b in range(ntx) for c in range(npat)]
    greet += [(a, b, c) for a in (-1, 1) for b in (-1, 0, 1) for c in range(npat)]
    greet += [(a, 0, 0) for a in range(2, nty - 1)]
    greet.remove((0, 0, 0))
    for move in greet:
        pl.semaphore_signal(
            barrier, inc=1, device_id=shifted(*move), device_id_type=MESH
        )

    for half in range(2):
        loads[half].wait()
    for strip in range(2):
        for half in range(2):
            rows = [est_rows[half, pl.ds(8 * strip + y, 32, stride=16)] for y in range(8)]
            for k, tile in enumerate(block_transpose(rows)):
                final_ref[2 * half + k // 4, k % 4, strip] = tile
    grid_ref[0, 1:5, 1:3] = final_ref[mine]

    moves = [
        ((slice(1, 3), 1), (slice(1, 3), 3), -1, 0),
        ((slice(3, 5), 1), (slice(3, 5), 3), -1, 0),
        ((slice(1, 3), 2), (slice(1, 3), 0), 1, 0),
        ((slice(3, 5), 2), (slice(3, 5), 0), 1, 0),
        ((1, 1), (5, 1), 0, -1),
        ((4, 1), (0, 1), 0, 1),
        ((1, 2), (5, 2), 0, -1),
        ((4, 2), (0, 2), 0, 1),
        ((1, 1), (5, 3), -1, -1),
        ((4, 1), (0, 3), -1, 1),
        ((1, 2), (5, 0), 1, -1),
        ((4, 2), (0, 0), 1, 1),
    ]
    from_strip = (((4, 8, 0), (5, 9, 1)), ((6, 10, 2), (7, 11, 3)))
    side_halo = (4, 5, 6, 7)
    row_halo = {0: (2, 3), 3: (0, 1)}
    corner_halo = {0: (10, 11), 3: (8, 9)}
    all_halo = (8, 9, 10, 11, 4, 5, 6, 7, 0, 1, 2, 3)

    def halo_copies(t, which):
        copies = []
        for k in which:
            source, target, dty, dcol = moves[k]
            copies.append(
                pltpu.make_async_remote_copy(
                    src_ref=grid_ref.at[(t, *source)],
                    dst_ref=grid_ref.at[(t, *target)],
                    send_sem=halo_send.at[t, k],
                    recv_sem=halo_recv.at[t, k],
                    device_id=at(dty, dcol),
                    device_id_type=MESH,
                )
            )
        return copies

    kind_rows = (range(4, 12), (12, 13, 14, 15, 0, 1, 2, 3))

    def make_strip(kind):
        first = lane_iota((8, LANES)) < 4
        group = lane_iota((8, LANES)) // 16
        for block in range(8):
            at_rows = slice(8 * block, 8 * block + 8)

            def rows_of(half):
                return [
                    pltpu.roll(data_rows[half, pl.ds(128 * block + y, 8, stride=16)], 4, 1)
                    for y in kind_rows[kind]
                ]

            low, high = rows_of(0), rows_of(1)
            for k, tile in enumerate(block_transpose(low)):
                home_ref[k, kind, at_rows] = tile
            mixed = [jnp.where(first, a, b) for a, b in zip(low, high)]
            for k, tile in enumerate(block_transpose(mixed)):
                home_ref[8 + k, kind, at_rows] = tile
            last = high[0]
            for y in range(1, 8):
                last = jnp.where(group == y, pltpu.roll(high[y], 16 * y, 1), last)
            home_ref[16, kind, at_rows] = last

    def strip_copy(kind, d):
        to = turned(tx, lax.rem(q + d, npat))
        return pltpu.make_async_remote_copy(
            src_ref=home_ref.at[pl.ds(4 * to, 5), kind],
            dst_ref=data_in.at[q, :, kind],
            send_sem=pat_send.at[kind, d - 1],
            recv_sem=pat_recv.at[kind, d - 1],
            device_id=peer(d),
            device_id_type=MESH,
        )

    def edge_copies(kind):
        after, before = lax.rem(tx + 1, ntx), lax.rem(tx + ntx - 1, ntx)
        return [
            pltpu.make_async_remote_copy(
                src_ref=home_ref.at[16, kind],
                dst_ref=left_ref.at[q, kind],
                send_sem=edge_send.at[0, kind],
                recv_sem=left_recv.at[q, kind],
                device_id={"ty": ty, "tx": after, "pat": turned(after, 0)},
                device_id_type=MESH,
            ),
            pltpu.make_async_remote_copy(
                src_ref=home_ref.at[0, kind],
                dst_ref=right_ref.at[q, kind],
                send_sem=edge_send.at[1, kind],
                recv_sem=right_recv.at[q, kind],
                device_id={"ty": ty, "tx": before, "pat": turned(before, npat - 1)},
                device_id_type=MESH,
            ),
        ]

    hops = (1, 3, 2)
    for copy in loads[2:]:
        copy.wait()
    make_strip(1)
    pl.semaphore_wait(barrier, len(greet))
    for copy in halo_copies(0, all_halo):
        copy.start()
    for copy in [strip_copy(1, d) for d in hops] + edge_copies(1):
        copy.start()
    make_strip(0)
    for copy in [strip_copy(0, d) for d in hops] + edge_copies(0):
        copy.start()
    data_in[q] = home_ref[pl.ds(4 * mine, 5)]

    def arrived(ref, sem):
        pltpu.make_async_copy(ref, ref, sem).wait()

    def receive(kind, d):
        source = lax.rem(q - d + npat, npat)
        if d:
            strip_copy(kind, d).wait_recv()
        keep = lane_iota((64, LANES)) % 16 < 4

        @pl.when(mine == 0)
        def _():
            arrived(left_ref.at[source, kind], left_recv.at[source, kind])
            data_in[source, 0, kind] = jnp.where(
                keep, left_ref[source, kind], data_in[source, 0, kind]
            )

        @pl.when(mine == npat - 1)
        def _():
            arrived(right_ref.at[source, kind], right_recv.at[source, kind])
            data_in[source, 4, kind] = jnp.where(
                keep, data_in[source, 4, kind], right_ref[source, kind]
            )

    lower = lane_iota((64, LANES)) < 64

    def relay_copies(d):
        source = lax.rem(q - d + npat, npat)
        return [
            pltpu.make_async_remote_copy(
                src_ref=relay_out.at[way, d],
                dst_ref=relay_in.at[way, source],
                send_sem=relay_send.at[way, d],
                recv_sem=relay_recv.at[way, d],
                device_id=at(1 - 2 * way, 0),
                device_id_type=MESH,
            )
            for way in range(2)
        ]

    def relay(d):
        source = lax.rem(q - d + npat, npat)
        receive(1, d)
        for k in range(2):
            a, b = data_in[source, 2 * k, 1], data_in[source, 2 * k + 1, 1]
            relay_out[0, d, k] = jnp.where(lower, a, pltpu.roll(b, 64, 1))
            relay_out[1, d, k] = jnp.where(lower, pltpu.roll(a, 64, 1), b)
        for way in range(2):
            relay_out[way, d, 2] = data_in[source, 4, 1]
        for copy in relay_copies(d):
            copy.start()

    def outer_strips(d):
        source = lax.rem(q - d + npat, npat)
        for copy in relay_copies(d):
            copy.wait_recv()
        for chunk in range(5):
            own = data_in[source, chunk, 1]
            above, below = relay_in[0, source, chunk // 2], relay_in[1, source, chunk // 2]
            if chunk % 2:
                above = pltpu.roll(above, 64, 1)
            elif chunk < 4:
                below = pltpu.roll(below, 64, 1)
            data_mid[source, chunk, 0] = jnp.where(lower, above, own)
            data_mid[source, chunk, 1] = jnp.where(lower, own, below)

    taps = [
        [jnp.where(abs(j - 4) <= radius_ref[i], taps_ref[i, j], 0.0) for j in range(TAPS)]
        for i in range(TAPS)
    ]
    narrow = (16, LANES)
    group = lane_iota(narrow) // 16
    for backward in (False, True):
        target = adjoint_ref if backward else forward_ref
        target[0:256, LANES:] = jnp.zeros((256, LANES), jnp.bfloat16)
        target[512:768, 0:LANES] = jnp.zeros((256, LANES), jnp.bfloat16)

        def tap(i, j):
            return taps[TAPS - 1 - i][TAPS - 1 - j] if backward else taps[i][j]

        for step in range(2):
            gap = 16 * step + row_iota(narrow) - lane_iota(narrow) % 16
            low = jnp.zeros(narrow, jnp.float32)
            high = jnp.zeros(narrow, jnp.float32)
            for j in range(TAPS):
                values = jnp.zeros(narrow, jnp.float32)
                for g in range(8):
                    values = jnp.where(group == g, tap(7 - g, j), values)
                high = jnp.where(gap == j, values, high)
                low = jnp.where((gap == j) & (group == 7), tap(8, j), low)
            for block in range(2):
                for y in range(8):
                    if block:
                        first = 7 - y
                        left, right = low, high
                    else:
                        first = 7 - y
                        left, right = high, None
                    turn = (LANES - 16 * first) % LANES
                    left = pltpu.roll(left, turn, 1) if turn else left
                    if right is None:
                        right = jnp.zeros(narrow, jnp.float32)
                    else:
                        right = pltpu.roll(right, turn, 1) if turn else right
                    values = jnp.where(group < 8 - first, left, right).astype(jnp.bfloat16)
                    for out_chunk in range(2):
                        start = 256 * (out_chunk + step) + LANES * block + 16 * y
                        target[start : start + 16, LANES * out_chunk : LANES * (out_chunk + 1)] = values

    spread = (row_iota((256, 32)) % 32 == lane_iota((256, 32))).astype(jnp.bfloat16)
    axial_b = axial_ref[...].astype(jnp.bfloat16)
    same = row_iota((256, 256)) // 32 == lane_iota((256, 256)) // 32
    nt = (((1,), (1,)), ((), ()))
    right_fwd = lax.dot_general(axial_b, spread, nt, preferred_element_type=jnp.float32)
    full = jnp.dot(spread, right_fwd.astype(jnp.bfloat16), preferred_element_type=jnp.float32)
    axial_fwd[...] = jnp.where(same, full, 0.0).astype(jnp.bfloat16)
    left_adj = lax.dot_general(spread, axial_b, nt, preferred_element_type=jnp.float32)
    full = lax.dot_general(left_adj.astype(jnp.bfloat16), spread, nt, preferred_element_type=jnp.float32)
    axial_adj[...] = jnp.where(same, full, 0.0).astype(jnp.bfloat16)

    relay(0)

    plane = row_iota((32, LANES)).astype(jnp.float32)
    planes_ref[...] = jnp.cos(plane * (2.0 * math.pi * 3.0 / 32.0))

    def positions(tile, strips, offset):
        spot = lane_iota(tile.shape)
        chunk, strip = tile // strips, tile % strips
        y = ty * 16 + 8 * strip - offset + spot // 16
        x = column * 64 + 16 * chunk - offset + spot % 16
        return y, x

    def waves(count, strips, offset):
        shape = (count * NPAT, LANES)
        index = row_iota(shape)
        y, x = positions(index // NPAT, strips, offset)
        pattern = index % NPAT
        angle = jnp.zeros(shape, jnp.int32)
        phase = jnp.zeros(shape, jnp.int32)
        for p in range(NPAT):
            angle = jnp.where(pattern == p, codes_ref[0, p], angle)
            phase = jnp.where(pattern == p, codes_ref[1, p], phase)
        cx = jnp.where(angle == 0, 2, -1)
        cy = jnp.where(angle == 0, 0, jnp.where(angle == 1, 2, -2))
        value = cx * x + cy * y + phase
        wide = value.astype(jnp.float32)
        m = wide - 5.0 * jnp.floor((wide + 0.5) * 0.2)
        wave = jnp.full(shape, COSINES[0], jnp.float32)
        for k in range(1, 5):
            wave = jnp.where(m == float(k), COSINES[k], wave)
        return 0.7 * wave

    wave_ext[...] = waves(20, 4, 8)
    wave_in[...] = waves(8, 2, 0)

    def inside(shape, strips, offset):
        y, x = positions(row_iota(shape), strips, offset)
        return (y >= 0) & (y < full_rows) & (x >= 0) & (x < full_cols)

    mask_ext[...] = inside((24, LANES), 4, 8).astype(jnp.float32)
    tile15 = (16, LANES)
    valid = inside(tile15, 3, 4) & ((row_iota(tile15) < 12) | (lane_iota(tile15) % 16 < 8))
    valid_ref[...] = valid.astype(jnp.float32)

    column_sum = lax.dot_general(
        axial_b, jnp.ones((32, LANES), jnp.bfloat16), (((0,), (0,)), ((), ())),
        preferred_element_type=jnp.float32,
    )
    cover_in = [
        jnp.broadcast_to(valid_ref[k : k + 1, :], (16, LANES)).astype(jnp.bfloat16)
        for k in range(15)
    ]
    plane_wave = planes_ref[...]
    for strip in range(2):
        for chunk in (0, 2):
            window = jnp.concatenate(
                [cover_in[3 * (chunk + k) + strip + a] for k in range(3) for a in range(2)], axis=1
            )
            cover = jnp.dot(window, adjoint_ref[...], preferred_element_type=jnp.float32)
            cover = cover.astype(jnp.bfloat16).astype(jnp.float32)
            for k in range(2):
                tile = 2 * (chunk + k) + strip
                row = cover[0:1, LANES * k : LANES * (k + 1)]
                light = jnp.zeros((32, LANES), jnp.float32)
                for p in range(NPAT):
                    light = light + (1.0 + wave_in[NPAT * tile + p : NPAT * tile + p + 1, :] * plane_wave)
                norm_ref[tile] = light * (row * column_sum)

    own = lane_iota((8, LANES))
    own_col, own_row = own % 16, own // 16

    def inner_mask(tile):
        chunk, strip = tile // 3, tile % 3
        x, y = 16 * chunk + own_col, 8 * strip + own_row
        return (x >= 4) & (x < 68) & (y >= 4) & (y < 20)

    blocks = ((1, 2), (0, 1), (3, 2))

    def predict(strip, chunk, width):
        count = min(width + 1, 5 - chunk)
        window = jnp.concatenate(
            [
                blur_ref[:, LANES * (4 * (chunk + k) + strip) : LANES * (4 * (chunk + k) + strip + 2)]
                for k in range(count)
            ],
            axis=1,
        )
        return jnp.dot(
            window,
            forward_ref[0 : 256 * count, 0 : LANES * width],
            preferred_element_type=jnp.float32,
        )

    def compare_rows(strip, tile_chunk, source, guess):
        tile = 3 * tile_chunk + strip
        ok = valid_ref[tile : tile + 1, :]
        if strip == 1:
            data = data_in[source, tile_chunk, 0]
        else:
            data = data_mid[source, tile_chunk, strip // 2]
        misfit = data - guess
        quotient = (data * ok) / (guess + (1.0 - ok))
        return jnp.sum((misfit * misfit).reshape(8, 8, LANES), axis=0), quotient.astype(jnp.bfloat16)

    def compare(strip, chunk, predicted, squares):
        for k in range(predicted.shape[1] // LANES):
            tile = 3 * (chunk + k) + strip
            total = jnp.zeros((8, LANES), jnp.float32)
            for source in range(4):
                rows = slice(64 * source, 64 * (source + 1))
                part, quotient = compare_rows(
                    strip, chunk + k, source, predicted[rows, LANES * k : LANES * (k + 1)]
                )
                quot_ref[rows, LANES * tile : LANES * (tile + 1)] = quotient
                total = total + part
            squares = squares + jnp.where(inner_mask(tile), total, 0.0)
        return squares

    def compare_source(source, squares):
        rows = pl.ds(pl.multiple_of(64 * source, 64), 64)
        for strip in range(3):
            for chunk in range(5):
                tile, place = 3 * chunk + strip, 5 * strip + chunk
                part, quotient = compare_rows(
                    strip, chunk, source, pred_ref[rows, LANES * place : LANES * (place + 1)]
                )
                quot_ref[rows, LANES * tile : LANES * (tile + 1)] = quotient
                squares = squares + jnp.where(inner_mask(tile), part, 0.0)
        return squares

    stages = [
        (sums_row, ncol, tx * npat + q, lambda d: shifted(0, d // npat, d % npat)),
        (sums_ty, nty, ty, lambda d: shifted(d, 0, 0)),
    ]

    def sum_copies(stage):
        slots, count, me, device = stages[stage]
        return [
            pltpu.make_async_remote_copy(
                src_ref=slots.at[me],
                dst_ref=slots.at[me],
                send_sem=sum_send.at[stage, d - 1],
                recv_sem=sum_recv.at[stage, d - 1],
                device_id=device(d),
                device_id_type=MESH,
            )
            for d in range(1, count)
        ]

    def send_sums(stage, value):
        slots, _, me, _ = stages[stage]
        slots[me] = value
        for copy in sum_copies(stage):
            copy.start()

    def gather_sums(stage):
        for copy in sum_copies(stage):
            copy.wait()
        slots, count, _, _ = stages[stage]
        total = slots[0]
        for k in range(1, count):
            total = total + slots[k]
        return total

    def lit_tiles(t, strips, chunks=range(5)):
        wave_z = planes_ref[...]
        left_half = lane_iota((32, LANES)) % 16 < 8

        def light(tile):
            chunk, strip = tile // 4, tile % 4
            a, b = grid_ref[t, chunk, strip], grid_ref[t, chunk + 1, strip]
            value = jnp.where(left_half, pltpu.roll(a, LANES - 8, 1), pltpu.roll(b, 8, 1))
            value = value * mask_ext[tile : tile + 1, :]
            for p in range(NPAT):
                wave = 1.0 + wave_ext[NPAT * tile + p : NPAT * tile + p + 1, :] * wave_z
                lit_ref[32 * p : 32 * (p + 1), LANES * tile : LANES * (tile + 1)] = (
                    wave * value
                ).astype(jnp.bfloat16)

        def blur(pair):
            pair = [slice(LANES * tile, LANES * (tile + 1)) for tile in pair]
            lit = jnp.concatenate([lit_ref[:, lanes] for lanes in pair], axis=1)
            blurred = jnp.dot(axial_fwd[...], lit, preferred_element_type=jnp.float32)
            for n, lanes in enumerate(pair):
                blur_ref[:, lanes] = blurred[:, LANES * n : LANES * (n + 1)].astype(jnp.bfloat16)

        tiles = [4 * chunk + strip for chunk in chunks for strip in strips]
        pairs = [tiles[k : k + 2] for k in range(0, len(tiles), 2)]
        for k, pair in enumerate(pairs):
            for tile in pair:
                light(tile)
            if k:
                blur(pairs[k - 1])
        blur(pairs[-1])

    def wait_halo(t, which):
        for copy in halo_copies(t, which):
            copy.wait_recv()

    def back_project(t, strip, chunk):
        wave_z = planes_ref[...]
        updated = []
        tile = 3 * chunk + strip
        window = jnp.concatenate(
            [quot_ref[:, LANES * (tile + 3 * k) : LANES * (tile + 3 * k + 2)] for k in range(3)],
            axis=1,
        )
        spread_back = jnp.dot(
            window, adjoint_ref[...], preferred_element_type=jnp.float32
        ).astype(jnp.bfloat16)
        gathered = jnp.dot(axial_adj[...], spread_back, preferred_element_type=jnp.float32)
        for k in range(2):
            here = 2 * (chunk + k) + strip
            summed = jnp.zeros((32, LANES), jnp.float32)
            for p in range(NPAT):
                light = 1.0 + wave_in[NPAT * here + p : NPAT * here + p + 1, :] * wave_z
                summed = summed + light * gathered[
                    32 * p : 32 * (p + 1), LANES * k : LANES * (k + 1)
                ]
            current = grid_ref[t, 1 + chunk + k, 1 + strip]
            updated.append((chunk + k, current * summed / norm_ref[here]))
        return updated

    def out_copies(strip):
        return [
            pltpu.make_async_remote_copy(
                src_ref=final_ref.at[mine, :, strip],
                dst_ref=final_ref.at[mine, :, strip],
                send_sem=out_send.at[strip, d - 1],
                recv_sem=out_recv.at[strip, d - 1],
                device_id=peer(d),
                device_id_type=MESH,
            )
            for d in range(1, npat)
        ]

    def compare_strip(strip, squares, some=blocks):
        waiting = None
        for chunk, width in some:
            predicted = predict(strip, chunk, width)
            if waiting is not None:
                squares = compare(strip, *waiting, squares)
            waiting = chunk, predicted
        return compare(strip, *waiting, squares)

    def finish_strip(t, strip):
        last = t == ITERS - 1
        for block in range(2):
            for chunk, value in back_project(t, strip, 2 * block):
                if last:
                    final_ref[mine, chunk, strip] = value
                else:
                    grid_ref[t + 1, 1 + chunk, 1 + strip] = value
            if not last:
                for copy in halo_copies(t + 1, from_strip[strip][block]):
                    copy.start()
        if last:
            for copy in out_copies(strip):
                copy.start()

    def share_squares():
        share = jnp.zeros((8, LANES), jnp.float32)
        for k in range(ITERS):
            total = jnp.sum(squares_ref[k], axis=0, keepdims=True)
            share = jnp.where(row_iota((8, LANES)) == k, total, share)
        send_sums(0, share)

    for t in range(ITERS):
        early = 1 - t % 2
        near, far = (2, 0) if early == 1 else (0, 2)
        near_halo, far_halo = (3, 0) if early == 1 else (0, 3)
        squares = jnp.zeros((8, LANES), jnp.float32)
        lit_tiles(t, (1, 2), (1, 2, 3))
        if t == 0:
            wait_halo(t, side_halo)
            lit_tiles(t, (1, 2), (0, 4))
            wait_halo(t, all_halo[:4] + all_halo[8:])
            lit_tiles(t, (0, 3))
            for strip in range(3):
                for chunk, width in blocks:
                    tile = 5 * strip + chunk
                    pred_ref[:, LANES * tile : LANES * (tile + width)] = predict(
                        strip, chunk, width
                    )
            for d in hops:
                relay(d)
            for d in (0, *hops):
                outer_strips(d)
                receive(0, d)
                squares = compare_source(lax.rem(q - d + npat, npat), squares)
        else:
            squares = compare_strip(1, squares, blocks[:1])
            wait_halo(t, side_halo + row_halo[near_halo] + corner_halo[near_halo])
            lit_tiles(t, (1, 2), (0, 4))
            lit_tiles(t, (near_halo,))
            squares = compare_strip(1, squares, blocks[1:])
            squares = compare_strip(near, squares)
            if t < ITERS - 1:
                finish_strip(t, early)
            wait_halo(t, row_halo[far_halo] + corner_halo[far_halo])
            lit_tiles(t, (far_halo,))
            squares = compare_strip(far, squares)
        squares_ref[t] = squares
        if t == ITERS - 1:
            share_squares()
        if t == 0 or t == ITERS - 1:
            finish_strip(t, early)
        finish_strip(t, 1 - early)

    send_sums(1, gather_sums(0))
    for kind in range(2):
        for copy in [strip_copy(kind, d) for d in hops] + edge_copies(kind):
            copy.wait_send()
    for d in range(npat):
        for copy in relay_copies(d):
            copy.wait_send()
    for t in range(ITERS):
        for copy in halo_copies(t, all_halo):
            copy.wait_send()
    for strip in (early, 1 - early):
        for copy in out_copies(strip):
            copy.wait()
        for half in range(2):
            tiles = [final_ref[2 * half + k // 4, k % 4, strip] for k in range(8)]
            for y, row in enumerate(block_transpose(tiles)):
                out_rows[half, pl.ds(8 * strip + y, 32, stride=16)] = row
    stores = [
        pltpu.make_async_copy(
            out_rows.at[half], out_ref.at[:, LANES * half : LANES * (half + 1)], store_sem.at[half]
        )
        for half in range(2)
    ]
    for copy in stores:
        copy.start()
    total = jnp.sum(gather_sums(1), axis=1, keepdims=True)
    rms = jnp.sqrt(total / cells)
    for k in range(ITERS):
        rms_ref[k] = rms[k, 0]
    for copy in stores:
        copy.wait()


def per_device(estimate, data, axial, lateral_kernel, psf_radius, pattern_codes):
    planes, height, width = estimate.shape
    local = data.shape[0]
    full_rows = height * lax.axis_size("ty")
    full_cols = width * lax.axis_size("tx")
    est_rows = estimate.reshape(planes * height, width)
    data_rows = data.reshape(local * planes * height, width)
    vmem = pl.BlockSpec(memory_space=pltpu.VMEM)
    hbm = pl.BlockSpec(memory_space=pltpu.HBM)
    smem = pl.BlockSpec(memory_space=pltpu.SMEM)
    f32, bf16 = jnp.float32, jnp.bfloat16
    dma = pltpu.SemaphoreType.DMA
    cells = float(local * lax.axis_size("pat") * planes * full_rows * full_cols)
    rows, rms = pl.pallas_call(
        functools.partial(kernel, full_rows, full_cols, cells),
        name="deconvolve",
        out_shape=(
            jax.ShapeDtypeStruct((planes * height, width), f32),
            jax.ShapeDtypeStruct((ITERS,), f32),
        ),
        in_specs=[hbm, hbm, vmem, smem, smem, smem],
        out_specs=(hbm, smem),
        scratch_shapes=[
            pltpu.VMEM((ITERS, 8, LANES), f32),
            pltpu.VMEM((lax.axis_size(("tx", "pat")), 8, LANES), f32),
            pltpu.VMEM((lax.axis_size("ty"), 8, LANES), f32),
            pltpu.VMEM((2, planes * height, LANES), f32),
            pltpu.VMEM((2, local * planes * height, LANES), f32),
            pltpu.VMEM((2, planes * height, LANES), f32),
            dma((2, 2)),
            dma((2,)),
            pltpu.VMEM((ITERS, 6, 4, 32, LANES), f32),
            pltpu.VMEM((4, 4, 2, 32, LANES), f32),
            pltpu.VMEM((17, 2, 64, LANES), f32),
            pltpu.VMEM((4, 5, 2, 64, LANES), f32),
            pltpu.VMEM((4, 5, 2, 64, LANES), f32),
            pltpu.VMEM((2, 4, 3, 64, LANES), f32),
            pltpu.VMEM((2, 4, 3, 64, LANES), f32),
            pltpu.VMEM((4, 2, 64, LANES), f32),
            pltpu.VMEM((4, 2, 64, LANES), f32),
            pltpu.VMEM((256, 20 * LANES), bf16),
            pltpu.VMEM((256, 20 * LANES), bf16),
            pltpu.VMEM((256, 15 * LANES), f32),
            pltpu.VMEM((256, 15 * LANES), bf16),
            pltpu.VMEM((768, 256), bf16),
            pltpu.VMEM((768, 256), bf16),
            pltpu.VMEM((256, 256), bf16),
            pltpu.VMEM((256, 256), bf16),
            pltpu.VMEM((20 * NPAT, LANES), f32),
            pltpu.VMEM((8 * NPAT, LANES), f32),
            pltpu.VMEM((32, LANES), f32),
            pltpu.VMEM((24, LANES), f32),
            pltpu.VMEM((16, LANES), f32),
            pltpu.VMEM((8, 32, LANES), f32),
            dma((ITERS, 12)),
            dma((ITERS, 12)),
            dma((2, 4)),
            dma((2, 4)),
            dma((2, 2)),
            dma((4, 2)),
            dma((4, 2)),
            dma((2, 3)),
            dma((2, 3)),
            dma((2, 3)),
            dma((2, 3)),
            dma((2, 15)),
            dma((2, 15)),
        ],
        compiler_params=pltpu.CompilerParams(
            collective_id=0, has_side_effects=True, vmem_limit_bytes=56 * 1024 * 1024
        ),
    )(est_rows, data_rows, axial, lateral_kernel, psf_radius, pattern_codes)
    return rows.reshape(planes, height, width), rms


def solution(mesh):
    in_specs = (P(None, "ty", "tx"), P("pat", None, "ty", "tx"), P(), P(), P(), P())
    out_specs = (P(None, "ty", "tx"), P())
    return jax.shard_map(
        per_device, mesh=mesh, in_specs=in_specs, out_specs=out_specs, check_vma=False
    )
```
